256 devices in a mesh: req: 16 (over y, x_hi, core), blk: 16 (over z, x_lo).
Axes of the slice: x: 4 (x_hi: 2, x_lo: 2; x = x_hi * 2 + x_lo), y: 4, z: 8, core: 2. Of those that a mesh axis runs over, the one named last changes fastest.
Arguments:
- tokens: bfloat16 [32, 256, 1600], P('req'), may hold values from -6 to 6
- cache_kv: bfloat16 [4, 8192, 16, 128], P(None, 'req', 'blk'), may hold values from -500 to 500
- w_qkv: bfloat16 [1600, 16, 192], P(None, 'blk'), may hold values from -0.15625 to 0.15625
- w_out: bfloat16 [16, 64, 1600], P('blk'), may hold values from -0.1875 to 0.1875
- w_fc: bfloat16 [1600, 6400], P(None, 'blk'), may hold values from -0.15625 to 0.15625
- w_proj: bfloat16 [6400, 1600], P('blk'), may hold values from -0.078125 to 0.078125
- embed_table: bfloat16 [50256, 1600], P('req', 'blk'), may hold values from -6 to 6
- group_ids: int32 [32], replicated, may hold values from 0 to 3, never falling along the last dimension, each value on 1 to 16 neighbouring positions
- cache_len: int32 [4], replicated, may hold values from 512 to 8192, as said below
- accept: int32 [2, 32, 256], P(None, 'req'), may hold values 0 or 1
- new_ids: int32 [2, 32, 256], replicated, may hold values from 0 to 50255
Outputs:
- denoised: bfloat16 [32, 256, 1600], P('req')
The draws below stay inside these ranges and needn't reach their ends.
Inputs may be any that keep to these rules, and one draw needn't show every extreme that they name: `group_ids`: requests of one group stand in consecutive order; each of the 4 groups holds 1 to 16 requests and one holds exactly 16. Cache positions 0 to cache_len[g] - 1 of group g are live; one group's cache is full in every draw.
All inputs are finite; a program needn't handle non-finite values. No bound on the sum of `accept` on one device may be relied on, other than what follows from the above.
Results may differ from the reference program's by a relative error of at most 0.04.
Values may be sent and summed in bfloat16 or wider, within the bound.
A program may use at most 128 MiB of HBM per device.

```python
import math
import jax
import jax.numpy as jnp
import numpy as np
from jax import lax

D = 1600
HEADS = 16
HEAD_DIM = 64
FF = 6400
VOCAB = 50256
CAP = 8192
BLOCK = 256
NG = 4
PASSES = 2
REQS = 32
CAP_DEV = 512
HEAD_DEV = 1
FF_DEV = 400
N_BLK = 16


def draw_cache_len(key, part):
    draw_key, pick_key = jax.random.split(key)
    lengths = jax.random.randint(draw_key, (NG,), CAP // 16, CAP + 1)
    full_at = jax.random.randint(pick_key, (), 0, NG)
    return jnp.where(jnp.arange(NG) == full_at, CAP, lengths).astype(jnp.int32)


def draw_cache_kv(key, part):
    subkeys = jax.random.split(key, 2)
    blocks = CAP // CAP_DEV
    full_shape = (NG, blocks, CAP_DEV, HEADS, 2 * HEAD_DIM)
    offset = jax.random.normal(subkeys[1], (NG, blocks, 1, HEADS, 2 * HEAD_DIM), jnp.float32)
    noise_part = jax.random.normal(subkeys[0], full_shape, jnp.float32)
    values_all = (noise_part + offset).reshape(NG, CAP, HEADS, 2 * HEAD_DIM)
    return jnp.clip(values_all, -500.0, 500.0).astype(jnp.bfloat16)


def place_ends(entries, rng, smallest, largest):
    place = [jax.random.randint(jax.random.fold_in(rng, axis), (), 0, length) for axis, length in enumerate(entries.shape)]
    widest = entries.shape.index(max(entries.shape))
    beside = place[:widest] + [(place[widest] + 1) % entries.shape[widest]] + place[widest + 1:]
    return entries.at[tuple(place)].set(smallest).at[tuple(beside)].set(largest)


def block_scale(stream_key, extent, pieces, smallest, high):
    gain, own = 1.0, jax.random.fold_in(stream_key, 6)
    for dim, parts in pieces:
        draws = jnp.exp(jax.random.uniform(jax.random.fold_in(own, dim), (parts,), jnp.float32, smallest / len(pieces), high / len(pieces)))
        gain = gain * jnp.repeat(draws, extent[dim] // parts).reshape([-1 if axis == dim else 1 for axis in range(len(extent))])
    return gain


def split_up(count, total, bound, slope):
    weights = [(1 << 20) // math.isqrt(grade ** slope) + 1 for grade in range(2, count + 1)]
    spare, holding = total - bound - (count - 1), [1] * (count - 1)
    while spare > 0:
        movable = [i for i in range(count - 1) if holding[i] < bound]
        pool, left = sum([weights[i] for i in movable]), spare
        for i in movable:
            more = min(bound - holding[i], max(1, left * weights[i] // pool), spare)
            holding[i] = holding[i] + more
            spare = spare - more
    return np.array([bound] + holding)


def ragged_sizes(stream_key, number_of, total, limit, skew):
    if number_of == 2:
        one = jax.random.randint(stream_key, (), max(1, total - limit), min(limit, total - 1) + 1)
        return jnp.stack([one, total - one])
    sizes = jnp.asarray(split_up(number_of, total, limit, skew), jnp.int32)
    couples = (number_of - 1) // 2
    source_of, taker = sizes[1:1 + 2 * couples:2], sizes[2:2 + 2 * couples:2]
    slack = jnp.minimum(source_of - 1, limit - taker)
    passed = jax.random.randint(jax.random.fold_in(stream_key, 1), (couples,), 0, 1 << 20) % (slack + 1)
    sizes = sizes.at[1:1 + 2 * couples:2].set(source_of - passed).at[2:2 + 2 * couples:2].set(taker + passed)
    return sizes[jax.random.permutation(jax.random.fold_in(stream_key, 2), number_of)]


def noise(own_key, shape, deviation, most, shards=(), held_as=jnp.bfloat16):
    values = deviation * jax.random.normal(own_key, shape, jnp.float32)
    if shards:
        values = values * block_scale(own_key, shape, shards, -0.22, 0.18)
    return jnp.clip(values, -most, most).astype(held_as)


def setup_inputs(seed: int = 0) -> dict:
    seeds = jax.random.split(jax.random.key(seed), 12)
    return {
        "tokens": noise(seeds[0], (REQS, BLOCK, D), 1.0, 6.0, ((0, 16),)),
        "cache_kv": draw_cache_kv(jax.random.fold_in(seeds[11], 71), 0),
        "w_qkv": noise(seeds[2], (D, HEADS, 3 * HEAD_DIM), D ** -0.5, 0.15625, ((1, 16),)),
        "w_out": noise(seeds[3], (HEADS, HEAD_DIM, D), (HEADS * HEAD_DIM) ** -0.5, 0.1875, ((0, 16),)),
        "w_fc": noise(seeds[4], (D, FF), D ** -0.5, 0.15625, ((1, 16),)),
        "w_proj": noise(seeds[5], (FF, D), FF ** -0.5, 0.078125, ((0, 16),)),
        "embed_table": noise(seeds[6], (VOCAB, D), 1.0, 6.0, ((0, 16), (1, 16))),
        "group_ids": jnp.searchsorted(jnp.cumsum(ragged_sizes(seeds[7], NG, REQS, REQS // 2, 1)), jnp.arange(REQS), side="right").astype(jnp.int32),
        "cache_len": draw_cache_len(jax.random.fold_in(seeds[11], 71), 0),
        "accept": place_ends((jax.random.randint(seeds[9], (PASSES, REQS, BLOCK), 0, 3) < 1).astype(jnp.int32), jax.random.fold_in(seeds[9], 1), 0, 1),
        "new_ids": place_ends(jax.random.randint(seeds[10], (PASSES, REQS, BLOCK), 0, VOCAB), jax.random.fold_in(seeds[10], 1), 0, VOCAB - 1).astype(jnp.int32),
    }


def layer_norm(values):
    centre = values - lax.optimization_barrier(jnp.mean(values, -1, keepdims=True))
    spread = lax.optimization_barrier(jnp.mean(centre * centre, -1, keepdims=True))
    return centre * lax.rsqrt(spread + 1e-05)

def attend_request(qkv_row, group_id, cache_kv, cache_len):
    queries = qkv_row[..., :HEAD_DIM].astype(jnp.float32)
    keys_new = qkv_row[..., HEAD_DIM:2 * HEAD_DIM].astype(jnp.float32)
    values_new = qkv_row[..., 2 * HEAD_DIM:].astype(jnp.float32)
    stored = lax.dynamic_index_in_dim(cache_kv, group_id, 0, keepdims=False).astype(jnp.float32)
    length = lax.dynamic_index_in_dim(cache_len, group_id, 0, keepdims=False)
    factor = HEAD_DIM ** (-0.5)
    cached_scores = jnp.einsum('qhd,khd->hqk', queries, stored[..., :HEAD_DIM]) * factor
    live_mask = jnp.arange(CAP, dtype=jnp.int32) < length
    cached_scores = jnp.where(live_mask[None, None, :], cached_scores, -1e+30)
    block_scores = jnp.einsum('qhd,khd->hqk', queries, keys_new) * factor
    scores = jnp.concatenate([cached_scores, block_scores], -1)
    highest = lax.optimization_barrier(jnp.max(scores, -1, keepdims=True))
    weights_raw = jnp.exp(scores - highest)
    totals = lax.optimization_barrier(jnp.sum(weights_raw, -1))
    rounded = lax.optimization_barrier(weights_raw.astype(jnp.bfloat16)).astype(jnp.float32)
    values_all = jnp.concatenate([stored[..., HEAD_DIM:], values_new], 0)
    mixed_heads = jnp.einsum('hqk,khd->qhd', rounded, values_all) / jnp.transpose(totals)[:, :, None]
    return mixed_heads.astype(jnp.bfloat16)

def finish_request(x_row, head_rows, w_out, w_fc, w_proj):
    grouped = head_rows.reshape(BLOCK, N_BLK, HEAD_DEV * HEAD_DIM).astype(jnp.float32)
    out_groups = w_out.reshape(N_BLK, HEAD_DEV * HEAD_DIM, D).astype(jnp.float32)
    partial_terms = jnp.einsum('bjc,jcd->jbd', grouped, out_groups)
    partial_terms = lax.optimization_barrier(partial_terms.astype(jnp.bfloat16)).astype(jnp.float32)
    middle = x_row.astype(jnp.float32) + lax.optimization_barrier(jnp.sum(partial_terms, 0))
    normed = layer_norm(middle).astype(jnp.bfloat16)
    hidden = jax.nn.gelu(jnp.dot(normed, w_fc, preferred_element_type=jnp.float32), approximate=True).astype(jnp.bfloat16)
    hidden_groups = hidden.reshape(BLOCK, N_BLK, FF_DEV).astype(jnp.float32)
    proj_groups = w_proj.reshape(N_BLK, FF_DEV, D).astype(jnp.float32)
    grown_rows = jnp.einsum('bjc,jcd->jbd', hidden_groups, proj_groups)
    grown_rows = lax.optimization_barrier(grown_rows.astype(jnp.bfloat16)).astype(jnp.float32)
    return (middle + lax.optimization_barrier(jnp.sum(grown_rows, 0))).astype(jnp.bfloat16)

def run_layer(current, group_ids, cache_kv, cache_len, w_qkv, w_out, w_fc, w_proj):
    normed = layer_norm(current.astype(jnp.float32)).astype(jnp.bfloat16)
    projected = jnp.einsum('rbd,dhc->rbhc', normed.astype(jnp.float32), w_qkv.astype(jnp.float32)).astype(jnp.bfloat16)

    def attend_one(member):
        return attend_request(member[0], member[1], cache_kv, cache_len)
    head_rows = lax.map(attend_one, (projected, group_ids))

    def finish_one(member):
        return finish_request(member[0], member[1], w_out, w_fc, w_proj)
    return lax.map(finish_one, (current, head_rows))

def reference(tokens, cache_kv, w_qkv, w_out, w_fc, w_proj, embed_table, group_ids, cache_len, accept, new_ids):
    fresh_rows = jnp.take(embed_table, new_ids, axis=0)
    current = tokens
    for pass_index in range(PASSES):
        current = run_layer(current, group_ids, cache_kv, cache_len, w_qkv, w_out, w_fc, w_proj)
        current = jnp.where(accept[pass_index][..., None] == 1, fresh_rows[pass_index], current)
    return current
```

```python
import functools

import jax
import jax.numpy as jnp
from jax import lax
from jax.experimental import pallas as pl
from jax.experimental.pallas import tpu as pltpu
from jax.sharding import PartitionSpec as P

PASSES = 2
MESH = pl.DeviceIdType.MESH
NEG = -1e30


def layer_norm(values):
    centre = values - jnp.mean(values, -1, keepdims=True)
    spread = jnp.mean(centre * centre, -1, keepdims=True)
    return centre * lax.rsqrt(spread + 1e-05)


class Net:
    def __init__(self):
        blk = lax.axis_index("blk")
        self.z = blk // 2
        self.x = blk % 2
        self.right = self.ring(1) * 2 + self.x
        self.left = self.ring(-1) * 2 + self.x
        self.pair = self.z * 2 + 1 - self.x
        self.started = []

    def ring(self, offset):
        return lax.rem(self.z + 8 + offset, 8)

    def greet(self):
        barrier = pltpu.get_barrier_semaphore()
        for other in (self.right, self.left, self.pair):
            pl.semaphore_signal(barrier, inc=1, device_id={"blk": other}, device_id_type=MESH)
        pl.semaphore_wait(barrier, 3)

    def send(self, src, dst, sems, slot, other):
        copy = pltpu.make_async_remote_copy(
            src_ref=src,
            dst_ref=dst,
            send_sem=sems[0].at[slot],
            recv_sem=sems[1].at[slot],
            device_id={"blk": other},
            device_id_type=MESH,
        )
        copy.start()
        self.started.append(copy)

    def arrived(self, dst, sems, slot):
        pltpu.make_async_remote_copy(
            src_ref=dst,
            dst_ref=dst,
            send_sem=sems[0].at[slot],
            recv_sem=sems[1].at[slot],
            device_id={"blk": self.pair},
            device_id_type=MESH,
        ).wait_recv()

    def finish(self):
        for copy in self.started:
            copy.wait_send()


R_A, R_B, R_O, L_A, L_B, L_O, X_A, X_B = 0, 4, 8, 12, 16, 20, 24, 25
GATHER_SLOTS = 33


def gather_begin_low(net, out, sems, half):
    low = out.at[net.z, net.x, 0:half]
    net.send(low, low, sems, R_A + 0, net.right)
    net.send(low, low, sems, L_A + 0, net.left)
    net.send(low, low, sems, X_A, net.pair)


def gather_begin_high(net, out, sems, half):
    high = out.at[net.z, net.x, half : 2 * half]
    net.send(high, high, sems, R_B + 0, net.right)
    net.send(high, high, sems, L_B + 0, net.left)
    net.send(high, high, sems, X_B + 0, net.pair)


def gather_rest(net, out, sems, half):
    other = 1 - net.x
    peer_low = out.at[net.z, other, 0:half]
    net.arrived(peer_low, sems, X_A)
    net.send(peer_low, peer_low, sems, R_O + 0, net.right)
    net.send(peer_low, peer_low, sems, L_O + 0, net.left)
    for step in range(1, 5):
        before, after = net.ring(-step), net.ring(step)
        piece = out.at[before, net.x, 0:half]
        net.arrived(piece, sems, R_A + step - 1)
        if step < 4:
            net.send(piece, piece, sems, R_A + step, net.right)
        piece = out.at[after, net.x, half : 2 * half]
        net.arrived(piece, sems, L_B + step - 1)
        if step < 4:
            net.send(piece, piece, sems, L_B + step, net.left)
        net.send(piece, piece, sems, X_B + (step if step < 4 else 7), net.pair)
        piece = out.at[after, other, 0:half]
        net.arrived(piece, sems, L_O + step - 1)
        if step < 4:
            net.send(piece, piece, sems, L_O + step, net.left)
        if step < 4:
            piece = out.at[after, net.x, 0:half]
            net.arrived(piece, sems, L_A + step - 1)
            if step < 3:
                net.send(piece, piece, sems, L_A + step, net.left)
            piece = out.at[before, net.x, half : 2 * half]
            net.arrived(piece, sems, R_B + step - 1)
            if step < 3:
                net.send(piece, piece, sems, R_B + step, net.right)
            net.send(piece, piece, sems, X_B + 3 + step, net.pair)
            piece = out.at[before, other, 0:half]
            net.arrived(piece, sems, R_O + step - 1)
            if step < 3:
                net.send(piece, piece, sems, R_O + step, net.right)
    for slot, offset in ((0, 0), (1, 1), (2, 2), (3, 3), (7, 4), (4, -1), (5, -2), (6, -3)):
        net.arrived(out.at[net.ring(offset), other, half : 2 * half], sems, X_B + slot)


def gather_kernel(x_ref, out, send_sems, recv_sems):
    net = Net()
    sems = (send_sems, recv_sems)
    half = x_ref.shape[0] // 2
    out[net.z, net.x] = x_ref[...]
    net.greet()
    gather_begin_low(net, out, sems, half)
    gather_begin_high(net, out, sems, half)
    gather_rest(net, out, sems, half)
    net.finish()


def gather_blk(x, collective_id):
    return pl.pallas_call(
        gather_kernel,
        out_shape=jax.ShapeDtypeStruct((8, 2) + x.shape, x.dtype),
        in_specs=[pl.BlockSpec(memory_space=pltpu.VMEM)],
        out_specs=pl.BlockSpec(memory_space=pltpu.VMEM),
        scratch_shapes=[
            pltpu.SemaphoreType.DMA((GATHER_SLOTS,)),
            pltpu.SemaphoreType.DMA((GATHER_SLOTS,)),
        ],
        compiler_params=pltpu.CompilerParams(
            collective_id=collective_id, has_side_effects=True, vmem_limit_bytes=32 << 20
        ),
        name=f"gather_blk_{collective_id}",
    )(x)


P_B, P_A, RR_A, RR_B, LL_A, LL_B = 0, 8, 9, 13, 16, 19
REDUCE_SLOTS = 23


def reduce_kernel(
    part, middle, fresh, accept, out,
    peer_high, peer_low, stage_low, to_right, to_left, right_low, right_high, left_low, left_high,
    send_r, recv_r, send_g, recv_g,
):
    net = Net()
    sems, gather_sems = (send_r, recv_r), (send_g, recv_g)
    half = part.shape[2] // 2
    other = 1 - net.x
    f32 = jnp.float32
    net.greet()

    for slot, offset in enumerate((4, 3, -3, 2, -2, 1, -1, 0)):
        place = net.ring(offset)
        net.send(part.at[place, other, half : 2 * half], peer_high.at[slot], sems, P_B + slot, net.pair)
        if slot == 0:
            net.send(part.at[place, :, 0:half], right_low.at[0], sems, RR_A, net.right)
            place = net.ring(-3)
            net.send(part.at[place, :, 0:half], left_low.at[0], sems, LL_A, net.left)

    def own_high(slot, offset):
        net.arrived(peer_high.at[slot], sems, P_B + slot)
        mine = part[net.ring(offset), net.x, half : 2 * half]
        return mine.astype(f32) + peer_high[slot].astype(f32)

    to_left[...] = own_high(0, 4).astype(jnp.bfloat16)
    net.send(to_left, left_high.at[0], sems, LL_B, net.left)
    to_right[...] = own_high(1, 3).astype(jnp.bfloat16)
    net.send(to_right, right_high.at[0], sems, RR_B, net.right)

    def pass_low(buf, slot, step, offset, target):
        piece = buf.at[step]
        net.arrived(piece, sems, slot + step)
        total = piece[...].astype(f32) + part[net.ring(offset), :, 0:half].astype(f32)
        buf[step] = total.astype(jnp.bfloat16)
        net.send(piece, buf.at[step + 1], sems, slot + step + 1, target)

    def pass_high(buf, slot, step, peer_slot, offset, target):
        total = own_high(peer_slot, offset)
        piece = buf.at[step]
        net.arrived(piece, sems, slot + step)
        buf[step] = (total + piece[...].astype(f32)).astype(jnp.bfloat16)
        net.send(piece, buf.at[step + 1], sems, slot + step + 1, target)

    pass_low(right_low, RR_A, 0, 3, net.right)
    pass_low(left_low, LL_A, 0, -2, net.left)
    pass_high(left_high, LL_B, 0, 2, -3, net.left)
    pass_high(right_high, RR_B, 0, 3, 2, net.right)
    pass_low(right_low, RR_A, 1, 2, net.right)
    pass_low(left_low, LL_A, 1, -1, net.left)
    pass_high(left_high, LL_B, 1, 4, -2, net.left)
    pass_high(right_high, RR_B, 1, 5, 1, net.right)
    pass_low(right_low, RR_A, 2, 1, net.right)
    pass_high(left_high, LL_B, 2, 6, -1, net.left)

    net.arrived(left_low.at[2], sems, LL_A + 2)
    net.arrived(right_low.at[3], sems, RR_A + 3)

    def low_total(parity):
        return (
            part[net.z, parity, 0:half].astype(f32)
            + right_low[3, parity].astype(f32)
            + left_low[2, parity].astype(f32)
        )

    stage_low[...] = low_total(other).astype(jnp.bfloat16)
    net.send(stage_low, peer_low, sems, P_A, net.pair)

    def close(total, rows):
        layer_out = (middle[rows] + total).astype(jnp.bfloat16)
        out[net.z, net.x, rows] = jnp.where(accept[rows] == 1, fresh[rows], layer_out)

    total = own_high(7, 0)
    net.arrived(right_high.at[2], sems, RR_B + 2)
    net.arrived(left_high.at[3], sems, LL_B + 3)
    total = total + right_high[2].astype(f32) + left_high[3].astype(f32)
    close(total, slice(half, 2 * half))
    gather_begin_high(net, out, gather_sems, half)
    total = low_total(net.x)
    net.arrived(peer_low, sems, P_A)
    close(total + peer_low[...].astype(f32), slice(0, half))
    gather_begin_low(net, out, gather_sems, half)
    gather_rest(net, out, gather_sems, half)
    net.finish()


def reduce_blk(part, middle, fresh, accept, collective_id):
    _, _, rows, width = part.shape
    half = rows // 2
    block = (half, width)
    bf16 = jnp.bfloat16
    return pl.pallas_call(
        reduce_kernel,
        out_shape=jax.ShapeDtypeStruct(part.shape, bf16),
        in_specs=[pl.BlockSpec(memory_space=pltpu.VMEM)] * 4,
        out_specs=pl.BlockSpec(memory_space=pltpu.VMEM),
        scratch_shapes=[
            pltpu.VMEM((8,) + block, bf16),
            pltpu.VMEM(block, bf16),
            pltpu.VMEM(block, bf16),
            pltpu.VMEM(block, bf16),
            pltpu.VMEM(block, bf16),
            pltpu.VMEM((4, 2) + block, bf16),
            pltpu.VMEM((3,) + block, bf16),
            pltpu.VMEM((3, 2) + block, bf16),
            pltpu.VMEM((4,) + block, bf16),
            pltpu.SemaphoreType.DMA((REDUCE_SLOTS,)),
            pltpu.SemaphoreType.DMA((REDUCE_SLOTS,)),
            pltpu.SemaphoreType.DMA((GATHER_SLOTS,)),
            pltpu.SemaphoreType.DMA((GATHER_SLOTS,)),
        ],
        compiler_params=pltpu.CompilerParams(
            collective_id=collective_id, has_side_effects=True, vmem_limit_bytes=32 << 20
        ),
        name=f"reduce_blk_{collective_id}",
    )(part, middle, fresh, accept)


def attend_kernel(groups, lengths, queries, own, cache, out, span):
    request = pl.program_id(0)
    length = lengths[request]
    q = queries[0]
    rows = q.shape[0]
    f32 = jnp.float32

    def scores_of(keys):
        return lax.dot_general(q, keys, (((1,), (1,)), ((), ())), preferred_element_type=f32)

    def weigh(weights, values):
        return jnp.dot(weights.astype(jnp.bfloat16), values, preferred_element_type=f32)

    own_block = own[0]
    scores = scores_of(own_block)
    top = jnp.max(scores, -1, keepdims=True)
    weights = jnp.exp(scores - top)
    total = jnp.sum(weights, -1, keepdims=True)
    mixed = weigh(weights, own_block)

    def visit(index, carried):
        top, total, mixed = carried
        start = pl.multiple_of(index * span, span)
        block = cache[0, pl.ds(start, span), :]
        position = start + lax.broadcasted_iota(jnp.int32, (1, span), 1)
        bias = jnp.where(position < length, 0.0, NEG).astype(f32)
        scores = scores_of(block) + bias
        raised = jnp.maximum(top, jnp.max(scores, -1, keepdims=True))
        shrink = jnp.exp(top - raised)
        weights = jnp.exp(scores - raised)
        total = total * shrink + jnp.sum(weights, -1, keepdims=True)
        return raised, total, mixed * shrink + weigh(weights, block)

    blocks = (length + span - 1) // span
    top, total, mixed = lax.fori_loop(0, blocks, visit, (top, total, mixed))
    head = (mixed / total).astype(f32)
    lane = lax.broadcasted_iota(jnp.int32, (rows, 128), 1)

    @pl.when(request == 0)
    def _():
        out[...] = pltpu.roll(head, 64, 1).astype(out.dtype)

    @pl.when(request == 1)
    def _():
        out[...] = jnp.where(lane < 64, out[...].astype(f32), head).astype(out.dtype)


def attend(queries, own, cache, groups, lengths):
    requests, rows, _ = queries.shape
    size = cache.shape[1]
    return pl.pallas_call(
        functools.partial(attend_kernel, span=1024),
        out_shape=jax.ShapeDtypeStruct((rows, 128), jnp.bfloat16),
        grid_spec=pltpu.PrefetchScalarGridSpec(
            num_scalar_prefetch=2,
            grid=(requests,),
            in_specs=[
                pl.BlockSpec((1, rows, 128), lambda r, g, n: (r, 0, 0)),
                pl.BlockSpec((1, rows, 128), lambda r, g, n: (r, 0, 0)),
                pl.BlockSpec((1, size, 128), lambda r, g, n: (g[r], 0, 0)),
            ],
            out_specs=pl.BlockSpec((rows, 128), lambda r, g, n: (0, 0)),
        ),
        compiler_params=pltpu.CompilerParams(vmem_limit_bytes=40 << 20),
        name="attend",
    )(groups, lengths, queries, own, cache)


def shards(
    tokens, cache_kv, w_qkv, w_out, w_fc, w_proj, embed_table, group_ids, cache_len, accept, new_ids
):
    req_index = lax.axis_index("req")
    blk_index = lax.axis_index("blk")
    requests, rows, width = tokens.shape
    kv_width = cache_kv.shape[3]
    head_dim = kv_width // 2
    all_rows = requests * rows
    share = all_rows // 16
    bf16, f32 = jnp.bfloat16, jnp.float32
    my_groups = lax.dynamic_slice_in_dim(group_ids, req_index * requests, requests)
    lengths = jnp.take(cache_len, my_groups)
    every_cache = lax.all_gather(cache_kv[:, :, 0, :], "req", axis=1, tiled=True)
    all_w_out = lax.all_gather(w_out[0], "blk", axis=0, tiled=True)
    vocab_dev = embed_table.shape[0]
    relative = new_ids - req_index * vocab_dev
    inside = (relative >= 0) & (relative < vocab_dev)
    looked = jnp.take(embed_table, jnp.clip(relative, 0, vocab_dev - 1), axis=0)
    looked = jnp.where(inside[..., None], looked, jnp.zeros((), bf16))
    picked = lax.psum_scatter(looked, "req", scatter_dimension=1, tiled=True)
    picked = picked.reshape(PASSES, 16, share, picked.shape[-1])
    mine = lax.all_to_all(picked, "blk", split_axis=1, concat_axis=3, tiled=True)
    mine = mine.reshape(PASSES, share, width)
    my_accept = lax.dynamic_slice_in_dim(
        accept.reshape(PASSES, all_rows, 1), blk_index * share, share, 1
    )
    w_qkv = w_qkv[:, 0, :]
    w_q = jnp.pad(w_qkv[:, :head_dim], ((0, 0), (0, head_dim)))
    w_kv = w_qkv[:, head_dim:]
    current = tokens.reshape(all_rows, width)
    for pass_index in range(PASSES):
        state_f32 = current.astype(f32)
        normed = layer_norm(state_f32).astype(bf16)
        q = jnp.dot(normed, w_q, preferred_element_type=f32).astype(bf16)
        q = q * jnp.asarray(head_dim**-0.5, bf16)
        kv = jnp.dot(normed, w_kv, preferred_element_type=f32).astype(bf16)
        heads = attend(
            q.reshape(requests, rows, kv_width),
            kv.reshape(requests, rows, kv_width),
            every_cache,
            my_groups,
            lengths,
        )
        every_head = gather_blk(heads, 2 * pass_index + 1).reshape(16, rows, requests, head_dim)
        head_rows = jnp.transpose(every_head, (2, 1, 0, 3)).reshape(all_rows, 16 * head_dim)
        middle = state_f32 + jnp.dot(head_rows, all_w_out, preferred_element_type=f32)
        normed_mid = layer_norm(middle).astype(bf16)
        hidden = jax.nn.gelu(
            jnp.dot(normed_mid, w_fc, preferred_element_type=f32), approximate=True
        ).astype(bf16)
        grown = jnp.dot(hidden, w_proj, preferred_element_type=f32).astype(bf16)
        my_middle = lax.dynamic_slice_in_dim(middle, blk_index * share, share, 0)
        current = reduce_blk(
            grown.reshape(8, 2, share, width),
            my_middle,
            mine[pass_index],
            my_accept[pass_index],
            2 * pass_index + 2,
        ).reshape(all_rows, width)
    return current.reshape(requests, rows, width)


def solution(mesh):
    return jax.shard_map(
        shards,
        mesh=mesh,
        in_specs=(
            P("req", None, None),
            P(None, "req", "blk", None),
            P(None, "blk", None),
            P("blk", None, None),
            P(None, "blk"),
            P("blk", None),
            P("req", "blk"),
            P(),
            P(),
            P(None, "req", None),
            P(),
        ),
        out_specs=P("req", None, None),
        check_vma=False,
    )
```

```python
import functools

import jax
import jax.numpy as jnp
from jax import lax
from jax.experimental import pallas as pl
from jax.experimental.pallas import tpu as pltpu
from jax.sharding import PartitionSpec as P

PASSES = 2
MESH = pl.DeviceIdType.MESH
NEG = -1e30


def layer_norm(values):
    centre = values - jnp.mean(values, -1, keepdims=True)
    spread = jnp.mean(centre * centre, -1, keepdims=True)
    return centre * lax.rsqrt(spread + 1e-05)


class Net:
    def __init__(self):
        blk = lax.axis_index("blk")
        self.z = blk // 2
        self.x = blk % 2
        self.right = self.ring(1) * 2 + self.x
        self.left = self.ring(-1) * 2 + self.x
        self.pair = self.z * 2 + 1 - self.x
        self.started = []

    def ring(self, offset):
        return lax.rem(self.z + 8 + offset, 8)

    def greet(self):
        barrier = pltpu.get_barrier_semaphore()
        for other in (self.right, self.left, self.pair):
            pl.semaphore_signal(barrier, inc=1, device_id={"blk": other}, device_id_type=MESH)
        pl.semaphore_wait(barrier, 3)

    def send(self, src, dst, sems, slot, other):
        copy = pltpu.make_async_remote_copy(
            src_ref=src,
            dst_ref=dst,
            send_sem=sems[0].at[slot],
            recv_sem=sems[1].at[slot],
            device_id={"blk": other},
            device_id_type=MESH,
        )
        copy.start()
        self.started.append(copy)

    def arrived(self, dst, sems, slot):
        pltpu.make_async_remote_copy(
            src_ref=dst,
            dst_ref=dst,
            send_sem=sems[0].at[slot],
            recv_sem=sems[1].at[slot],
            device_id={"blk": self.pair},
            device_id_type=MESH,
        ).wait_recv()

    def finish(self):
        for copy in self.started:
            copy.wait_send()


R_A, R_B, R_O, L_A, L_B, L_O, X_A, X_B = 0, 4, 8, 12, 16, 20, 24, 25
GATHER_SLOTS = 33


def gather_begin_low(net, out, sems, half):
    low = out.at[net.z, net.x, 0:half]
    net.send(low, low, sems, R_A + 0, net.right)
    net.send(low, low, sems, L_A + 0, net.left)
    net.send(low, low, sems, X_A, net.pair)


def gather_begin_high(net, out, sems, half):
    high = out.at[net.z, net.x, half : 2 * half]
    net.send(high, high, sems, R_B + 0, net.right)
    net.send(high, high, sems, L_B + 0, net.left)
    net.send(high, high, sems, X_B + 0, net.pair)


def gather_rest(net, out, sems, half):
    other = 1 - net.x
    peer_low = out.at[net.z, other, 0:half]
    net.arrived(peer_low, sems, X_A)
    net.send(peer_low, peer_low, sems, R_O + 0, net.right)
    net.send(peer_low, peer_low, sems, L_O + 0, net.left)
    for step in range(1, 5):
        before, after = net.ring(-step), net.ring(step)
        piece = out.at[before, net.x, 0:half]
        net.arrived(piece, sems, R_A + step - 1)
        if step < 4:
            net.send(piece, piece, sems, R_A + step, net.right)
        piece = out.at[after, net.x, half : 2 * half]
        net.arrived(piece, sems, L_B + step - 1)
        if step < 4:
            net.send(piece, piece, sems, L_B + step, net.left)
        net.send(piece, piece, sems, X_B + (step if step < 4 else 7), net.pair)
        piece = out.at[after, other, 0:half]
        net.arrived(piece, sems, L_O + step - 1)
        if step < 4:
            net.send(piece, piece, sems, L_O + step, net.left)
        if step < 4:
            piece = out.at[after, net.x, 0:half]
            net.arrived(piece, sems, L_A + step - 1)
            if step < 3:
                net.send(piece, piece, sems, L_A + step, net.left)
            piece = out.at[before, net.x, half : 2 * half]
            net.arrived(piece, sems, R_B + step - 1)
            if step < 3:
                net.send(piece, piece, sems, R_B + step, net.right)
            net.send(piece, piece, sems, X_B + 3 + step, net.pair)
            piece = out.at[before, other, 0:half]
            net.arrived(piece, sems, R_O + step - 1)
            if step < 3:
                net.send(piece, piece, sems, R_O + step, net.right)
    for slot, offset in ((0, 0), (1, 1), (2, 2), (3, 3), (7, 4), (4, -1), (5, -2), (6, -3)):
        net.arrived(out.at[net.ring(offset), other, half : 2 * half], sems, X_B + slot)


def gather_kernel(x_ref, out, send_sems, recv_sems):
    net = Net()
    sems = (send_sems, recv_sems)
    half = x_ref.shape[0] // 2
    out[net.z, net.x] = x_ref[...]
    net.greet()
    gather_begin_low(net, out, sems, half)
    gather_begin_high(net, out, sems, half)
    gather_rest(net, out, sems, half)
    net.finish()


def gather_blk(x, collective_id):
    return pl.pallas_call(
        gather_kernel,
        out_shape=jax.ShapeDtypeStruct((8, 2) + x.shape, x.dtype),
        in_specs=[pl.BlockSpec(memory_space=pltpu.VMEM)],
        out_specs=pl.BlockSpec(memory_space=pltpu.VMEM),
        scratch_shapes=[
            pltpu.SemaphoreType.DMA((GATHER_SLOTS,)),
            pltpu.SemaphoreType.DMA((GATHER_SLOTS,)),
        ],
        compiler_params=pltpu.CompilerParams(
            collective_id=collective_id, has_side_effects=True, vmem_limit_bytes=32 << 20
        ),
        name=f"gather_blk_{collective_id}",
    )(x)


P_B, P_A, RR_A, RR_B, LL_A, LL_B = 0, 8, 9, 13, 16, 19
REDUCE_SLOTS = 23


def reduce_kernel(
    part, middle, fresh, accept, out,
    peer_high, peer_low, stage_low, to_right, to_left, right_low, right_high, left_low, left_high,
    send_r, recv_r, send_g, recv_g,
):
    net = Net()
    sems, gather_sems = (send_r, recv_r), (send_g, recv_g)
    half = part.shape[2] // 2
    other = 1 - net.x
    f32 = jnp.float32
    net.greet()

    for slot, offset in enumerate((4, 3, -3, 2, -2, 1, -1, 0)):
        place = net.ring(offset)
        net.send(part.at[place, other, half : 2 * half], peer_high.at[slot], sems, P_B + slot, net.pair)
        if slot == 0:
            net.send(part.at[place, :, 0:half], right_low.at[0], sems, RR_A, net.right)
            place = net.ring(-3)
            net.send(part.at[place, :, 0:half], left_low.at[0], sems, LL_A, net.left)

    def own_high(slot, offset):
        net.arrived(peer_high.at[slot], sems, P_B + slot)
        mine = part[net.ring(offset), net.x, half : 2 * half]
        return mine.astype(f32) + peer_high[slot].astype(f32)

    to_left[...] = own_high(0, 4).astype(jnp.bfloat16)
    net.send(to_left, left_high.at[0], sems, LL_B, net.left)
    to_right[...] = own_high(1, 3).astype(jnp.bfloat16)
    net.send(to_right, right_high.at[0], sems, RR_B, net.right)

    def pass_low(buf, slot, step, offset, target):
        piece = buf.at[step]
        net.arrived(piece, sems, slot + step)
        total = piece[...].astype(f32) + part[net.ring(offset), :, 0:half].astype(f32)
        buf[step] = total.astype(jnp.bfloat16)
        net.send(piece, buf.at[step + 1], sems, slot + step + 1, target)

    def pass_high(buf, slot, step, peer_slot, offset, target):
        total = own_high(peer_slot, offset)
        piece = buf.at[step]
        net.arrived(piece, sems, slot + step)
        buf[step] = (total + piece[...].astype(f32)).astype(jnp.bfloat16)
        net.send(piece, buf.at[step + 1], sems, slot + step + 1, target)

    pass_low(right_low, RR_A, 0, 3, net.right)
    pass_low(left_low, LL_A, 0, -2, net.left)
    pass_high(left_high, LL_B, 0, 2, -3, net.left)
    pass_high(right_high, RR_B, 0, 3, 2, net.right)
    pass_low(right_low, RR_A, 1, 2, net.right)
    pass_low(left_low, LL_A, 1, -1, net.left)
    pass_high(left_high, LL_B, 1, 4, -2, net.left)
    pass_high(right_high, RR_B, 1, 5, 1, net.right)
    pass_low(right_low, RR_A, 2, 1, net.right)
    pass_high(left_high, LL_B, 2, 6, -1, net.left)

    net.arrived(left_low.at[2], sems, LL_A + 2)
    net.arrived(right_low.at[3], sems, RR_A + 3)

    def low_total(parity):
        return (
            part[net.z, parity, 0:half].astype(f32)
            + right_low[3, parity].astype(f32)
            + left_low[2, parity].astype(f32)
        )

    stage_low[...] = low_total(other).astype(jnp.bfloat16)
    net.send(stage_low, peer_low, sems, P_A, net.pair)

    def close(total, rows):
        layer_out = (middle[rows] + total).astype(jnp.bfloat16)
        out[net.z, net.x, rows] = jnp.where(accept[rows] == 1, fresh[rows], layer_out)

    total = own_high(7, 0)
    net.arrived(right_high.at[2], sems, RR_B + 2)
    net.arrived(left_high.at[3], sems, LL_B + 3)
    total = total + right_high[2].astype(f32) + left_high[3].astype(f32)
    close(total, slice(half, 2 * half))
    gather_begin_high(net, out, gather_sems, half)
    total = low_total(net.x)
    net.arrived(peer_low, sems, P_A)
    close(total + peer_low[...].astype(f32), slice(0, half))
    gather_begin_low(net, out, gather_sems, half)
    gather_rest(net, out, gather_sems, half)
    net.finish()


def reduce_blk(part, middle, fresh, accept, collective_id):
    _, _, rows, width = part.shape
    half = rows // 2
    block = (half, width)
    bf16 = jnp.bfloat16
    return pl.pallas_call(
        reduce_kernel,
        out_shape=jax.ShapeDtypeStruct(part.shape, bf16),
        in_specs=[pl.BlockSpec(memory_space=pltpu.VMEM)] * 4,
        out_specs=pl.BlockSpec(memory_space=pltpu.VMEM),
        scratch_shapes=[
            pltpu.VMEM((8,) + block, bf16),
            pltpu.VMEM(block, bf16),
            pltpu.VMEM(block, bf16),
            pltpu.VMEM(block, bf16),
            pltpu.VMEM(block, bf16),
            pltpu.VMEM((4, 2) + block, bf16),
            pltpu.VMEM((3,) + block, bf16),
            pltpu.VMEM((3, 2) + block, bf16),
            pltpu.VMEM((4,) + block, bf16),
            pltpu.SemaphoreType.DMA((REDUCE_SLOTS,)),
            pltpu.SemaphoreType.DMA((REDUCE_SLOTS,)),
            pltpu.SemaphoreType.DMA((GATHER_SLOTS,)),
            pltpu.SemaphoreType.DMA((GATHER_SLOTS,)),
        ],
        compiler_params=pltpu.CompilerParams(
            collective_id=collective_id, has_side_effects=True, vmem_limit_bytes=32 << 20
        ),
        name=f"reduce_blk_{collective_id}",
    )(part, middle, fresh, accept)


PIECES = (0, 2, 1, 3)


def gather_req_kernel(own, out, copy_sem, send_sems, recv_sems):
    me = lax.axis_index("req")
    y, x, core = me // 4, (me // 2) % 2, me % 2

    def device(step, other_x, other_core=False):
        return (
            lax.rem(y + 4 + step, 4) * 4
            + (1 - x if other_x else x) * 2
            + (1 - core if other_core else core)
        )

    up, down, side, twin = device(1, 0), device(-1, 0), device(0, 1), device(0, 0, True)
    barrier = pltpu.get_barrier_semaphore()
    for other in (up, down, side, twin):
        pl.semaphore_signal(barrier, inc=1, device_id={"req": other}, device_id_type=MESH)
    pl.semaphore_wait(barrier, 4)
    started = []

    def copy_of(src, dst, slot, other):
        return pltpu.make_async_remote_copy(
            src_ref=src,
            dst_ref=dst,
            send_sem=send_sems.at[slot],
            recv_sem=recv_sems.at[slot],
            device_id={"req": other},
            device_id_type=MESH,
        )

    def send(src, dst, slot, other):
        copy = copy_of(src, dst, slot, other)
        copy.start()
        started.append(copy)

    def arrived(dst, slot):
        copy_of(dst, dst, slot, twin).wait_recv()

    U0, D0, SIDE, U1, D1, UF0, UF1, DF0, DF1, TWIN = 0, 4, 8, 12, 16, 20, 22, 24, 26, 28
    places = {(0, 0): 0, (0, 1): 1, (-1, 0): 2, (1, 0): 3, (-1, 1): 4, (1, 1): 5, (2, 0): 6, (2, 1): 7}

    def share(step, other_x, g):
        piece = out.at[g, device(step, other_x)]
        send(piece, piece, TWIN + 4 * places[(step, other_x)] + g, twin)

    for g in PIECES:
        dst = out.at[g, me]
        send(own.at[g], dst, U0 + g, up)
        send(own.at[g], dst, D0 + g, down)
        send(own.at[g], dst, SIDE + g, side)
    keep = pltpu.make_async_copy(own, out.at[:, me], copy_sem)
    keep.start()
    for g in PIECES:
        send(own.at[g], out.at[g, me], TWIN + g, twin)

    def from_below(g, other_x, base, forward):
        piece = out.at[g, device(-1, other_x)]
        arrived(piece, base + g)
        if g < 2:
            send(piece, piece, forward + g, up)
        share(-1, other_x, g)

    def from_above(g, other_x, base, forward):
        piece = out.at[g, device(1, other_x)]
        arrived(piece, base + g)
        if g >= 2:
            send(piece, piece, forward + g - 2, down)
        share(1, other_x, g)

    def from_far(g, other_x):
        piece = out.at[g, device(2, other_x)]
        if g < 2:
            arrived(piece, (UF1 if other_x else UF0) + g)
        else:
            arrived(piece, (DF1 if other_x else DF0) + g - 2)
        share(2, other_x, g)

    for g in PIECES:
        piece = out.at[g, side]
        arrived(piece, SIDE + g)
        send(piece, piece, U1 + g, up)
        send(piece, piece, D1 + g, down)
        share(0, 1, g)
        from_below(g, 0, U0, UF0)
        from_above(g, 0, D0, DF0)
    for g in PIECES:
        from_far(g, 0)
        from_below(g, 1, U1, UF1)
        from_above(g, 1, D1, DF1)
    for g in PIECES:
        from_far(g, 1)
    for (step, other_x), place in places.items():
        for g in PIECES:
            arrived(out.at[g, device(step, other_x, True)], TWIN + 4 * place + g)
    keep.wait()
    for copy in started:
        copy.wait_send()


def gather_req(own, collective_id):
    groups = own.shape[0]
    return pl.pallas_call(
        gather_req_kernel,
        out_shape=jax.ShapeDtypeStruct((groups, 16) + own.shape[1:], own.dtype),
        in_specs=[pl.BlockSpec(memory_space=pl.ANY)],
        out_specs=pl.BlockSpec(memory_space=pl.ANY),
        scratch_shapes=[
            pltpu.SemaphoreType.DMA,
            pltpu.SemaphoreType.DMA((60,)),
            pltpu.SemaphoreType.DMA((60,)),
        ],
        compiler_params=pltpu.CompilerParams(
            collective_id=collective_id, has_side_effects=True, vmem_limit_bytes=4 << 20
        ),
        name="gather_req",
    )(own)


SLOTS = 128


def fresh_columns(embed_table, new_ids, req_index):
    vocab_dev = embed_table.shape[0]
    passes = new_ids.shape[0]
    bf16 = jnp.bfloat16
    by_device = jnp.transpose(new_ids.reshape(passes, 16, -1), (1, 0, 2)).reshape(16, -1)
    count = by_device.shape[1]
    earlier = (jnp.arange(count)[:, None] < jnp.arange(count)[None, :]).astype(bf16)

    def ranks(inside):
        return jnp.dot(inside.astype(bf16), earlier, preferred_element_type=jnp.float32).astype(jnp.int32)

    relative = by_device - req_index * vocab_dev
    inside = (relative >= 0) & (relative < vocab_dev)
    rank = jnp.where(inside, ranks(inside), -1)
    chosen = rank[:, None, :] == jnp.arange(SLOTS)[None, :, None]
    wanted = jnp.sum(jnp.where(chosen, relative[:, None, :], 0), -1)
    sent = jnp.take(embed_table, wanted, axis=0)
    got = lax.all_to_all(sent, "req", split_axis=0, concat_axis=0, tiled=True)

    mine = lax.dynamic_index_in_dim(by_device, req_index, 0, keepdims=True)
    owners = jnp.arange(16)[:, None]
    theirs = mine - owners * vocab_dev
    theirs_inside = (theirs >= 0) & (theirs < vocab_dev)
    place = jnp.sum(jnp.where(theirs_inside, owners * SLOTS + ranks(theirs_inside), 0), 0)
    quick = jnp.take(got.reshape(16 * SLOTS, -1), jnp.minimum(place, 16 * SLOTS - 1), axis=0)

    owner = by_device // vocab_dev
    asked = jnp.sum((owner[:, None, :] == owners[None]).astype(jnp.int32), -1)
    crowded = jnp.max(asked) > SLOTS

    def dense():
        looked = jnp.take(embed_table, jnp.clip(relative, 0, vocab_dev - 1).reshape(-1), axis=0)
        looked = jnp.where(inside.reshape(-1)[:, None], looked, jnp.zeros((), bf16))
        return lax.psum_scatter(looked, "req", scatter_dimension=0, tiled=True)

    return lax.cond(crowded, dense, lambda: quick)


def attend_kernel(groups, lengths, queries, own, cache, out, span):
    request = pl.program_id(0)
    length = lengths[request]
    q = queries[0]
    rows = q.shape[0]
    f32 = jnp.float32

    def scores_of(keys):
        return lax.dot_general(q, keys, (((1,), (1,)), ((), ())), preferred_element_type=f32)

    def weigh(weights, values):
        return jnp.dot(weights.astype(jnp.bfloat16), values, preferred_element_type=f32)

    own_block = own[0]
    scores = scores_of(own_block)
    top = jnp.max(scores, -1, keepdims=True)
    weights = jnp.exp(scores - top)
    total = jnp.sum(weights, -1, keepdims=True)
    mixed = weigh(weights, own_block)

    def visit(index, carried):
        top, total, mixed = carried
        start = pl.multiple_of(index * span, span)
        block = cache[0, pl.ds(start, span), :]
        position = start + lax.broadcasted_iota(jnp.int32, (1, span), 1)
        bias = jnp.where(position < length, 0.0, NEG).astype(f32)
        scores = scores_of(block) + bias
        raised = jnp.maximum(top, jnp.max(scores, -1, keepdims=True))
        shrink = jnp.exp(top - raised)
        weights = jnp.exp(scores - raised)
        total = total * shrink + jnp.sum(weights, -1, keepdims=True)
        return raised, total, mixed * shrink + weigh(weights, block)

    blocks = (length + span - 1) // span
    top, total, mixed = lax.fori_loop(0, blocks, visit, (top, total, mixed))
    head = (mixed / total).astype(f32)
    lane = lax.broadcasted_iota(jnp.int32, (rows, 128), 1)

    @pl.when(request == 0)
    def _():
        out[...] = pltpu.roll(head, 64, 1).astype(out.dtype)

    @pl.when(request == 1)
    def _():
        out[...] = jnp.where(lane < 64, out[...].astype(f32), head).astype(out.dtype)


def attend(queries, own, cache, groups, lengths):
    requests, rows, _ = queries.shape
    size = cache.shape[1]
    return pl.pallas_call(
        functools.partial(attend_kernel, span=1024),
        out_shape=jax.ShapeDtypeStruct((rows, 128), jnp.bfloat16),
        grid_spec=pltpu.PrefetchScalarGridSpec(
            num_scalar_prefetch=2,
            grid=(requests,),
            in_specs=[
                pl.BlockSpec((1, rows, 128), lambda r, g, n: (r, 0, 0)),
                pl.BlockSpec((1, rows, 128), lambda r, g, n: (r, 0, 0)),
                pl.BlockSpec((1, size, 128), lambda r, g, n: (g[r], 0, 0)),
            ],
            out_specs=pl.BlockSpec((rows, 128), lambda r, g, n: (0, 0)),
        ),
        compiler_params=pltpu.CompilerParams(vmem_limit_bytes=40 << 20),
        name="attend",
    )(groups, lengths, queries, own, cache)


def shards(
    tokens, cache_kv, w_qkv, w_out, w_fc, w_proj, embed_table, group_ids, cache_len, accept, new_ids
):
    req_index = lax.axis_index("req")
    blk_index = lax.axis_index("blk")
    requests, rows, width = tokens.shape
    kv_width = cache_kv.shape[3]
    head_dim = kv_width // 2
    all_rows = requests * rows
    share = all_rows // 16
    bf16, f32 = jnp.bfloat16, jnp.float32
    my_groups = lax.dynamic_slice_in_dim(group_ids, req_index * requests, requests)
    lengths = jnp.take(cache_len, my_groups)
    every_cache = gather_req(cache_kv[:, :, 0, :], 5).reshape(cache_kv.shape[0], -1, kv_width)
    all_w_out = lax.all_gather(w_out[0], "blk", axis=0, tiled=True)
    picked = fresh_columns(embed_table, new_ids, req_index)
    picked = picked.reshape(PASSES, 16, share, picked.shape[-1])
    mine = lax.all_to_all(picked, "blk", split_axis=1, concat_axis=3, tiled=True)
    mine = mine.reshape(PASSES, share, width)
    my_accept = lax.dynamic_slice_in_dim(
        accept.reshape(PASSES, all_rows, 1), blk_index * share, share, 1
    )
    w_qkv = w_qkv[:, 0, :]
    w_q = jnp.pad(w_qkv[:, :head_dim], ((0, 0), (0, head_dim)))
    w_kv = w_qkv[:, head_dim:]
    current = tokens.reshape(all_rows, width)
    for pass_index in range(PASSES):
        state_f32 = current.astype(f32)
        normed = layer_norm(state_f32).astype(bf16)
        q = jnp.dot(normed, w_q, preferred_element_type=f32).astype(bf16)
        q = q * jnp.asarray(head_dim**-0.5, bf16)
        kv = jnp.dot(normed, w_kv, preferred_element_type=f32).astype(bf16)
        heads = attend(
            q.reshape(requests, rows, kv_width),
            kv.reshape(requests, rows, kv_width),
            every_cache,
            my_groups,
            lengths,
        )
        every_head = gather_blk(heads, 2 * pass_index + 1).reshape(16, rows, requests, head_dim)
        head_rows = jnp.transpose(every_head, (2, 1, 0, 3)).reshape(all_rows, 16 * head_dim)
        middle = state_f32 + jnp.dot(head_rows, all_w_out, preferred_element_type=f32)
        normed_mid = layer_norm(middle).astype(bf16)
        hidden = jax.nn.gelu(
            jnp.dot(normed_mid, w_fc, preferred_element_type=f32), approximate=True
        ).astype(bf16)
        grown = jnp.dot(hidden, w_proj, preferred_element_type=f32).astype(bf16)
        my_middle = lax.dynamic_slice_in_dim(middle, blk_index * share, share, 0)
        current = reduce_blk(
            grown.reshape(8, 2, share, width),
            my_middle,
            mine[pass_index],
            my_accept[pass_index],
            2 * pass_index + 2,
        ).reshape(all_rows, width)
    return current.reshape(requests, rows, width)


def solution(mesh):
    return jax.shard_map(
        shards,
        mesh=mesh,
        in_specs=(
            P("req", None, None),
            P(None, "req", "blk", None),
            P(None, "blk", None),
            P("blk", None, None),
            P(None, "blk"),
            P("blk", None),
            P("req", "blk"),
            P(),
            P(),
            P(None, "req", None),
            P(),
        ),
        out_specs=P("req", None, None),
        check_vma=False,
    )
```

```python
import functools

import jax
import jax.numpy as jnp
from jax import lax
from jax.experimental import pallas as pl
from jax.experimental.pallas import tpu as pltpu
from jax.sharding import PartitionSpec as P

PASSES = 2
MESH = pl.DeviceIdType.MESH
NEG = -1e30


def layer_norm(values):
    centre = values - jnp.mean(values, -1, keepdims=True)
    spread = jnp.mean(centre * centre, -1, keepdims=True)
    return centre * lax.rsqrt(spread + 1e-05)


class Net:
    def __init__(self):
        self.blk = lax.axis_index("blk")
        self.z = self.blk // 2
        self.x = self.blk % 2
        self.right = self.ring(1) * 2 + self.x
        self.left = self.ring(-1) * 2 + self.x
        self.pair = self.z * 2 + 1 - self.x
        self.started = []

    def ring(self, offset):
        return lax.rem(self.z + 8 + offset, 8)

    def greet(self, axis="blk", others=None):
        barrier = pltpu.get_barrier_semaphore()
        others = (self.right, self.left, self.pair) if others is None else others
        for other in others:
            pl.semaphore_signal(barrier, inc=1, device_id={axis: other}, device_id_type=MESH)
        pl.semaphore_wait(barrier, len(others))

    def copy_of(self, src, dst, sems, slot, other, axis):
        return pltpu.make_async_remote_copy(
            src_ref=src,
            dst_ref=dst,
            send_sem=sems[0].at[slot],
            recv_sem=sems[1].at[slot],
            device_id={axis: other},
            device_id_type=MESH,
        )

    def send(self, src, dst, sems, slot, other, axis="blk"):
        copy = self.copy_of(src, dst, sems, slot, other, axis)
        copy.start()
        self.started.append(copy)

    def arrived(self, dst, sems, slot):
        self.copy_of(dst, dst, sems, slot, self.pair, "blk").wait_recv()

    def finish(self):
        for copy in self.started:
            copy.wait_send()


def sem_pair(count):
    return [pltpu.SemaphoreType.DMA((count,)), pltpu.SemaphoreType.DMA((count,))]


def whole(count):
    return [pl.BlockSpec(memory_space=pltpu.VMEM)] * count


RING_A, RING_B, RING_C, RING_D = 0, 4, 7, 10
RING_SLOTS = 14


def ring_begin(net, out, sems, half, high):
    piece = out.at[net.z, half : 2 * half] if high else out.at[net.z, 0:half]
    net.send(piece, piece, sems, RING_B if high else RING_A, net.right)
    net.send(piece, piece, sems, RING_D if high else RING_C, net.left)


def ring_rest(net, out, sems, half):
    def take(offset, high, slot, last, target):
        at = net.ring(offset)
        piece = out.at[at, half : 2 * half] if high else out.at[at, 0:half]
        net.arrived(piece, sems, slot)
        if not last:
            net.send(piece, piece, sems, slot + 1, target)

    for step in range(1, 5):
        take(-step, False, RING_A + step - 1, step == 4, net.right)
        take(step, True, RING_D + step - 1, step == 4, net.left)
        if step < 4:
            take(-step, True, RING_B + step - 1, step == 3, net.right)
            take(step, False, RING_C + step - 1, step == 3, net.left)


def heads_kernel(heads, *refs, with_fresh):
    if with_fresh:
        picked, out, mine, peer, copy_sem, *sem_refs = refs
    else:
        out, peer, *sem_refs = refs
    net = Net()
    ring_sems, pair_sems = tuple(sem_refs[0:2]), tuple(sem_refs[2:4])
    half = heads.shape[1] // 2
    if with_fresh:
        net.greet(others=[lax.rem(net.blk + step, 16) for step in range(1, 16)])
    else:
        net.greet()
    parts = (slice(0, half), slice(half, 2 * half))
    for part, rows in enumerate(parts):
        net.send(heads.at[1 - net.x, rows], peer.at[rows], pair_sems, part, net.pair)
    if with_fresh:
        fresh_sems = tuple(sem_refs[4:6])
        keep = pltpu.make_async_copy(picked.at[net.blk], mine.at[net.blk], copy_sem)
        keep.start()
    for part, rows in enumerate(parts):
        net.arrived(peer.at[rows], pair_sems, part)
        out[net.z, rows] = heads[net.x, rows] + peer[rows]
        ring_begin(net, out, ring_sems, half, part == 1)
    if with_fresh:
        for step in range(1, 16):
            other = lax.rem(net.blk + step, 16)
            net.send(picked.at[other], mine.at[net.blk], fresh_sems, step - 1, other)
    ring_rest(net, out, ring_sems, half)
    if with_fresh:
        for step in range(1, 16):
            net.arrived(mine.at[lax.rem(net.blk + 16 - step, 16)], fresh_sems, step - 1)
        keep.wait()
    net.finish()


def gather_heads(heads, picked, collective_id):
    _, rows, lanes = heads.shape
    with_fresh = picked is not None
    shape = jax.ShapeDtypeStruct((8, rows, lanes), heads.dtype)
    scratch = [pltpu.VMEM((rows, lanes), heads.dtype)]
    sems = sem_pair(RING_SLOTS) + sem_pair(2)
    if with_fresh:
        scratch = scratch + [pltpu.SemaphoreType.DMA]
        sems = sems + sem_pair(15)
        shapes = (shape, jax.ShapeDtypeStruct(picked.shape, picked.dtype))
        operands = (heads, picked)
    else:
        shapes, operands = (shape,), (heads,)
    return pl.pallas_call(
        functools.partial(heads_kernel, with_fresh=with_fresh),
        out_shape=shapes,
        in_specs=whole(len(operands)),
        out_specs=tuple(whole(len(shapes))),
        scratch_shapes=scratch + sems,
        compiler_params=pltpu.CompilerParams(
            collective_id=collective_id, has_side_effects=True, vmem_limit_bytes=16 << 20
        ),
        name=f"gather_heads_{collective_id}",
    )(*operands)


def mlp_kernel(
    every_head, current, w_out, w_fc, w_proj, w_fc_b, w_proj_b, w_fc_c, w_proj_c, grown, my_middle,
    head_rows, middle,
):
    f32, bf16 = jnp.float32, jnp.bfloat16
    for z in range(8):
        head_rows[:, 128 * z : 128 * (z + 1)] = every_head[z]
    middle[...] = current[...].astype(f32) + jnp.dot(
        head_rows[...], w_out[...], preferred_element_type=f32
    )
    share = my_middle.shape[0]
    start = pl.multiple_of(lax.axis_index("blk") // 2 * share, share)
    my_middle[...] = middle[pl.ds(start, share), :]
    normed = layer_norm(middle[...]).astype(bf16)

    def hidden(weights):
        raw = jnp.dot(normed, weights[...], preferred_element_type=f32)
        return jax.nn.gelu(raw, approximate=True).astype(bf16)

    def back(rows, weights):
        return jnp.dot(rows, weights[...], preferred_element_type=f32)

    first, second, third = hidden(w_fc), hidden(w_fc_b), hidden(w_fc_c)
    grown[...] = (back(first, w_proj) + back(second, w_proj_b) + back(third, w_proj_c)).astype(bf16)


def mlp(every_head, current, weights):
    rows, width = current.shape
    return pl.pallas_call(
        mlp_kernel,
        out_shape=(
            jax.ShapeDtypeStruct((rows, width), jnp.bfloat16),
            jax.ShapeDtypeStruct((rows // 8, width), jnp.float32),
        ),
        in_specs=whole(2 + len(weights)),
        out_specs=tuple(whole(2)),
        scratch_shapes=[
            pltpu.VMEM((rows, 8 * every_head.shape[2]), jnp.bfloat16),
            pltpu.VMEM((rows, width), jnp.float32),
        ],
        compiler_params=pltpu.CompilerParams(vmem_limit_bytes=40 << 20),
        name="mlp",
    )(every_head, current, *weights)


def project(rows_f32, weights):
    bf16 = jnp.bfloat16
    normed = layer_norm(rows_f32).astype(bf16)
    got = jnp.dot(normed, weights, preferred_element_type=jnp.float32).astype(bf16)
    lane = lax.broadcasted_iota(jnp.int32, (1, got.shape[1]), 1)
    return (got.astype(jnp.float32) * jnp.where(lane < 128, 0.125, 1.0)).astype(bf16)


def reduce_kernel(part, middle, fresh, accept, *refs, last):
    if last:
        out, *refs = refs
    else:
        w_own, w_pair, out, qkv, stage, *refs = refs
    right_low, right_high, left_low, left_high, *sem_refs = refs
    net = Net()
    sems, gather_sems = tuple(sem_refs[0:2]), tuple(sem_refs[2:4])
    half = part.shape[1] // 2
    f32, bf16 = jnp.float32, jnp.bfloat16
    low, high = slice(0, half), slice(half, 2 * half)
    net.greet()

    def begin(buf, rows, slot, offset, target):
        net.send(part.at[net.ring(offset), rows], buf.at[0], sems, slot, target)

    def hand_on(buf, rows, slot, step, offset, target):
        piece = buf.at[step]
        net.arrived(piece, sems, slot + step)
        total = piece[...].astype(f32) + part[net.ring(offset), rows].astype(f32)
        buf[step] = total.astype(bf16)
        net.send(piece, buf.at[step + 1], sems, slot + step + 1, target)

    begin(right_low, low, RING_A, 4, net.right)
    begin(left_high, high, RING_D, -4, net.left)
    begin(right_high, high, RING_B, 3, net.right)
    begin(left_low, low, RING_C, -3, net.left)
    for step in range(3):
        hand_on(right_low, low, RING_A, step, 3 - step, net.right)
        hand_on(left_high, high, RING_D, step, step - 3, net.left)
        if step < 2:
            hand_on(right_high, high, RING_B, step, 2 - step, net.right)
            hand_on(left_low, low, RING_C, step, step - 2, net.left)

    def close(rows, from_left, from_right):
        total = part[net.z, rows].astype(f32) + from_left.astype(f32) + from_right.astype(f32)
        layer_out = (middle[rows] + total).astype(bf16)
        return jnp.where(accept[rows] == 1, fresh[rows], layer_out)

    net.arrived(left_low.at[2], sems, RING_C + 2)
    net.arrived(right_low.at[3], sems, RING_A + 3)
    result = close(low, right_low[3], left_low[2])
    if last:
        out[net.x, net.z, low] = result
        gather_begin_low(net, out, gather_sems, half)
    else:
        out[net.z, low] = result
        ring_begin(net, out, gather_sems, half, False)
    net.arrived(right_high.at[2], sems, RING_B + 2)
    net.arrived(left_high.at[3], sems, RING_D + 3)
    result = close(high, right_high[2], left_high[3])
    if last:
        out[net.x, net.z, high] = result
        gather_begin_high(net, out, gather_sems, half)
        gather_rest(net, out, gather_sems, half)
    else:
        out[net.z, high] = result
        ring_begin(net, out, gather_sems, half, True)
        ring_rest(net, out, gather_sems, half)
        swap_sems = tuple(sem_refs[4:6])
        rows_f32 = out[...].reshape(8 * 2 * half, out.shape[2]).astype(f32)
        stage[...] = project(rows_f32, w_pair[...])
        net.send(stage, qkv.at[net.x], swap_sems, 0, net.pair)
        qkv[net.x] = project(rows_f32, w_own[...])
        net.arrived(qkv.at[1 - net.x], swap_sems, 0)
    net.finish()


def reduce_blk(part, middle, fresh, accept, w_pair, collective_id):
    blocks, rows, width = part.shape
    bf16 = jnp.bfloat16
    last = w_pair is None
    block = (rows // 2, width)
    rings = [pltpu.VMEM((count,) + block, bf16) for count in (4, 3, 3, 4)]
    operands = (part, middle, fresh, accept)
    if last:
        shapes = (jax.ShapeDtypeStruct((2,) + part.shape, bf16),)
        sems = sem_pair(RING_SLOTS) + sem_pair(GATHER_SLOTS)
    else:
        operands = operands + w_pair
        columns = w_pair[0].shape[1]
        shapes = (
            jax.ShapeDtypeStruct(part.shape, bf16),
            jax.ShapeDtypeStruct((2, blocks * rows, columns), bf16),
        )
        rings = [pltpu.VMEM((blocks * rows, columns), bf16)] + rings
        sems = sem_pair(RING_SLOTS) + sem_pair(RING_SLOTS) + sem_pair(1)
    return pl.pallas_call(
        functools.partial(reduce_kernel, last=last),
        out_shape=shapes,
        in_specs=whole(len(operands)),
        out_specs=tuple(whole(len(shapes))),
        scratch_shapes=rings + sems,
        compiler_params=pltpu.CompilerParams(
            collective_id=collective_id, has_side_effects=True, vmem_limit_bytes=40 << 20
        ),
        name=f"reduce_blk_{collective_id}",
    )(*operands)


R_A, R_B, R_O, L_A, L_B, L_O, X_A, X_B = 0, 4, 8, 12, 16, 20, 24, 25
GATHER_SLOTS = 33


def gather_begin_low(net, out, sems, half):
    low = out.at[net.x, net.z, 0:half]
    net.send(low, low, sems, R_A + 0, net.right)
    net.send(low, low, sems, L_A + 0, net.left)
    net.send(low, low, sems, X_A, net.pair)


def gather_begin_high(net, out, sems, half):
    high = out.at[net.x, net.z, half : 2 * half]
    net.send(high, high, sems, R_B + 0, net.right)
    net.send(high, high, sems, L_B + 0, net.left)
    net.send(high, high, sems, X_B + 0, net.pair)


def gather_rest(net, out, sems, half):
    other = 1 - net.x
    peer_low = out.at[other, net.z, 0:half]
    net.arrived(peer_low, sems, X_A)
    net.send(peer_low, peer_low, sems, R_O + 0, net.right)
    net.send(peer_low, peer_low, sems, L_O + 0, net.left)
    for step in range(1, 5):
        before, after = net.ring(-step), net.ring(step)
        piece = out.at[net.x, before, 0:half]
        net.arrived(piece, sems, R_A + step - 1)
        if step < 4:
            net.send(piece, piece, sems, R_A + step, net.right)
        piece = out.at[net.x, after, half : 2 * half]
        net.arrived(piece, sems, L_B + step - 1)
        if step < 4:
            net.send(piece, piece, sems, L_B + step, net.left)
        net.send(piece, piece, sems, X_B + (step if step < 4 else 7), net.pair)
        piece = out.at[other, after, 0:half]
        net.arrived(piece, sems, L_O + step - 1)
        if step < 4:
            net.send(piece, piece, sems, L_O + step, net.left)
        if step < 4:
            piece = out.at[net.x, after, 0:half]
            net.arrived(piece, sems, L_A + step - 1)
            if step < 3:
                net.send(piece, piece, sems, L_A + step, net.left)
            piece = out.at[net.x, before, half : 2 * half]
            net.arrived(piece, sems, R_B + step - 1)
            if step < 3:
                net.send(piece, piece, sems, R_B + step, net.right)
            net.send(piece, piece, sems, X_B + 3 + step, net.pair)
            piece = out.at[other, before, 0:half]
            net.arrived(piece, sems, R_O + step - 1)
            if step < 3:
                net.send(piece, piece, sems, R_O + step, net.right)
    for slot, offset in ((0, 0), (1, 1), (2, 2), (3, 3), (7, 4), (4, -1), (5, -2), (6, -3)):
        net.arrived(out.at[other, net.ring(offset), half : 2 * half], sems, X_B + slot)


PIECES = (0, 2, 1, 3)


def start_kernel(
    own, w_own, sent, out, w_all, got, copy_sems, send_sems, recv_sems, send_w, recv_w, send_f, recv_f
):
    net = Net()
    me = lax.axis_index("req")
    y, x, core = me // 4, (me // 2) % 2, me % 2

    def device(step, other_x, other_core=False):
        return (
            lax.rem(y + 4 + step, 4) * 4
            + (1 - x if other_x else x) * 2
            + (1 - core if other_core else core)
        )

    up, down, side, twin = device(1, 0), device(-1, 0), device(0, 1), device(0, 0, True)
    barrier = pltpu.get_barrier_semaphore()
    for step in range(1, 16):
        other = lax.rem(me + step, 16)
        pl.semaphore_signal(barrier, inc=1, device_id={"req": other}, device_id_type=MESH)
    for other in (net.right, net.left, net.pair):
        pl.semaphore_signal(barrier, inc=1, device_id={"blk": other}, device_id_type=MESH)
    pl.semaphore_wait(barrier, 18)
    w_sems, f_sems = (send_w, recv_w), (send_f, recv_f)
    started = []

    def copy_of(src, dst, slot, other):
        return pltpu.make_async_remote_copy(
            src_ref=src,
            dst_ref=dst,
            send_sem=send_sems.at[slot],
            recv_sem=recv_sems.at[slot],
            device_id={"req": other},
            device_id_type=MESH,
        )

    def send(src, dst, slot, other):
        copy = copy_of(src, dst, slot, other)
        copy.start()
        started.append(copy)

    def arrived(dst, slot):
        copy_of(dst, dst, slot, twin).wait_recv()

    U0, D0, SIDE, U1, D1, UF0, UF1, DF0, DF1, TWIN = 0, 4, 8, 12, 16, 20, 22, 24, 26, 28
    places = {(0, 0): 0, (0, 1): 1, (-1, 0): 2, (1, 0): 3, (-1, 1): 4, (1, 1): 5, (2, 0): 6, (2, 1): 7}

    def share(step, other_x, g):
        piece = out.at[g, device(step, other_x)]
        send(piece, piece, TWIN + 4 * places[(step, other_x)] + g, twin)

    for g in PIECES:
        dst = out.at[g, me]
        send(own.at[g], dst, U0 + g, up)
        send(own.at[g], dst, D0 + g, down)
        send(own.at[g], dst, SIDE + g, side)
    RO, LO, RQ, LQ, PX = 0, 4, 7, 10, 14
    w_mine, w_peer = w_all.at[net.z, net.x], w_all.at[net.z, 1 - net.x]
    net.send(w_own, w_mine, w_sems, PX, net.pair)
    net.send(w_own, w_mine, w_sems, RO, net.right)
    net.send(w_own, w_mine, w_sems, LO, net.left)
    for step in range(1, 16):
        other = lax.rem(me + step, 16)
        net.send(sent.at[other], got.at[me], f_sems, step - 1, other, "req")
    keeps = [
        pltpu.make_async_copy(own, out.at[:, me], copy_sems.at[0]),
        pltpu.make_async_copy(w_own, w_mine, copy_sems.at[1]),
        pltpu.make_async_copy(sent.at[me], got.at[me], copy_sems.at[2]),
    ]
    for keep in keeps:
        keep.start()

    def w_peer_begin():
        net.arrived(w_peer, w_sems, PX)
        net.send(w_peer, w_peer, w_sems, RQ, net.right)
        net.send(w_peer, w_peer, w_sems, LQ, net.left)

    def w_step(step, parity, slot_r, slot_l, last_r, last_l):
        if step < last_r:
            piece = w_all.at[net.ring(-1 - step), parity]
            net.arrived(piece, w_sems, slot_r + step)
            if step < last_r - 1:
                net.send(piece, piece, w_sems, slot_r + step + 1, net.right)
        if step < last_l:
            piece = w_all.at[net.ring(1 + step), parity]
            net.arrived(piece, w_sems, slot_l + step)
            if step < last_l - 1:
                net.send(piece, piece, w_sems, slot_l + step + 1, net.left)

    def w_mine_step(step):
        w_step(step, net.x, RO, LO, 4, 3)

    def w_peer_step(step):
        w_step(step, 1 - net.x, RQ, LQ, 3, 4)

    w_order = iter(
        [w_peer_begin, lambda: w_mine_step(0), lambda: w_peer_step(0), lambda: w_mine_step(1),
         lambda: w_peer_step(1), lambda: w_mine_step(2), lambda: w_peer_step(2)]
    )
    for g in PIECES:
        send(own.at[g], out.at[g, me], TWIN + g, twin)

    def from_below(g, other_x, base, forward):
        piece = out.at[g, device(-1, other_x)]
        arrived(piece, base + g)
        if g < 2:
            send(piece, piece, forward + g, up)
        share(-1, other_x, g)

    def from_above(g, other_x, base, forward):
        piece = out.at[g, device(1, other_x)]
        arrived(piece, base + g)
        if g >= 2:
            send(piece, piece, forward + g - 2, down)
        share(1, other_x, g)

    def from_far(g, other_x):
        piece = out.at[g, device(2, other_x)]
        if g < 2:
            arrived(piece, (UF1 if other_x else UF0) + g)
        else:
            arrived(piece, (DF1 if other_x else DF0) + g - 2)
        share(2, other_x, g)

    for g in PIECES:
        piece = out.at[g, side]
        arrived(piece, SIDE + g)
        send(piece, piece, U1 + g, up)
        send(piece, piece, D1 + g, down)
        share(0, 1, g)
        from_below(g, 0, U0, UF0)
        from_above(g, 0, D0, DF0)
        next(w_order)()
    for g in PIECES:
        from_far(g, 0)
        from_below(g, 1, U1, UF1)
        from_above(g, 1, D1, DF1)
        next(w_order, lambda: None)()
    for g in PIECES:
        from_far(g, 1)
    for (step, other_x), place in places.items():
        for g in PIECES:
            arrived(out.at[g, device(step, other_x, True)], TWIN + 4 * place + g)
    w_mine_step(3)
    w_peer_step(3)
    for step in range(1, 16):
        net.arrived(got.at[lax.rem(me + 16 - step, 16)], f_sems, step - 1)
    for keep in keeps:
        keep.wait()
    for copy in started:
        copy.wait_send()
    net.finish()


def start_gathers(own, w_own, sent, collective_id):
    groups = own.shape[0]
    anywhere = pl.BlockSpec(memory_space=pl.ANY)
    return pl.pallas_call(
        start_kernel,
        out_shape=(
            jax.ShapeDtypeStruct((groups, 16) + own.shape[1:], own.dtype),
            jax.ShapeDtypeStruct((8, 2) + w_own.shape, w_own.dtype),
            jax.ShapeDtypeStruct(sent.shape, sent.dtype),
        ),
        in_specs=[anywhere] * 3,
        out_specs=(anywhere,) * 3,
        scratch_shapes=[pltpu.SemaphoreType.DMA((3,))] + sem_pair(60) + sem_pair(15) + sem_pair(15),
        compiler_params=pltpu.CompilerParams(
            collective_id=collective_id, has_side_effects=True, vmem_limit_bytes=4 << 20
        ),
        name="start_gathers",
    )(own, w_own, sent)


SLOTS = 128


class Fresh:
    def __init__(self, embed_table, new_ids, req_index):
        self.table, self.req_index = embed_table, req_index
        passes = new_ids.shape[0]
        by_device = new_ids.reshape(passes, 16, 2, 8, -1)
        self.ids = jnp.transpose(by_device, (1, 3, 2, 0, 4)).reshape(16, -1)
        count = self.ids.shape[1]
        places = jnp.arange(count)
        self.earlier = (places[:, None] < places[None, :]).astype(jnp.bfloat16)

    def ranks(self, inside):
        got = jnp.dot(inside.astype(jnp.bfloat16), self.earlier, preferred_element_type=jnp.float32)
        return got.astype(jnp.int32)

    def sent(self):
        vocab_dev = self.table.shape[0]
        relative = self.ids - self.req_index * vocab_dev
        inside = (relative >= 0) & (relative < vocab_dev)
        rank = jnp.where(inside, self.ranks(inside), -1)
        chosen = rank[:, None, :] == jnp.arange(SLOTS)[None, :, None]
        wanted = jnp.sum(jnp.where(chosen, relative[:, None, :], 0), -1)
        rows = jnp.take(self.table, wanted, axis=0)
        return jnp.pad(rows, ((0, 0), (0, 0), (0, 128 - rows.shape[2])))

    def picked(self, got):
        vocab_dev, columns = self.table.shape
        mine = lax.dynamic_index_in_dim(self.ids, self.req_index, 0, keepdims=True)
        owners = jnp.arange(16)[:, None]
        theirs = mine - owners * vocab_dev
        inside = (theirs >= 0) & (theirs < vocab_dev)
        place = jnp.sum(jnp.where(inside, owners * SLOTS + self.ranks(inside), 0), 0)
        quick = jnp.take(got.reshape(16 * SLOTS, -1), jnp.minimum(place, 16 * SLOTS - 1), axis=0)

        owner = self.ids // vocab_dev
        asked = jnp.sum((owner[:, None, :] == owners[None]).astype(jnp.int32), -1)
        crowded = jnp.max(asked) > SLOTS

        def dense():
            relative = (self.ids - self.req_index * vocab_dev).reshape(-1)
            here = (relative >= 0) & (relative < vocab_dev)
            looked = jnp.take(self.table, jnp.clip(relative, 0, vocab_dev - 1), axis=0)
            looked = jnp.where(here[:, None], looked, jnp.zeros((), jnp.bfloat16))
            summed = lax.psum_scatter(looked, "req", scatter_dimension=0, tiled=True)
            return jnp.pad(summed, ((0, 0), (0, 128 - columns)))

        chosen = lax.cond(crowded, dense, lambda: quick)
        return chosen.reshape(16, -1, chosen.shape[1])


def attend_kernel(groups, lengths, rows_or_qkv, *refs, span, first):
    if first:
        weights, cache, out = refs
        qkv = project(rows_or_qkv[0].astype(jnp.float32), weights[...])
    else:
        cache, out = refs
        qkv = rows_or_qkv[0]
    length = lengths[pl.program_id(0)]
    q, own_block = qkv[:, 0:128], qkv[:, 128:256]
    f32 = jnp.float32

    def scores_of(keys):
        return lax.dot_general(q, keys, (((1,), (1,)), ((), ())), preferred_element_type=f32)

    def weigh(weights, values):
        return jnp.dot(weights.astype(jnp.bfloat16), values, preferred_element_type=f32)

    scores = scores_of(own_block)
    top = jnp.max(scores, -1, keepdims=True)
    weights = jnp.exp(scores - top)
    total = jnp.sum(weights, -1, keepdims=True)
    mixed = weigh(weights, own_block)

    def visit(index, carried):
        top, total, mixed = carried
        start = pl.multiple_of(index * span, span)
        block = cache[0, pl.ds(start, span), :]
        position = start + lax.broadcasted_iota(jnp.int32, (1, span), 1)
        bias = jnp.where(position < length, 0.0, NEG).astype(f32)
        scores = scores_of(block) + bias
        raised = jnp.maximum(top, jnp.max(scores, -1, keepdims=True))
        shrink = jnp.exp(top - raised)
        weights = jnp.exp(scores - raised)
        total = total * shrink + jnp.sum(weights, -1, keepdims=True)
        return raised, total, mixed * shrink + weigh(weights, block)

    blocks = (length + span - 1) // span
    top, total, mixed = lax.fori_loop(0, blocks, visit, (top, total, mixed))
    head = mixed / total
    parity = lax.axis_index("blk") % 2
    lane = lax.broadcasted_iota(jnp.int32, (1, 128), 1)
    moved = jnp.where(parity == 0, pltpu.roll(head, 64, 1), head)
    out[0] = jnp.where(lane // 64 == parity, moved, 0.0).astype(out.dtype)


def attend(rows_or_qkv, weights, cache, groups, lengths):
    requests, rows, width = rows_or_qkv.shape
    size = cache.shape[1]
    first = weights is not None
    in_specs = [pl.BlockSpec((1, rows, width), lambda r, g, n: (r, 0, 0))]
    operands = (rows_or_qkv,)
    if first:
        in_specs.append(pl.BlockSpec(weights.shape, lambda r, g, n: (0, 0)))
        operands = operands + (weights,)
    in_specs.append(pl.BlockSpec((1, size, 128), lambda r, g, n: (g[r], 0, 0)))
    return pl.pallas_call(
        functools.partial(attend_kernel, span=1024, first=first),
        out_shape=jax.ShapeDtypeStruct((requests, rows, 128), jnp.bfloat16),
        grid_spec=pltpu.PrefetchScalarGridSpec(
            num_scalar_prefetch=2,
            grid=(requests,),
            in_specs=in_specs,
            out_specs=pl.BlockSpec((1, rows, 128), lambda r, g, n: (r, 0, 0)),
        ),
        compiler_params=pltpu.CompilerParams(vmem_limit_bytes=40 << 20),
        name="attend",
    )(groups, lengths, *operands, cache)


def shards(
    tokens, cache_kv, w_qkv, w_out, w_fc, w_proj, embed_table, group_ids, cache_len, accept, new_ids
):
    req_index = lax.axis_index("req")
    blk_index = lax.axis_index("blk")
    z, x, core = blk_index // 2, blk_index % 2, req_index % 2
    requests, rows, width = tokens.shape
    kv_width = cache_kv.shape[3]
    head_dim = kv_width // 2
    share = rows // 8
    my_groups = lax.dynamic_slice_in_dim(group_ids, req_index * requests, requests)
    lengths = jnp.take(cache_len, my_groups)
    pairs = [(index, index ^ 1) for index in range(16)]
    hidden = w_fc.shape[1] // 2
    w_fc_half = lax.dynamic_slice_in_dim(w_fc, core * hidden, hidden, 1)
    w_proj_half = lax.dynamic_slice_in_dim(w_proj, core * hidden, hidden, 0)
    w_fc_b, w_proj_b = (lax.ppermute(half, "blk", pairs) for half in (w_fc_half, w_proj_half))
    w_fc_c, w_proj_c = (lax.ppermute(half, "req", pairs) for half in (w_fc_b, w_proj_b))
    w_qkv = w_qkv[:, 0, :]
    w_own = jnp.concatenate(
        [w_qkv[:, :head_dim], jnp.zeros_like(w_qkv[:, :head_dim]), w_qkv[:, head_dim:]], 1
    )
    w_other = lax.ppermute(w_own, "blk", pairs)

    asked = Fresh(embed_table, new_ids, req_index)
    every_cache, w_out_all, got = start_gathers(cache_kv[:, :, 0, :], w_out[0], asked.sent(), 1)
    every_cache = every_cache.reshape(cache_kv.shape[0], -1, kv_width)
    w_out_all = w_out_all.reshape(16 * head_dim, width)
    my_accept = lax.dynamic_index_in_dim(accept, x, 1, keepdims=False)
    my_accept = lax.dynamic_slice_in_dim(my_accept, z * share, share, 1)[..., None]
    weights = (w_out_all, w_fc, w_proj, w_fc_b, w_proj_b, w_fc_c, w_proj_c)

    heads = attend(tokens, w_own, every_cache, my_groups, lengths)
    every_head, mine = gather_heads(heads, asked.picked(got), 2)
    columns = embed_table.shape[1]
    mine = jnp.transpose(mine[:, :, :columns], (1, 0, 2)).reshape(PASSES, share, width)
    current = lax.dynamic_index_in_dim(tokens, x, 0, keepdims=False)
    for pass_index in range(PASSES):
        last = pass_index == PASSES - 1
        grown, my_middle = mlp(every_head, current, weights)
        done = reduce_blk(
            grown.reshape(8, share, width),
            my_middle,
            mine[pass_index],
            my_accept[pass_index],
            None if last else (w_own, w_other),
            3 + 2 * pass_index,
        )
        if last:
            return done[0].reshape(requests, rows, width)
        current = done[0].reshape(rows, width)
        heads = attend(done[1], None, every_cache, my_groups, lengths)
        (every_head,) = gather_heads(heads, None, 4 + 2 * pass_index)


def solution(mesh):
    return jax.shard_map(
        shards,
        mesh=mesh,
        in_specs=(
            P("req", None, None),
            P(None, "req", "blk", None),
            P(None, "blk", None),
            P("blk", None, None),
            P(None, "blk"),
            P("blk", None),
            P("req", "blk"),
            P(),
            P(),
            P(None, "req", None),
            P(),
        ),
        out_specs=P("req", None, None),
        check_vma=False,
    )
```

```python
import functools

import jax
import jax.numpy as jnp
from jax import lax
from jax.experimental import pallas as pl
from jax.experimental.pallas import tpu as pltpu
from jax.sharding import PartitionSpec as P

PASSES = 2
MESH = pl.DeviceIdType.MESH
NEG = -1e30


def layer_norm(values):
    centre = values - jnp.mean(values, -1, keepdims=True)
    spread = jnp.mean(centre * centre, -1, keepdims=True)
    return centre * lax.rsqrt(spread + 1e-05)


class Net:
    def __init__(self):
        self.blk = lax.axis_index("blk")
        self.z = self.blk // 2
        self.x = self.blk % 2
        self.right = self.ring(1) * 2 + self.x
        self.left = self.ring(-1) * 2 + self.x
        self.pair = self.z * 2 + 1 - self.x
        self.started = []

    def ring(self, offset):
        return lax.rem(self.z + 8 + offset, 8)

    def greet(self, axis="blk", others=None):
        barrier = pltpu.get_barrier_semaphore()
        others = (self.right, self.left, self.pair) if others is None else others
        for other in others:
            pl.semaphore_signal(barrier, inc=1, device_id={axis: other}, device_id_type=MESH)
        pl.semaphore_wait(barrier, len(others))

    def copy_of(self, src, dst, sems, slot, other, axis):
        return pltpu.make_async_remote_copy(
            src_ref=src,
            dst_ref=dst,
            send_sem=sems[0].at[slot],
            recv_sem=sems[1].at[slot],
            device_id={axis: other},
            device_id_type=MESH,
        )

    def send(self, src, dst, sems, slot, other, axis="blk"):
        copy = self.copy_of(src, dst, sems, slot, other, axis)
        copy.start()
        self.started.append(copy)

    def arrived(self, dst, sems, slot):
        self.copy_of(dst, dst, sems, slot, self.pair, "blk").wait_recv()

    def finish(self):
        for copy in self.started:
            copy.wait_send()


def sem_pair(count):
    return [pltpu.SemaphoreType.DMA((count,)), pltpu.SemaphoreType.DMA((count,))]


def whole(count):
    return [pl.BlockSpec(memory_space=pltpu.VMEM)] * count


RING_A, RING_B, RING_C, RING_D = 0, 4, 7, 10
RING_SLOTS = 14


def ring_begin(net, out, sems, half, high):
    piece = out.at[net.z, half : 2 * half] if high else out.at[net.z, 0:half]
    net.send(piece, piece, sems, RING_B if high else RING_A, net.right)
    net.send(piece, piece, sems, RING_D if high else RING_C, net.left)


def ring_rest(net, out, sems, half):
    def take(offset, high, slot, last, target):
        at = net.ring(offset)
        piece = out.at[at, half : 2 * half] if high else out.at[at, 0:half]
        net.arrived(piece, sems, slot)
        if not last:
            net.send(piece, piece, sems, slot + 1, target)

    for step in range(1, 5):
        take(-step, False, RING_A + step - 1, step == 4, net.right)
        take(step, True, RING_D + step - 1, step == 4, net.left)
        if step < 4:
            take(-step, True, RING_B + step - 1, step == 3, net.right)
            take(step, False, RING_C + step - 1, step == 3, net.left)


def heads_kernel(heads, out, peer, *sem_refs):
    net = Net()
    ring_sems, pair_sems = tuple(sem_refs[0:2]), tuple(sem_refs[2:4])
    half = heads.shape[1] // 2
    net.greet()
    parts = (slice(0, half), slice(half, 2 * half))
    for part, rows in enumerate(parts):
        net.send(heads.at[1 - net.x, rows], peer.at[rows], pair_sems, part, net.pair)
    for part, rows in enumerate(parts):
        net.arrived(peer.at[rows], pair_sems, part)
        out[net.z, rows] = heads[net.x, rows] + peer[rows]
        ring_begin(net, out, ring_sems, half, part == 1)
    ring_rest(net, out, ring_sems, half)
    net.finish()


def gather_heads(heads, collective_id):
    _, rows, lanes = heads.shape
    return pl.pallas_call(
        heads_kernel,
        out_shape=jax.ShapeDtypeStruct((8, rows, lanes), heads.dtype),
        in_specs=whole(1),
        out_specs=whole(1)[0],
        scratch_shapes=[pltpu.VMEM((rows, lanes), heads.dtype)] + sem_pair(RING_SLOTS) + sem_pair(2),
        compiler_params=pltpu.CompilerParams(
            collective_id=collective_id, has_side_effects=True, vmem_limit_bytes=16 << 20
        ),
        name=f"gather_heads_{collective_id}",
    )(heads)


def mlp_kernel(
    every_head, current, w_out, w_fc, w_proj, others, twins, grown, my_middle, head_rows, middle
):
    f32, bf16 = jnp.float32, jnp.bfloat16
    blk = lax.axis_index("blk")
    for z in range(8):
        head_rows[:, 128 * z : 128 * (z + 1)] = every_head[z]
    rows = current[blk % 2] if len(current.shape) == 3 else current[...]
    middle[...] = rows.astype(f32) + jnp.dot(
        head_rows[...], w_out[...], preferred_element_type=f32
    )
    share = my_middle.shape[0]
    my_middle[...] = middle[pl.ds(pl.multiple_of(blk // 2 * share, share), share), :]
    normed = layer_norm(middle[...]).astype(bf16)

    def term(enter, leave):
        raw = lax.dot_general(normed, enter, (((1,), (1,)), ((), ())), preferred_element_type=f32)
        rows = jax.nn.gelu(raw, approximate=True).astype(bf16)
        return jnp.dot(rows, leave, preferred_element_type=f32)

    total = term(w_fc[...], w_proj[...])
    total = total + term(others[0], others[1]) + term(twins[0], twins[1])
    grown[...] = total.astype(bf16)


def mlp(every_head, current, weights):
    rows, width = current.shape[-2:]
    return pl.pallas_call(
        mlp_kernel,
        out_shape=(
            jax.ShapeDtypeStruct((rows, width), jnp.bfloat16),
            jax.ShapeDtypeStruct((rows // 8, width), jnp.float32),
        ),
        in_specs=whole(2 + len(weights)),
        out_specs=tuple(whole(2)),
        scratch_shapes=[
            pltpu.VMEM((rows, 8 * every_head.shape[2]), jnp.bfloat16),
            pltpu.VMEM((rows, width), jnp.float32),
        ],
        compiler_params=pltpu.CompilerParams(vmem_limit_bytes=40 << 20),
        name="mlp",
    )(every_head, current, *weights)


def project(rows_f32, weights):
    bf16 = jnp.bfloat16
    normed = layer_norm(rows_f32).astype(bf16)
    got = jnp.dot(normed, weights, preferred_element_type=jnp.float32).astype(bf16)
    lane = lax.broadcasted_iota(jnp.int32, (1, got.shape[1]), 1)
    return (got.astype(jnp.float32) * jnp.where(lane < 128, 0.125, 1.0)).astype(bf16)


def reduce_kernel(part, middle, fresh, accept, *refs, last):
    if last:
        out, *refs = refs
    else:
        w_own, w_pair, out, qkv, stage, *refs = refs
    right_low, right_high, left_low, left_high, *sem_refs = refs
    net = Net()
    sems, gather_sems = tuple(sem_refs[0:2]), tuple(sem_refs[2:4])
    half = part.shape[1] // 2
    f32, bf16 = jnp.float32, jnp.bfloat16
    low, high = slice(0, half), slice(half, 2 * half)
    net.greet()

    def begin(buf, rows, slot, offset, target):
        net.send(part.at[net.ring(offset), rows], buf.at[0], sems, slot, target)

    def hand_on(buf, rows, slot, step, offset, target):
        piece = buf.at[step]
        net.arrived(piece, sems, slot + step)
        total = piece[...].astype(f32) + part[net.ring(offset), rows].astype(f32)
        buf[step] = total.astype(bf16)
        net.send(piece, buf.at[step + 1], sems, slot + step + 1, target)

    begin(right_low, low, RING_A, 4, net.right)
    begin(left_high, high, RING_D, -4, net.left)
    begin(right_high, high, RING_B, 3, net.right)
    begin(left_low, low, RING_C, -3, net.left)
    for step in range(3):
        hand_on(right_low, low, RING_A, step, 3 - step, net.right)
        hand_on(left_high, high, RING_D, step, step - 3, net.left)
        if step < 2:
            hand_on(right_high, high, RING_B, step, 2 - step, net.right)
            hand_on(left_low, low, RING_C, step, step - 2, net.left)

    def close(rows, from_left, from_right):
        total = part[net.z, rows].astype(f32) + from_left.astype(f32) + from_right.astype(f32)
        layer_out = (middle[rows] + total).astype(bf16)
        return jnp.where(accept[rows] == 1, fresh[rows], layer_out)

    net.arrived(left_low.at[2], sems, RING_C + 2)
    net.arrived(right_low.at[3], sems, RING_A + 3)
    result = close(low, right_low[3], left_low[2])
    if last:
        out[net.x, net.z, low] = result
        gather_begin_low(net, out, gather_sems, half)
    else:
        out[net.z, low] = result
        ring_begin(net, out, gather_sems, half, False)
    net.arrived(right_high.at[2], sems, RING_B + 2)
    net.arrived(left_high.at[3], sems, RING_D + 3)
    result = close(high, right_high[2], left_high[3])
    if last:
        out[net.x, net.z, high] = result
        gather_begin_high(net, out, gather_sems, half)
        gather_rest(net, out, gather_sems, half)
    else:
        out[net.z, high] = result
        ring_begin(net, out, gather_sems, half, True)
        ring_rest(net, out, gather_sems, half)
        swap_sems = tuple(sem_refs[4:6])
        rows_f32 = out[...].reshape(8 * 2 * half, out.shape[2]).astype(f32)
        stage[...] = project(rows_f32, w_pair[...])
        net.send(stage, qkv.at[net.x], swap_sems, 0, net.pair)
        qkv[net.x] = project(rows_f32, w_own[...])
        net.arrived(qkv.at[1 - net.x], swap_sems, 0)
    net.finish()


def reduce_blk(part, middle, fresh, accept, w_pair, collective_id):
    blocks, rows, width = part.shape
    bf16 = jnp.bfloat16
    last = w_pair is None
    block = (rows // 2, width)
    rings = [pltpu.VMEM((count,) + block, bf16) for count in (4, 3, 3, 4)]
    operands = (part, middle, fresh, accept)
    if last:
        shapes = (jax.ShapeDtypeStruct((2,) + part.shape, bf16),)
        sems = sem_pair(RING_SLOTS) + sem_pair(GATHER_SLOTS)
    else:
        operands = operands + w_pair
        columns = w_pair[0].shape[1]
        shapes = (
            jax.ShapeDtypeStruct(part.shape, bf16),
            jax.ShapeDtypeStruct((2, blocks * rows, columns), bf16),
        )
        rings = [pltpu.VMEM((blocks * rows, columns), bf16)] + rings
        sems = sem_pair(RING_SLOTS) + sem_pair(RING_SLOTS) + sem_pair(1)
    return pl.pallas_call(
        functools.partial(reduce_kernel, last=last),
        out_shape=shapes,
        in_specs=whole(len(operands)),
        out_specs=tuple(whole(len(shapes))),
        scratch_shapes=rings + sems,
        compiler_params=pltpu.CompilerParams(
            collective_id=collective_id, has_side_effects=True, vmem_limit_bytes=40 << 20
        ),
        name=f"reduce_blk_{collective_id}",
    )(*operands)


R_A, R_B, R_O, L_A, L_B, L_O, X_A, X_B = 0, 4, 8, 12, 16, 20, 24, 25
GATHER_SLOTS = 33


def gather_begin_low(net, out, sems, half):
    low = out.at[net.x, net.z, 0:half]
    net.send(low, low, sems, R_A + 0, net.right)
    net.send(low, low, sems, L_A + 0, net.left)
    net.send(low, low, sems, X_A, net.pair)


def gather_begin_high(net, out, sems, half):
    high = out.at[net.x, net.z, half : 2 * half]
    net.send(high, high, sems, R_B + 0, net.right)
    net.send(high, high, sems, L_B + 0, net.left)
    net.send(high, high, sems, X_B + 0, net.pair)


def gather_rest(net, out, sems, half):
    other = 1 - net.x
    peer_low = out.at[other, net.z, 0:half]
    net.arrived(peer_low, sems, X_A)
    net.send(peer_low, peer_low, sems, R_O + 0, net.right)
    net.send(peer_low, peer_low, sems, L_O + 0, net.left)
    for step in range(1, 5):
        before, after = net.ring(-step), net.ring(step)
        piece = out.at[net.x, before, 0:half]
        net.arrived(piece, sems, R_A + step - 1)
        if step < 4:
            net.send(piece, piece, sems, R_A + step, net.right)
        piece = out.at[net.x, after, half : 2 * half]
        net.arrived(piece, sems, L_B + step - 1)
        if step < 4:
            net.send(piece, piece, sems, L_B + step, net.left)
        net.send(piece, piece, sems, X_B + (step if step < 4 else 7), net.pair)
        piece = out.at[other, after, 0:half]
        net.arrived(piece, sems, L_O + step - 1)
        if step < 4:
            net.send(piece, piece, sems, L_O + step, net.left)
        if step < 4:
            piece = out.at[net.x, after, 0:half]
            net.arrived(piece, sems, L_A + step - 1)
            if step < 3:
                net.send(piece, piece, sems, L_A + step, net.left)
            piece = out.at[net.x, before, half : 2 * half]
            net.arrived(piece, sems, R_B + step - 1)
            if step < 3:
                net.send(piece, piece, sems, R_B + step, net.right)
            net.send(piece, piece, sems, X_B + 3 + step, net.pair)
            piece = out.at[other, before, 0:half]
            net.arrived(piece, sems, R_O + step - 1)
            if step < 3:
                net.send(piece, piece, sems, R_O + step, net.right)
    for slot, offset in ((0, 0), (1, 1), (2, 2), (3, 3), (7, 4), (4, -1), (5, -2), (6, -3)):
        net.arrived(out.at[other, net.ring(offset), half : 2 * half], sems, X_B + slot)


PIECES = (0, 2, 1, 3)


SLOTS = 128


def start_kernel(
    own, w_own, ids, table, out, w_all, fresh,
    ranks, relatives, sent, got, picked, mine, copy_sems,
    send_sems, recv_sems, send_w, recv_w, send_f, recv_f, send_g, recv_g, *, vocab_dev, columns,
):
    net = Net()
    f32, bf16 = jnp.float32, jnp.bfloat16
    me = lax.axis_index("req")
    y, x, core = me // 4, (me // 2) % 2, me % 2

    def device(step, other_x, other_core=False):
        return (
            lax.rem(y + 4 + step, 4) * 4
            + (1 - x if other_x else x) * 2
            + (1 - core if other_core else core)
        )

    up, down, side, twin = device(1, 0), device(-1, 0), device(0, 1), device(0, 0, True)
    barrier = pltpu.get_barrier_semaphore()
    for step in range(1, 16):
        other = lax.rem(me + step, 16)
        pl.semaphore_signal(barrier, inc=1, device_id={"req": other}, device_id_type=MESH)
    for step in range(1, 16):
        other = lax.rem(net.blk + step, 16)
        pl.semaphore_signal(barrier, inc=1, device_id={"blk": other}, device_id_type=MESH)
    pl.semaphore_wait(barrier, 30)
    w_sems, f_sems, g_sems = (send_w, recv_w), (send_f, recv_f), (send_g, recv_g)
    started = []

    def copy_of(src, dst, slot, other):
        return pltpu.make_async_remote_copy(
            src_ref=src,
            dst_ref=dst,
            send_sem=send_sems.at[slot],
            recv_sem=recv_sems.at[slot],
            device_id={"req": other},
            device_id_type=MESH,
        )

    def send(src, dst, slot, other):
        copy = copy_of(src, dst, slot, other)
        copy.start()
        started.append(copy)

    def arrived(dst, slot):
        copy_of(dst, dst, slot, twin).wait_recv()

    U0, D0, SIDE, U1, D1, UF0, UF1, DF0, DF1, TWIN = 0, 4, 8, 12, 16, 20, 22, 24, 26, 28
    places = {(0, 0): 0, (0, 1): 1, (-1, 0): 2, (1, 0): 3, (-1, 1): 4, (1, 1): 5, (2, 0): 6, (2, 1): 7}

    def share(step, other_x, g):
        piece = out.at[g, device(step, other_x)]
        send(piece, piece, TWIN + 4 * places[(step, other_x)] + g, twin)

    for g in PIECES:
        dst = out.at[g, me]
        send(own.at[g], dst, U0 + g, up)
        send(own.at[g], dst, D0 + g, down)
        send(own.at[g], dst, SIDE + g, side)
    RO, LO, RQ, LQ, PX = 0, 4, 7, 10, 14
    w_mine, w_peer = w_all.at[net.z, net.x], w_all.at[net.z, 1 - net.x]
    net.send(w_own, w_mine, w_sems, PX, net.pair)
    net.send(w_own, w_mine, w_sems, RO, net.right)
    net.send(w_own, w_mine, w_sems, LO, net.left)
    keeps = [
        pltpu.make_async_copy(own, out.at[:, me], copy_sems.at[0]),
        pltpu.make_async_copy(w_own, w_mine, copy_sems.at[1]),
    ]
    for keep in keeps:
        keep.start()

    def w_peer_begin():
        net.arrived(w_peer, w_sems, PX)
        net.send(w_peer, w_peer, w_sems, RQ, net.right)
        net.send(w_peer, w_peer, w_sems, LQ, net.left)

    def w_step(step, parity, slot_r, slot_l, last_r, last_l):
        if step < last_r:
            piece = w_all.at[net.ring(-1 - step), parity]
            net.arrived(piece, w_sems, slot_r + step)
            if step < last_r - 1:
                net.send(piece, piece, w_sems, slot_r + step + 1, net.right)
        if step < last_l:
            piece = w_all.at[net.ring(1 + step), parity]
            net.arrived(piece, w_sems, slot_l + step)
            if step < last_l - 1:
                net.send(piece, piece, w_sems, slot_l + step + 1, net.left)

    def w_mine_step(step):
        w_step(step, net.x, RO, LO, 4, 3)

    def w_peer_step(step):
        w_step(step, 1 - net.x, RQ, LQ, 3, 4)

    count = ids.shape[1]

    def within(values, owner):
        offset = values - owner * vocab_dev
        return (offset >= 0) & (offset < vocab_dev), offset

    inside, offset = within(ids[...], me)
    owners = lax.broadcasted_iota(jnp.int32, (16, 1), 0)
    theirs, _ = within(ids[pl.ds(me, 1), :], owners)
    both = jnp.concatenate([jnp.where(inside, 1.0, 0.0), jnp.where(theirs, 1.0, 0.0)], 0)
    earlier = lax.broadcasted_iota(jnp.int32, (count, count), 0) < lax.broadcasted_iota(
        jnp.int32, (count, count), 1
    )
    rank = jnp.dot(
        both.astype(bf16), jnp.where(earlier, 1.0, 0.0).astype(bf16), preferred_element_type=f32
    )
    ranks[...] = jnp.where(inside, rank[0:16], -1.0)
    relatives[...] = offset.astype(f32)
    slot_of = jnp.where(theirs, rank[16:32] + owners.astype(f32) * SLOTS, 0.0)
    place_row = jnp.sum(slot_of, 0, keepdims=True)

    def pick(chunk):
        slots = lax.broadcasted_iota(jnp.int32, (SLOTS, 1), 0).astype(f32)
        wanted = []
        for step in range(4 * chunk, 4 * chunk + 4):
            other = pl.ds(lax.rem(me + step, 16), 1)
            chosen = ranks[other, :] == slots
            wanted.append(jnp.sum(jnp.where(chosen, relatives[other, :], 0.0), 1, keepdims=True))
        wanted = jnp.concatenate(wanted, 0).astype(jnp.int32)
        row = lax.broadcasted_iota(jnp.int32, (1, table.shape[1]), 1)
        one_hot = jnp.where(wanted == row, 1.0, 0.0).astype(bf16)
        rows = lax.dot_general(
            one_hot, table[...], (((1,), (1,)), ((), ())), preferred_element_type=f32
        ).astype(bf16)
        for index, step in enumerate(range(4 * chunk, 4 * chunk + 4)):
            block = rows[SLOTS * index : SLOTS * (index + 1)]
            if step == 0:
                got[me] = block
            else:
                other = lax.rem(me + step, 16)
                sent[step] = block
                net.send(sent.at[step], got.at[me], f_sems, step - 1, other, "req")

    def spread():
        for step in range(1, 16):
            net.arrived(got.at[lax.rem(me + 16 - step, 16)], f_sems, step - 1)
        place = jnp.transpose(jnp.broadcast_to(place_row, (8, count)))[:, 0:1].astype(jnp.int32)
        slot = lax.broadcasted_iota(jnp.int32, (1, 16 * SLOTS), 1)
        one_hot = jnp.where(place == slot, 1.0, 0.0).astype(bf16)
        rows = jnp.dot(
            one_hot, got[...].reshape(16 * SLOTS, got.shape[2]), preferred_element_type=f32
        )
        picked[...] = rows.astype(bf16).reshape(picked.shape)
        mine[net.blk] = picked[net.blk]
        for step in range(1, 16):
            other = lax.rem(net.blk + step, 16)
            net.send(picked.at[other], mine.at[net.blk], g_sems, step - 1, other)

    def join():
        for step in range(1, 16):
            net.arrived(mine.at[lax.rem(net.blk + 16 - step, 16)], g_sems, step - 1)
        fresh[...] = jnp.concatenate([mine[index, :, 0:columns] for index in range(16)], 1)

    pick(0)
    w_order = iter(
        [w_peer_begin, lambda: w_mine_step(0), lambda: w_peer_step(0), lambda: w_mine_step(1),
         lambda: w_peer_step(1), lambda: w_mine_step(2), lambda: w_peer_step(2)]
    )
    for g in PIECES:
        send(own.at[g], out.at[g, me], TWIN + g, twin)

    def from_below(g, other_x, base, forward):
        piece = out.at[g, device(-1, other_x)]
        arrived(piece, base + g)
        if g < 2:
            send(piece, piece, forward + g, up)
        share(-1, other_x, g)

    def from_above(g, other_x, base, forward):
        piece = out.at[g, device(1, other_x)]
        arrived(piece, base + g)
        if g >= 2:
            send(piece, piece, forward + g - 2, down)
        share(1, other_x, g)

    def from_far(g, other_x):
        piece = out.at[g, device(2, other_x)]
        if g < 2:
            arrived(piece, (UF1 if other_x else UF0) + g)
        else:
            arrived(piece, (DF1 if other_x else DF0) + g - 2)
        share(2, other_x, g)

    for g in PIECES:
        piece = out.at[g, side]
        arrived(piece, SIDE + g)
        send(piece, piece, U1 + g, up)
        send(piece, piece, D1 + g, down)
        share(0, 1, g)
        from_below(g, 0, U0, UF0)
        from_above(g, 0, D0, DF0)
        next(w_order)()
        if g == PIECES[-1]:
            spread()
        else:
            pick(PIECES.index(g) + 1)
    for g in PIECES:
        from_far(g, 0)
        from_below(g, 1, U1, UF1)
        from_above(g, 1, D1, DF1)
        next(w_order, lambda: None)()
    for g in PIECES:
        from_far(g, 1)
    for (step, other_x), place in places.items():
        for g in PIECES:
            arrived(out.at[g, device(step, other_x, True)], TWIN + 4 * place + g)
    w_mine_step(3)
    w_peer_step(3)
    join()
    for keep in keeps:
        keep.wait()
    for copy in started:
        copy.wait_send()
    net.finish()


def start_gathers(own, w_own, ids, table, vocab_dev, columns, collective_id):
    groups = own.shape[0]
    count = ids.shape[1]
    bf16 = jnp.bfloat16
    anywhere = pl.BlockSpec(memory_space=pl.ANY)
    blocks = pltpu.VMEM((16, SLOTS, 128), bf16)
    rows = pltpu.VMEM((16, count // 16, 128), bf16)
    return pl.pallas_call(
        functools.partial(start_kernel, vocab_dev=vocab_dev, columns=columns),
        out_shape=(
            jax.ShapeDtypeStruct((groups, 16) + own.shape[1:], own.dtype),
            jax.ShapeDtypeStruct((8, 2) + w_own.shape, w_own.dtype),
            jax.ShapeDtypeStruct((count // 16, 16 * columns), bf16),
        ),
        in_specs=[anywhere, anywhere] + whole(2),
        out_specs=(anywhere, anywhere, whole(1)[0]),
        scratch_shapes=[
            pltpu.VMEM((16, count), jnp.float32),
            pltpu.VMEM((16, count), jnp.float32),
            blocks,
            blocks,
            rows,
            rows,
            pltpu.SemaphoreType.DMA((2,)),
        ]
        + sem_pair(60)
        + sem_pair(15)
        + sem_pair(15)
        + sem_pair(15),
        compiler_params=pltpu.CompilerParams(
            collective_id=collective_id, has_side_effects=True, vmem_limit_bytes=56 << 20
        ),
        name="start_gathers",
    )(own, w_own, ids, table)


def asked_rows(new_ids):
    by_device = new_ids.reshape(new_ids.shape[0], 16, 2, 8, -1)
    return jnp.transpose(by_device, (1, 3, 2, 0, 4)).reshape(16, -1)


def settle_fresh(quick, ids, embed_table, req_index):
    vocab_dev = embed_table.shape[0]
    owner = ids // vocab_dev
    owners = jnp.arange(16)[:, None]
    asked = jnp.sum((owner[:, None, :] == owners[None]).astype(jnp.int32), -1)
    crowded = jnp.max(asked) > SLOTS

    def dense():
        relative = (ids - req_index * vocab_dev).reshape(-1)
        here = (relative >= 0) & (relative < vocab_dev)
        looked = jnp.take(embed_table, jnp.clip(relative, 0, vocab_dev - 1), axis=0)
        looked = jnp.where(here[:, None], looked, jnp.zeros((), jnp.bfloat16))
        summed = lax.psum_scatter(looked, "req", scatter_dimension=0, tiled=True)
        summed = summed.reshape(16, -1, summed.shape[1])
        mine = lax.all_to_all(summed, "blk", split_axis=0, concat_axis=0, tiled=True)
        return jnp.transpose(mine, (1, 0, 2)).reshape(quick.shape)

    return lax.cond(crowded, dense, lambda: quick)


def attend_kernel(groups, lengths, rows_or_qkv, *refs, span, first):
    if first:
        weights, cache, out = refs
        qkv = project(rows_or_qkv[0].astype(jnp.float32), weights[...])
    else:
        cache, out = refs
        qkv = rows_or_qkv[0]
    length = lengths[pl.program_id(0)]
    q, own_block = qkv[:, 0:128], qkv[:, 128:256]
    f32 = jnp.float32

    def scores_of(keys):
        return lax.dot_general(q, keys, (((1,), (1,)), ((), ())), preferred_element_type=f32)

    def weigh(weights, values):
        return jnp.dot(weights.astype(jnp.bfloat16), values, preferred_element_type=f32)

    scores = scores_of(own_block)
    top = jnp.max(scores, -1, keepdims=True)
    weights = jnp.exp(scores - top)
    total = jnp.sum(weights, -1, keepdims=True)
    mixed = weigh(weights, own_block)

    def visit(index, carried):
        top, total, mixed = carried
        start = pl.multiple_of(index * span, span)
        block = cache[0, pl.ds(start, span), :]
        position = start + lax.broadcasted_iota(jnp.int32, (1, span), 1)
        bias = jnp.where(position < length, 0.0, NEG).astype(f32)
        scores = scores_of(block) + bias
        raised = jnp.maximum(top, jnp.max(scores, -1, keepdims=True))
        shrink = jnp.exp(top - raised)
        weights = jnp.exp(scores - raised)
        total = total * shrink + jnp.sum(weights, -1, keepdims=True)
        return raised, total, mixed * shrink + weigh(weights, block)

    blocks = (length + span - 1) // span
    top, total, mixed = lax.fori_loop(0, blocks, visit, (top, total, mixed))
    head = mixed / total
    parity = lax.axis_index("blk") % 2
    lane = lax.broadcasted_iota(jnp.int32, (1, 128), 1)
    moved = jnp.where(parity == 0, pltpu.roll(head, 64, 1), head)
    out[0] = jnp.where(lane // 64 == parity, moved, 0.0).astype(out.dtype)


def attend(rows_or_qkv, weights, cache, groups, lengths):
    requests, rows, width = rows_or_qkv.shape
    size = cache.shape[1]
    first = weights is not None
    in_specs = [pl.BlockSpec((1, rows, width), lambda r, g, n: (r, 0, 0))]
    operands = (rows_or_qkv,)
    if first:
        in_specs.append(pl.BlockSpec(weights.shape, lambda r, g, n: (0, 0)))
        operands = operands + (weights,)
    in_specs.append(pl.BlockSpec((1, size, 128), lambda r, g, n: (g[r], 0, 0)))
    return pl.pallas_call(
        functools.partial(attend_kernel, span=1024, first=first),
        out_shape=jax.ShapeDtypeStruct((requests, rows, 128), jnp.bfloat16),
        grid_spec=pltpu.PrefetchScalarGridSpec(
            num_scalar_prefetch=2,
            grid=(requests,),
            in_specs=in_specs,
            out_specs=pl.BlockSpec((1, rows, 128), lambda r, g, n: (r, 0, 0)),
        ),
        compiler_params=pltpu.CompilerParams(vmem_limit_bytes=58 << 20),
        name="attend",
    )(groups, lengths, *operands, cache)


def shards(
    tokens, cache_kv, w_qkv, w_out, w_fc, w_proj, embed_table, group_ids, cache_len, accept, new_ids
):
    req_index = lax.axis_index("req")
    blk_index = lax.axis_index("blk")
    z, x, core = blk_index // 2, blk_index % 2, req_index % 2
    requests, rows, width = tokens.shape
    kv_width = cache_kv.shape[3]
    head_dim = kv_width // 2
    share = rows // 8
    my_groups = lax.dynamic_slice_in_dim(group_ids, req_index * requests, requests)
    lengths = jnp.take(cache_len, my_groups)
    w_qkv = w_qkv[:, 0, :]
    w_own = jnp.concatenate(
        [w_qkv[:, :head_dim], jnp.zeros_like(w_qkv[:, :head_dim]), w_qkv[:, head_dim:]], 1
    )
    w_fc = jnp.transpose(w_fc)
    ids = asked_rows(new_ids)
    vocab_dev, columns = embed_table.shape
    table = jnp.pad(jnp.transpose(embed_table), ((0, 128 - columns), (0, -vocab_dev % 128)))
    every_cache, w_out_all, fresh = start_gathers(
        cache_kv[:, :, 0, :], w_out[0], ids, table, vocab_dev, columns, 1
    )
    every_cache = every_cache.reshape(cache_kv.shape[0], -1, kv_width)
    w_out_all = w_out_all.reshape(16 * head_dim, width)
    pairs = [(index, index ^ 1) for index in range(16)]
    hidden = w_fc.shape[0] // 2
    halves = jnp.stack(
        [lax.dynamic_slice_in_dim(weights, core * hidden, hidden, 0) for weights in (w_fc, w_proj)]
    )
    halves, w_sent, fresh = lax.optimization_barrier((halves, w_own, fresh))
    others = lax.ppermute(halves, "blk", pairs)
    w_other = lax.ppermute(w_sent, "blk", pairs)

    my_accept = lax.dynamic_index_in_dim(accept, x, 1, keepdims=False)
    my_accept = lax.dynamic_slice_in_dim(my_accept, z * share, share, 1)[..., None]

    heads = attend(tokens, w_own, every_cache, my_groups, lengths)
    heads, others = lax.optimization_barrier((heads, others))
    twins = lax.ppermute(others, "req", pairs)
    weights = (w_out_all, w_fc, w_proj, others, twins)
    every_head = gather_heads(heads, 2)
    fresh = settle_fresh(fresh, ids, embed_table, req_index).reshape(PASSES, share, width)
    current = tokens
    for pass_index in range(PASSES):
        last = pass_index == PASSES - 1
        grown, my_middle = mlp(every_head, current, weights)
        done = reduce_blk(
            grown.reshape(8, share, width),
            my_middle,
            fresh[pass_index],
            my_accept[pass_index],
            None if last else (w_own, w_other),
            3 + 2 * pass_index,
        )
        if last:
            return done[0].reshape(requests, rows, width)
        current = done[0].reshape(rows, width)
        heads = attend(done[1], None, every_cache, my_groups, lengths)
        every_head = gather_heads(heads, 4 + 2 * pass_index)


def solution(mesh):
    return jax.shard_map(
        shards,
        mesh=mesh,
        in_specs=(
            P("req", None, None),
            P(None, "req", "blk", None),
            P(None, "blk", None),
            P("blk", None, None),
            P(None, "blk"),
            P("blk", None),
            P("req", "blk"),
            P(),
            P(),
            P(None, "req", None),
            P(),
        ),
        out_specs=P("req", None, None),
        check_vma=False,
    )
```

```python
import functools

import jax
import jax.numpy as jnp
from jax import lax
from jax.experimental import pallas as pl
from jax.experimental.pallas import tpu as pltpu
from jax.sharding import PartitionSpec as P

PASSES = 2
MESH = pl.DeviceIdType.MESH
NEG = -1e30


def layer_norm(values):
    centre = values - jnp.mean(values, -1, keepdims=True)
    spread = jnp.mean(centre * centre, -1, keepdims=True)
    return centre * lax.rsqrt(spread + 1e-05)


class Net:
    def __init__(self):
        self.blk = lax.axis_index("blk")
        self.z = self.blk // 2
        self.x = self.blk % 2
        self.right = self.ring(1) * 2 + self.x
        self.left = self.ring(-1) * 2 + self.x
        self.pair = self.z * 2 + 1 - self.x
        self.started = []

    def ring(self, offset):
        return lax.rem(self.z + 8 + offset, 8)

    def greet(self, axis="blk", others=None):
        barrier = pltpu.get_barrier_semaphore()
        others = (self.right, self.left, self.pair) if others is None else others
        for other in others:
            pl.semaphore_signal(barrier, inc=1, device_id={axis: other}, device_id_type=MESH)
        pl.semaphore_wait(barrier, len(others))

    def copy_of(self, src, dst, sems, slot, other, axis):
        return pltpu.make_async_remote_copy(
            src_ref=src,
            dst_ref=dst,
            send_sem=sems[0].at[slot],
            recv_sem=sems[1].at[slot],
            device_id={axis: other},
            device_id_type=MESH,
        )

    def send(self, src, dst, sems, slot, other, axis="blk"):
        copy = self.copy_of(src, dst, sems, slot, other, axis)
        copy.start()
        self.started.append(copy)

    def arrived(self, dst, sems, slot):
        self.copy_of(dst, dst, sems, slot, self.pair, "blk").wait_recv()

    def finish(self):
        for copy in self.started:
            copy.wait_send()


def busy(us):
    return pl.CostEstimate(flops=us * 400_000_000, bytes_accessed=us * 3_000_000, transcendentals=0)


def sem_pair(count):
    return [pltpu.SemaphoreType.DMA((count,)), pltpu.SemaphoreType.DMA((count,))]


def whole(count):
    return [pl.BlockSpec(memory_space=pltpu.VMEM)] * count


RING_A, RING_B, RING_C, RING_D = 0, 4, 7, 10
RING_SLOTS = 14


def ring_begin(net, out, sems, half, high):
    piece = out.at[net.z, half : 2 * half] if high else out.at[net.z, 0:half]
    net.send(piece, piece, sems, RING_B if high else RING_A, net.right)
    net.send(piece, piece, sems, RING_D if high else RING_C, net.left)


def ring_rest(net, out, sems, half):
    def take(offset, high, slot, last, target):
        at = net.ring(offset)
        piece = out.at[at, half : 2 * half] if high else out.at[at, 0:half]
        net.arrived(piece, sems, slot)
        if not last:
            net.send(piece, piece, sems, slot + 1, target)

    for step in range(1, 5):
        take(-step, False, RING_A + step - 1, step == 4, net.right)
        take(step, True, RING_D + step - 1, step == 4, net.left)
        if step < 4:
            take(-step, True, RING_B + step - 1, step == 3, net.right)
            take(step, False, RING_C + step - 1, step == 3, net.left)


def heads_kernel(heads, out, peer, *sem_refs):
    net = Net()
    ring_sems, pair_sems = tuple(sem_refs[0:2]), tuple(sem_refs[2:4])
    half = heads.shape[1] // 2
    net.greet()
    parts = (slice(0, half), slice(half, 2 * half))
    for part, rows in enumerate(parts):
        net.send(heads.at[1 - net.x, rows], peer.at[rows], pair_sems, part, net.pair)
    for part, rows in enumerate(parts):
        net.arrived(peer.at[rows], pair_sems, part)
        out[net.z, rows] = heads[net.x, rows] + peer[rows]
        ring_begin(net, out, ring_sems, half, part == 1)
    ring_rest(net, out, ring_sems, half)
    net.finish()


def gather_heads(heads, collective_id):
    _, rows, lanes = heads.shape
    return pl.pallas_call(
        heads_kernel,
        out_shape=jax.ShapeDtypeStruct((8, rows, lanes), heads.dtype),
        in_specs=whole(1),
        out_specs=whole(1)[0],
        scratch_shapes=[pltpu.VMEM((rows, lanes), heads.dtype)] + sem_pair(RING_SLOTS) + sem_pair(2),
        compiler_params=pltpu.CompilerParams(
            collective_id=collective_id, has_side_effects=True, vmem_limit_bytes=16 << 20
        ),
        cost_estimate=busy(15),
        name="gather_heads",
    )(heads)


def mlp_kernel(
    every_head, current, w_out, w_fc, w_proj, others, twins, grown, my_middle, head_rows, middle
):
    f32, bf16 = jnp.float32, jnp.bfloat16
    blk = lax.axis_index("blk")
    for z in range(8):
        head_rows[:, 128 * z : 128 * (z + 1)] = every_head[z]
    rows = current[blk % 2] if len(current.shape) == 3 else current[...]
    middle[...] = rows.astype(f32) + jnp.dot(
        head_rows[...], w_out[...], preferred_element_type=f32
    )
    share = my_middle.shape[0]
    my_middle[...] = middle[pl.ds(pl.multiple_of(blk // 2 * share, share), share), :]
    normed = layer_norm(middle[...]).astype(bf16)

    def term(enter, leave):
        raw = lax.dot_general(normed, enter, (((1,), (1,)), ((), ())), preferred_element_type=f32)
        rows = jax.nn.gelu(raw, approximate=True).astype(bf16)
        return jnp.dot(rows, leave, preferred_element_type=f32)

    total = term(w_fc[...], w_proj[...])
    total = total + term(others[0], others[1]) + term(twins[0], twins[1])
    grown[...] = total.astype(bf16)


def mlp(every_head, current, weights):
    rows, width = current.shape[-2:]
    return pl.pallas_call(
        mlp_kernel,
        out_shape=(
            jax.ShapeDtypeStruct((rows, width), jnp.bfloat16),
            jax.ShapeDtypeStruct((rows // 8, width), jnp.float32),
        ),
        in_specs=whole(2 + len(weights)),
        out_specs=tuple(whole(2)),
        scratch_shapes=[
            pltpu.VMEM((rows, 8 * every_head.shape[2]), jnp.bfloat16),
            pltpu.VMEM((rows, width), jnp.float32),
        ],
        compiler_params=pltpu.CompilerParams(vmem_limit_bytes=28 << 20),
        cost_estimate=busy(6),
        name="mlp",
    )(every_head, current, *weights)


def project(rows_f32, weights):
    f32, bf16 = jnp.float32, jnp.bfloat16
    normed = layer_norm(rows_f32).astype(bf16)
    got = lax.dot_general(normed, weights, (((1,), (1,)), ((), ())), preferred_element_type=f32)
    got = jnp.concatenate([got, jnp.zeros((got.shape[0], 64), f32)], 1)
    lane = lax.broadcasted_iota(jnp.int32, (1, 128), 1)
    queries = jnp.where(lane < 64, got[:, 0:128].astype(bf16).astype(f32) * 0.125, 0.0)
    return jnp.concatenate([queries, pltpu.roll(got, 192, 1)[:, 0:128]], 1).astype(bf16)


def reduce_kernel(part, middle, fresh, accept, *refs, last):
    if last:
        out, *refs = refs
    else:
        w_own, w_pair, out, qkv, stage, *refs = refs
    right_low, right_high, left_low, left_high, *sem_refs = refs
    net = Net()
    sems, gather_sems = tuple(sem_refs[0:2]), tuple(sem_refs[2:4])
    half = part.shape[1] // 2
    f32, bf16 = jnp.float32, jnp.bfloat16
    low, high = slice(0, half), slice(half, 2 * half)
    net.greet()

    def begin(buf, rows, slot, offset, target):
        net.send(part.at[net.ring(offset), rows], buf.at[0], sems, slot, target)

    def hand_on(buf, rows, slot, step, offset, target):
        piece = buf.at[step]
        net.arrived(piece, sems, slot + step)
        total = piece[...].astype(f32) + part[net.ring(offset), rows].astype(f32)
        buf[step] = total.astype(bf16)
        net.send(piece, buf.at[step + 1], sems, slot + step + 1, target)

    begin(right_low, low, RING_A, 4, net.right)
    begin(left_high, high, RING_D, -4, net.left)
    begin(right_high, high, RING_B, 3, net.right)
    begin(left_low, low, RING_C, -3, net.left)
    for step in range(3):
        hand_on(right_low, low, RING_A, step, 3 - step, net.right)
        hand_on(left_high, high, RING_D, step, step - 3, net.left)
        if step < 2:
            hand_on(right_high, high, RING_B, step, 2 - step, net.right)
            hand_on(left_low, low, RING_C, step, step - 2, net.left)

    def close(rows, from_left, from_right):
        total = part[net.z, rows].astype(f32) + from_left.astype(f32) + from_right.astype(f32)
        layer_out = (middle[rows] + total).astype(bf16)
        return jnp.where(accept[rows] == 1, fresh[rows], layer_out)

    net.arrived(left_low.at[2], sems, RING_C + 2)
    net.arrived(right_low.at[3], sems, RING_A + 3)
    result = close(low, right_low[3], left_low[2])
    if last:
        out[net.x, net.z, low] = result
        gather_begin_low(net, out, gather_sems, half)
    else:
        out[net.z, low] = result
        ring_begin(net, out, gather_sems, half, False)
    net.arrived(right_high.at[2], sems, RING_B + 2)
    net.arrived(left_high.at[3], sems, RING_D + 3)
    result = close(high, right_high[2], left_high[3])
    if last:
        out[net.x, net.z, high] = result
        gather_begin_high(net, out, gather_sems, half)
        gather_rest(net, out, gather_sems, half)
    else:
        out[net.z, high] = result
        ring_begin(net, out, gather_sems, half, True)
        ring_rest(net, out, gather_sems, half)
        swap_sems = tuple(sem_refs[4:6])
        rows_f32 = out[...].reshape(8 * 2 * half, out.shape[2]).astype(f32)
        stage[...] = project(rows_f32, w_pair[...])
        net.send(stage, qkv.at[net.x], swap_sems, 0, net.pair)
        qkv[net.x] = project(rows_f32, w_own[...])
        net.arrived(qkv.at[1 - net.x], swap_sems, 0)
    net.finish()


def reduce_blk(part, middle, fresh, accept, w_pair, collective_id):
    blocks, rows, width = part.shape
    bf16 = jnp.bfloat16
    last = w_pair is None
    block = (rows // 2, width)
    rings = [pltpu.VMEM((count,) + block, bf16) for count in (4, 3, 3, 4)]
    operands = (part, middle, fresh, accept)
    if last:
        shapes = (jax.ShapeDtypeStruct((2,) + part.shape, bf16),)
        sems = sem_pair(RING_SLOTS) + sem_pair(GATHER_SLOTS)
    else:
        operands = operands + w_pair
        columns = 256
        shapes = (
            jax.ShapeDtypeStruct(part.shape, bf16),
            jax.ShapeDtypeStruct((2, blocks * rows, columns), bf16),
        )
        rings = [pltpu.VMEM((blocks * rows, columns), bf16)] + rings
        sems = sem_pair(RING_SLOTS) + sem_pair(RING_SLOTS) + sem_pair(1)
    return pl.pallas_call(
        functools.partial(reduce_kernel, last=last),
        out_shape=shapes,
        in_specs=whole(len(operands)),
        out_specs=tuple(whole(len(shapes))),
        scratch_shapes=rings + sems,
        compiler_params=pltpu.CompilerParams(
            collective_id=collective_id, has_side_effects=True, vmem_limit_bytes=24 << 20
        ),
        cost_estimate=busy(30),
        name=f"reduce_blk_{collective_id}",
    )(*operands)


R_A, R_B, R_O, L_A, L_B, L_O, X_A, X_B = 0, 4, 8, 12, 16, 20, 24, 25
GATHER_SLOTS = 33


def gather_begin_low(net, out, sems, half):
    low = out.at[net.x, net.z, 0:half]
    net.send(low, low, sems, R_A + 0, net.right)
    net.send(low, low, sems, L_A + 0, net.left)
    net.send(low, low, sems, X_A, net.pair)


def gather_begin_high(net, out, sems, half):
    high = out.at[net.x, net.z, half : 2 * half]
    net.send(high, high, sems, R_B + 0, net.right)
    net.send(high, high, sems, L_B + 0, net.left)
    net.send(high, high, sems, X_B + 0, net.pair)


def gather_rest(net, out, sems, half):
    other = 1 - net.x
    peer_low = out.at[other, net.z, 0:half]
    net.arrived(peer_low, sems, X_A)
    net.send(peer_low, peer_low, sems, R_O + 0, net.right)
    net.send(peer_low, peer_low, sems, L_O + 0, net.left)
    for step in range(1, 5):
        before, after = net.ring(-step), net.ring(step)
        piece = out.at[net.x, before, 0:half]
        net.arrived(piece, sems, R_A + step - 1)
        if step < 4:
            net.send(piece, piece, sems, R_A + step, net.right)
        piece = out.at[net.x, after, half : 2 * half]
        net.arrived(piece, sems, L_B + step - 1)
        if step < 4:
            net.send(piece, piece, sems, L_B + step, net.left)
        net.send(piece, piece, sems, X_B + (step if step < 4 else 7), net.pair)
        piece = out.at[other, after, 0:half]
        net.arrived(piece, sems, L_O + step - 1)
        if step < 4:
            net.send(piece, piece, sems, L_O + step, net.left)
        if step < 4:
            piece = out.at[net.x, after, 0:half]
            net.arrived(piece, sems, L_A + step - 1)
            if step < 3:
                net.send(piece, piece, sems, L_A + step, net.left)
            piece = out.at[net.x, before, half : 2 * half]
            net.arrived(piece, sems, R_B + step - 1)
            if step < 3:
                net.send(piece, piece, sems, R_B + step, net.right)
            net.send(piece, piece, sems, X_B + 3 + step, net.pair)
            piece = out.at[other, before, 0:half]
            net.arrived(piece, sems, R_O + step - 1)
            if step < 3:
                net.send(piece, piece, sems, R_O + step, net.right)
    for slot, offset in ((0, 0), (1, 1), (2, 2), (3, 3), (7, 4), (4, -1), (5, -2), (6, -3)):
        net.arrived(out.at[other, net.ring(offset), half : 2 * half], sems, X_B + slot)


PIECES = (0, 2, 1, 3)


SLOTS = 128


def start_kernel(
    own, w_own, ids, raw_table, tokens, w_qkv, out, w_all, fresh, rows_out, qkv,
    table, ranks, relatives, sent, got, picked, mine, copy_sems,
    send_sems, recv_sems, send_w, recv_w, send_f, recv_f, send_g, recv_g,
):
    net = Net()
    f32, bf16 = jnp.float32, jnp.bfloat16
    me = lax.axis_index("req")
    y, x, core = me // 4, (me // 2) % 2, me % 2

    def device(step, other_x, other_core=False):
        return (
            lax.rem(y + 4 + step, 4) * 4
            + (1 - x if other_x else x) * 2
            + (1 - core if other_core else core)
        )

    up, down, side, twin = device(1, 0), device(-1, 0), device(0, 1), device(0, 0, True)
    barrier = pltpu.get_barrier_semaphore()
    for step in range(1, 16):
        other = lax.rem(me + step, 16)
        pl.semaphore_signal(barrier, inc=1, device_id={"req": other}, device_id_type=MESH)
    for step in range(1, 16):
        other = lax.rem(net.blk + step, 16)
        pl.semaphore_signal(barrier, inc=1, device_id={"blk": other}, device_id_type=MESH)
    pl.semaphore_wait(barrier, 30)
    w_sems, f_sems, g_sems = (send_w, recv_w), (send_f, recv_f), (send_g, recv_g)
    columns, vocab_dev = raw_table.shape
    started = []

    def copy_of(src, dst, slot, other):
        return pltpu.make_async_remote_copy(
            src_ref=src,
            dst_ref=dst,
            send_sem=send_sems.at[slot],
            recv_sem=recv_sems.at[slot],
            device_id={"req": other},
            device_id_type=MESH,
        )

    def send(src, dst, slot, other):
        copy = copy_of(src, dst, slot, other)
        copy.start()
        started.append(copy)

    def arrived(dst, slot):
        copy_of(dst, dst, slot, twin).wait_recv()

    U0, D0, SIDE, U1, D1, UF0, UF1, DF0, DF1, TWIN = 0, 4, 8, 12, 16, 20, 22, 24, 26, 28
    places = {(0, 0): 0, (0, 1): 1, (-1, 0): 2, (1, 0): 3, (-1, 1): 4, (1, 1): 5, (2, 0): 6, (2, 1): 7}

    def share(step, other_x, g):
        piece = out.at[g, device(step, other_x)]
        send(piece, piece, TWIN + 4 * places[(step, other_x)] + g, twin)

    for g in PIECES:
        dst = out.at[g, me]
        send(own.at[g], dst, U0 + g, up)
        send(own.at[g], dst, D0 + g, down)
        send(own.at[g], dst, SIDE + g, side)
    RO, LO, RQ, LQ, PX, TW = 0, 4, 7, 10, 14, 15

    def w_piece(offset, parity, half):
        return w_all.at[net.ring(offset), parity, half]

    def w_twin(offset, parity, slot):
        piece = w_piece(offset, parity, core)
        net.send(piece, piece, w_sems, TW + slot, twin, "req")

    w_half, w_mine = w_own.at[core], w_piece(0, net.x, core)
    net.send(w_half, w_mine, w_sems, PX, net.pair)
    net.send(w_half, w_mine, w_sems, RO, net.right)
    net.send(w_half, w_mine, w_sems, LO, net.left)
    net.send(w_half, w_mine, w_sems, TW, twin, "req")
    keeps = [
        pltpu.make_async_copy(own, out.at[:, me], copy_sems.at[0]),
        pltpu.make_async_copy(w_half, w_mine, copy_sems.at[1]),
    ]
    for keep in keeps:
        keep.start()

    def w_begin():
        piece = w_piece(0, 1 - net.x, core)
        net.arrived(piece, w_sems, PX)
        net.send(piece, piece, w_sems, RQ, net.right)
        net.send(piece, piece, w_sems, LQ, net.left)
        w_twin(0, 1 - net.x, 8)

    def w_step(step):
        for parity, slot_r, slot_l, last_r, last_l, twin_slot in (
            (net.x, RO, LO, 4, 3, 0), (1 - net.x, RQ, LQ, 3, 4, 8)
        ):
            if step < last_r:
                piece = w_piece(-1 - step, parity, core)
                net.arrived(piece, w_sems, slot_r + step)
                if step < last_r - 1:
                    net.send(piece, piece, w_sems, slot_r + step + 1, net.right)
                w_twin(-1 - step, parity, twin_slot + (7 - step))
            if step < last_l:
                piece = w_piece(1 + step, parity, core)
                net.arrived(piece, w_sems, slot_l + step)
                if step < last_l - 1:
                    net.send(piece, piece, w_sems, slot_l + step + 1, net.left)
                w_twin(1 + step, parity, twin_slot + 1 + step)

    def w_end():
        for twin_slot, parity in ((0, net.x), (8, 1 - net.x)):
            for offset in range(8):
                net.arrived(w_piece(offset, parity, 1 - core), w_sems, TW + twin_slot + offset)

    count = ids.shape[1]

    def within(values, owner):
        offset = values - owner * vocab_dev
        return (offset >= 0) & (offset < vocab_dev), offset

    table[...] = jnp.zeros_like(table)
    table[0:columns, 0:vocab_dev] = raw_table[...]
    inside, offset = within(ids[...], me)
    owners = lax.broadcasted_iota(jnp.int32, (16, 1), 0)
    theirs, _ = within(ids[pl.ds(me, 1), :], owners)
    both = jnp.concatenate([jnp.where(inside, 1.0, 0.0), jnp.where(theirs, 1.0, 0.0)], 0)
    earlier = lax.broadcasted_iota(jnp.int32, (count, count), 0) < lax.broadcasted_iota(
        jnp.int32, (count, count), 1
    )
    rank = jnp.dot(
        both.astype(bf16), jnp.where(earlier, 1.0, 0.0).astype(bf16), preferred_element_type=f32
    )
    ranks[...] = jnp.where(inside, rank[0:16], -1.0)
    relatives[...] = offset.astype(f32)
    slot_of = jnp.where(theirs, rank[16:32] + owners.astype(f32) * SLOTS, 0.0)
    place_row = jnp.sum(slot_of, 0, keepdims=True)

    def pick(chunk, _):
        slots = lax.broadcasted_iota(jnp.int32, (SLOTS, 1), 0).astype(f32)
        wanted = []
        for step in range(4):
            other = pl.ds(lax.rem(me + 4 * chunk + step, 16), 1)
            chosen = ranks[other, :] == slots
            wanted.append(jnp.sum(jnp.where(chosen, relatives[other, :], 0.0), 1, keepdims=True))
        wanted = jnp.concatenate(wanted, 0).astype(jnp.int32)
        row = lax.broadcasted_iota(jnp.int32, (1, table.shape[1]), 1)
        one_hot = jnp.where(wanted == row, 1.0, 0.0).astype(bf16)
        rows = lax.dot_general(
            one_hot, table[...], (((1,), (1,)), ((), ())), preferred_element_type=f32
        ).astype(bf16)
        sent[pl.ds(4 * chunk, 4)] = rows.reshape(4, SLOTS, rows.shape[1])
        return 0

    def send_picked():
        got[me] = sent[0]
        for step in range(1, 16):
            other = lax.rem(me + step, 16)
            net.send(sent.at[step], got.at[me], f_sems, step - 1, other, "req")

    def spread():
        for step in range(1, 16):
            net.arrived(got.at[lax.rem(me + 16 - step, 16)], f_sems, step - 1)
        place = jnp.transpose(jnp.broadcast_to(place_row, (8, count)))[:, 0:1].astype(jnp.int32)
        slot = lax.broadcasted_iota(jnp.int32, (1, 16 * SLOTS), 1)
        one_hot = jnp.where(place == slot, 1.0, 0.0).astype(bf16)
        rows = jnp.dot(
            one_hot, got[...].reshape(16 * SLOTS, got.shape[2]), preferred_element_type=f32
        )
        picked[...] = rows.astype(bf16).reshape(picked.shape)
        mine[net.blk] = picked[net.blk]
        for step in range(1, 16):
            other = lax.rem(net.blk + step, 16)
            net.send(picked.at[other], mine.at[net.blk], g_sems, step - 1, other)

    def join():
        for step in range(1, 16):
            net.arrived(mine.at[lax.rem(net.blk + 16 - step, 16)], g_sems, step - 1)
        fresh[...] = jnp.concatenate([mine[index, :, 0:columns] for index in range(16)], 1)

    def first_qkv(request, _):
        rows_f32 = jnp.transpose(tokens[request].astype(f32))
        rows_out[request] = rows_f32.astype(bf16)
        qkv[request] = project(rows_f32, w_qkv[...])
        return 0

    lax.fori_loop(0, 4, pick, 0)
    send_picked()
    for g in PIECES:
        send(own.at[g], out.at[g, me], TWIN + g, twin)

    def from_below(g, other_x, base, forward):
        piece = out.at[g, device(-1, other_x)]
        arrived(piece, base + g)
        if g < 2:
            send(piece, piece, forward + g, up)
        share(-1, other_x, g)

    def from_above(g, other_x, base, forward):
        piece = out.at[g, device(1, other_x)]
        arrived(piece, base + g)
        if g >= 2:
            send(piece, piece, forward + g - 2, down)
        share(1, other_x, g)

    def from_far(g, other_x):
        piece = out.at[g, device(2, other_x)]
        if g < 2:
            arrived(piece, (UF1 if other_x else UF0) + g)
        else:
            arrived(piece, (DF1 if other_x else DF0) + g - 2)
        share(2, other_x, g)

    for g in PIECES:
        piece = out.at[g, side]
        arrived(piece, SIDE + g)
        send(piece, piece, U1 + g, up)
        send(piece, piece, D1 + g, down)
        share(0, 1, g)
        from_below(g, 0, U0, UF0)
        from_above(g, 0, D0, DF0)
        if g == PIECES[0]:
            w_begin()
        else:
            w_step(PIECES.index(g) - 1)
        if g == PIECES[-1]:
            spread()
    for g in PIECES:
        from_far(g, 0)
        from_below(g, 1, U1, UF1)
        from_above(g, 1, D1, DF1)
        if g == PIECES[0]:
            w_step(3)
            lax.fori_loop(0, 2, first_qkv, 0)
    for g in PIECES:
        from_far(g, 1)
    for (step, other_x), place in places.items():
        for g in PIECES:
            arrived(out.at[g, device(step, other_x, True)], TWIN + 4 * place + g)
    join()
    w_end()
    for keep in keeps:
        keep.wait()
    for copy in started:
        copy.wait_send()
    net.finish()


def start_gathers(own, w_own, ids, table, tokens, w_qkv, collective_id):
    groups = own.shape[0]
    count = ids.shape[1]
    columns, vocab_dev = table.shape
    requests, width, rows = tokens.shape
    bf16 = jnp.bfloat16
    blocks = pltpu.VMEM((16, SLOTS, 128), bf16)
    asked = pltpu.VMEM((16, count // 16, 128), bf16)
    return pl.pallas_call(
        start_kernel,
        out_shape=(
            jax.ShapeDtypeStruct((groups, 16) + own.shape[1:], own.dtype),
            jax.ShapeDtypeStruct((8, 2) + w_own.shape, w_own.dtype),
            jax.ShapeDtypeStruct((count // 16, 16 * columns), bf16),
            jax.ShapeDtypeStruct((requests, rows, width), bf16),
            jax.ShapeDtypeStruct((requests, rows, 256), bf16),
        ),
        in_specs=[pl.BlockSpec(memory_space=pl.ANY)] * 2 + whole(4),
        out_specs=(pl.BlockSpec(memory_space=pl.ANY),) * 2 + tuple(whole(3)),
        scratch_shapes=[
            pltpu.VMEM((128, -(-vocab_dev // 128) * 128), bf16),
            pltpu.VMEM((16, count), jnp.float32),
            pltpu.VMEM((16, count), jnp.float32),
            blocks,
            blocks,
            asked,
            asked,
            pltpu.SemaphoreType.DMA((2,)),
        ]
        + sem_pair(60)
        + sem_pair(31)
        + sem_pair(15)
        + sem_pair(15),
        compiler_params=pltpu.CompilerParams(
            collective_id=collective_id, has_side_effects=True, vmem_limit_bytes=40 << 20
        ),
        cost_estimate=busy(45),
        name="start_gathers",
    )(own, w_own, ids, table, tokens, w_qkv)


def asked_rows(new_ids):
    by_device = new_ids.reshape(new_ids.shape[0], 16, 2, 8, -1)
    return jnp.transpose(by_device, (1, 3, 2, 0, 4)).reshape(16, -1)


def settle_fresh(quick, ids, embed_table, req_index):
    vocab_dev = embed_table.shape[0]
    owner = ids // vocab_dev
    owners = jnp.arange(16)[:, None]
    asked = jnp.sum((owner[:, None, :] == owners[None]).astype(jnp.int32), -1)
    crowded = jnp.max(asked) > SLOTS

    def dense():
        relative = (ids - req_index * vocab_dev).reshape(-1)
        here = (relative >= 0) & (relative < vocab_dev)
        looked = jnp.take(embed_table, jnp.clip(relative, 0, vocab_dev - 1), axis=0)
        looked = jnp.where(here[:, None], looked, jnp.zeros((), jnp.bfloat16))
        looked = lax.all_to_all(
            looked.reshape(16, -1, looked.shape[1]), "req", split_axis=0, concat_axis=0, tiled=True
        )
        summed = jnp.sum(looked.astype(jnp.float32), 0).astype(jnp.bfloat16)
        summed = summed.reshape(16, -1, summed.shape[1])
        mine = lax.all_to_all(summed, "blk", split_axis=0, concat_axis=0, tiled=True)
        return jnp.transpose(mine, (1, 0, 2)).reshape(quick.shape)

    return lax.cond(crowded, dense, lambda: quick)


def attend_kernel(groups, lengths, qkv, cache, out, *, span):
    length = lengths[pl.program_id(0)]
    q, own_block = qkv[0, :, 0:128], qkv[0, :, 128:256]
    f32 = jnp.float32

    def scores_of(keys):
        return lax.dot_general(q, keys, (((1,), (1,)), ((), ())), preferred_element_type=f32)

    def weigh(weights, values):
        return jnp.dot(weights.astype(jnp.bfloat16), values, preferred_element_type=f32)

    scores = scores_of(own_block)
    top = jnp.max(scores, -1, keepdims=True)
    weights = jnp.exp(scores - top)
    total = jnp.sum(weights, -1, keepdims=True)
    mixed = weigh(weights, own_block)
    for start in range(0, cache.shape[1], span):
        block = cache[0, start : start + span, :]
        position = start + lax.broadcasted_iota(jnp.int32, (1, span), 1)
        scores = scores_of(block) + jnp.where(position < length, 0.0, NEG).astype(f32)
        raised = jnp.maximum(top, jnp.max(scores, -1, keepdims=True))
        shrink = jnp.exp(top - raised)
        weights = jnp.exp(scores - raised)
        total = total * shrink + jnp.sum(weights, -1, keepdims=True)
        mixed = mixed * shrink + weigh(weights, block)
        top = raised
    head = mixed / total
    parity = lax.axis_index("blk") % 2
    lane = lax.broadcasted_iota(jnp.int32, (1, 128), 1)
    moved = jnp.where(parity == 0, pltpu.roll(head, 64, 1), head)
    out[0] = jnp.where(lane // 64 == parity, moved, 0.0).astype(out.dtype)


def attend(qkv, cache, groups, lengths):
    requests, rows, width = qkv.shape
    size = cache.shape[1]
    return pl.pallas_call(
        functools.partial(attend_kernel, span=min(2048, size)),
        out_shape=jax.ShapeDtypeStruct((requests, rows, 128), jnp.bfloat16),
        grid_spec=pltpu.PrefetchScalarGridSpec(
            num_scalar_prefetch=2,
            grid=(requests,),
            in_specs=[
                pl.BlockSpec((1, rows, width), lambda r, g, n: (r, 0, 0)),
                pl.BlockSpec((1, size, 128), lambda r, g, n: (g[r], 0, 0)),
            ],
            out_specs=pl.BlockSpec((1, rows, 128), lambda r, g, n: (r, 0, 0)),
        ),
        compiler_params=pltpu.CompilerParams(vmem_limit_bytes=58 << 20),
        cost_estimate=busy(11),
        name="attend",
    )(groups, lengths, qkv, cache)


def shards(
    tokens, cache_kv, w_qkv, w_out, w_fc, w_proj, embed_table, group_ids, cache_len, accept, new_ids
):
    req_index = lax.axis_index("req")
    blk_index = lax.axis_index("blk")
    z, x, core = blk_index // 2, blk_index % 2, req_index % 2
    requests, rows, width = tokens.shape
    kv_width = cache_kv.shape[3]
    head_dim = kv_width // 2
    share = rows // 8
    my_groups = lax.dynamic_slice_in_dim(group_ids, req_index * requests, requests)
    lengths = jnp.take(cache_len, my_groups)
    w_own = jnp.transpose(w_qkv[:, 0, :])
    w_fc = jnp.transpose(w_fc)
    pairs = [(index, index ^ 1) for index in range(16)]
    hidden = w_fc.shape[0] // 2
    halves = jnp.stack(
        [lax.dynamic_slice_in_dim(weights, core * hidden, hidden, 0) for weights in (w_fc, w_proj)]
    )
    others = lax.ppermute(halves, "blk", pairs)
    w_other = lax.ppermute(w_own, "blk", pairs)
    ids = asked_rows(new_ids)
    every_cache, all_w_out, fresh, current, qkv = start_gathers(
        cache_kv[:, :, 0, :], w_out.reshape(2, head_dim // 2, width), ids, jnp.transpose(embed_table), jnp.transpose(tokens, (0, 2, 1)), w_own, 1
    )
    all_w_out = all_w_out.reshape(16 * head_dim, width)
    every_cache = every_cache.reshape(cache_kv.shape[0], -1, kv_width)
    others, w_other, fresh = lax.optimization_barrier((others, w_other, fresh))
    twins = lax.ppermute(others, "req", pairs)
    weights = (all_w_out, w_fc, w_proj, others, twins)

    my_accept = lax.dynamic_index_in_dim(accept, x, 1, keepdims=False)
    my_accept = lax.dynamic_slice_in_dim(my_accept, z * share, share, 1)[..., None]
    heads = attend(qkv, every_cache, my_groups, lengths)
    every_head = gather_heads(heads, 2)
    fresh = settle_fresh(fresh, ids, embed_table, req_index).reshape(PASSES, share, width)
    for pass_index in range(PASSES):
        last = pass_index == PASSES - 1
        grown, my_middle = mlp(every_head, current, weights)
        done = reduce_blk(
            grown.reshape(8, share, width),
            my_middle,
            fresh[pass_index],
            my_accept[pass_index],
            None if last else (w_own, w_other),
            3 + 2 * pass_index,
        )
        if last:
            return done[0].reshape(requests, rows, width)
        current = done[0].reshape(rows, width)
        heads = attend(done[1], every_cache, my_groups, lengths)
        every_head = gather_heads(heads, 2)


def solution(mesh):
    return jax.shard_map(
        shards,
        mesh=mesh,
        in_specs=(
            P("req", None, None),
            P(None, "req", "blk", None),
            P(None, "blk", None),
            P("blk", None, None),
            P(None, "blk"),
            P("blk", None),
            P("req", "blk"),
            P(),
            P(),
            P(None, "req", None),
            P(),
        ),
        out_specs=P("req", None, None),
        check_vma=False,
    )
```

```python
import functools

import jax
import jax.numpy as jnp
from jax import lax
from jax.experimental import pallas as pl
from jax.experimental.pallas import tpu as pltpu
from jax.sharding import PartitionSpec as P

PASSES = 2
MESH = pl.DeviceIdType.MESH
NEG = -1e30


def layer_norm(values):
    centre = values - jnp.mean(values, -1, keepdims=True)
    spread = jnp.mean(centre * centre, -1, keepdims=True)
    return centre * lax.rsqrt(spread + 1e-05)


class Net:
    def __init__(self):
        self.blk = lax.axis_index("blk")
        self.z = self.blk // 2
        self.x = self.blk % 2
        self.right = self.ring(1) * 2 + self.x
        self.left = self.ring(-1) * 2 + self.x
        self.pair = self.z * 2 + 1 - self.x
        self.started = []

    def ring(self, offset):
        return lax.rem(self.z + 8 + offset, 8)

    def greet(self, axis="blk", others=None):
        barrier = pltpu.get_barrier_semaphore()
        others = (self.right, self.left, self.pair) if others is None else others
        for other in others:
            pl.semaphore_signal(barrier, inc=1, device_id={axis: other}, device_id_type=MESH)
        pl.semaphore_wait(barrier, len(others))

    def copy_of(self, src, dst, sems, slot, other, axis):
        return pltpu.make_async_remote_copy(
            src_ref=src,
            dst_ref=dst,
            send_sem=sems[0].at[slot],
            recv_sem=sems[1].at[slot],
            device_id={axis: other},
            device_id_type=MESH,
        )

    def send(self, src, dst, sems, slot, other, axis="blk"):
        copy = self.copy_of(src, dst, sems, slot, other, axis)
        copy.start()
        self.started.append(copy)

    def arrived(self, dst, sems, slot):
        self.copy_of(dst, dst, sems, slot, self.pair, "blk").wait_recv()

    def finish(self):
        for copy in self.started:
            copy.wait_send()


def busy(us):
    return pl.CostEstimate(flops=us * 400_000_000, bytes_accessed=us * 3_000_000, transcendentals=0)


def sem_pair(count):
    return [pltpu.SemaphoreType.DMA((count,)), pltpu.SemaphoreType.DMA((count,))]


def whole(count):
    return [pl.BlockSpec(memory_space=pltpu.VMEM)] * count


RING_A, RING_B, RING_C, RING_D = 0, 4, 7, 10
RING_SLOTS = 14


def ring_begin(net, out, sems, half, high):
    piece = out.at[net.z, half : 2 * half] if high else out.at[net.z, 0:half]
    net.send(piece, piece, sems, RING_B if high else RING_A, net.right)
    net.send(piece, piece, sems, RING_D if high else RING_C, net.left)


def ring_rest(net, out, sems, half):
    def take(offset, high, slot, last, target):
        at = net.ring(offset)
        piece = out.at[at, half : 2 * half] if high else out.at[at, 0:half]
        net.arrived(piece, sems, slot)
        if not last:
            net.send(piece, piece, sems, slot + 1, target)

    for step in range(1, 5):
        take(-step, False, RING_A + step - 1, step == 4, net.right)
        take(step, True, RING_D + step - 1, step == 4, net.left)
        if step < 4:
            take(-step, True, RING_B + step - 1, step == 3, net.right)
            take(step, False, RING_C + step - 1, step == 3, net.left)


def swap_heads(net, heads, peer, out, ring_sems, pair_sems):
    half = heads.shape[1] // 2
    parts = (slice(0, half), slice(half, 2 * half))
    for part, rows in enumerate(parts):
        net.send(heads.at[1 - net.x, rows], peer.at[rows], pair_sems, part, net.pair)
    for part, rows in enumerate(parts):
        net.arrived(peer.at[rows], pair_sems, part)
        out[net.z, rows] = heads[net.x, rows] + peer[rows]
        ring_begin(net, out, ring_sems, half, part == 1)
    ring_rest(net, out, ring_sems, half)


def mlp(net, every_head, current, w_out, w_mlp, w_mlp_pair, head_rows, middle):
    f32, bf16 = jnp.float32, jnp.bfloat16
    for z in range(8):
        head_rows[:, 128 * z : 128 * (z + 1)] = every_head[z]
    middle[...] = current[...].astype(f32) + jnp.dot(
        head_rows[...], w_out[...], preferred_element_type=f32
    )
    normed = layer_norm(middle[...]).astype(bf16)

    def term(weights):
        raw = lax.dot_general(
            normed, weights[0], (((1,), (1,)), ((), ())), preferred_element_type=f32
        )
        rows = jax.nn.gelu(raw, approximate=True).astype(bf16)
        return jnp.dot(rows, weights[1], preferred_element_type=f32)

    return (term(w_mlp) + term(w_mlp_pair)).astype(bf16)


def project(rows_f32, weights):
    f32, bf16 = jnp.float32, jnp.bfloat16
    normed = layer_norm(rows_f32).astype(bf16)
    got = lax.dot_general(normed, weights, (((1,), (1,)), ((), ())), preferred_element_type=f32)
    got = jnp.concatenate([got, jnp.zeros((got.shape[0], 64), f32)], 1)
    lane = lax.broadcasted_iota(jnp.int32, (1, 128), 1)
    queries = jnp.where(lane < 64, got[:, 0:128].astype(bf16).astype(f32) * 0.125, 0.0)
    return jnp.concatenate([queries, pltpu.roll(got, 192, 1)[:, 0:128]], 1).astype(bf16)


def pass_kernel(heads, fresh, accept, current_in, *refs, last):
    net = Net()
    current_in = current_in.at[net.x] if len(current_in.shape) == 3 else current_in
    loads = 4 if last else 6
    sources, refs = (current_in,) + tuple(refs[0 : loads - 1]), refs[loads - 1 :]
    if last:
        out, *refs = refs
    else:
        out, qkv, stage, *refs = refs
    held, refs = refs[0:loads], refs[loads:]
    load_sems, peer, every_head, head_rows, middle_all, part, *refs = refs
    right_low, right_high, left_low, left_high, *sem_refs = refs
    copies = [
        pltpu.make_async_copy(source, place, load_sems.at[index])
        for index, (source, place) in enumerate(zip(sources, held))
    ]
    current, w_out, w_mlp, w_mlp_pair = held[0:4]
    sems, gather_sems, head_sems, pair_sems, swap_sems = (
        tuple(sem_refs[index : index + 2]) for index in range(0, 10, 2)
    )
    half = part.shape[1] // 2
    f32, bf16 = jnp.float32, jnp.bfloat16
    low, high = slice(0, half), slice(half, 2 * half)
    for copy in copies:
        copy.start()
    net.greet()
    swap_heads(net, heads, peer, every_head, head_sems, pair_sems)
    for copy in copies:
        copy.wait()
    grown = mlp(net, every_head, current, w_out, w_mlp, w_mlp_pair, head_rows, middle_all)
    part[...] = grown.reshape(part.shape)

    def begin(buf, rows, slot, offset, target):
        net.send(part.at[net.ring(offset), rows], buf.at[0], sems, slot, target)

    def hand_on(buf, rows, slot, step, offset, target):
        piece = buf.at[step]
        net.arrived(piece, sems, slot + step)
        total = piece[...].astype(f32) + part[net.ring(offset), rows].astype(f32)
        buf[step] = total.astype(bf16)
        net.send(piece, buf.at[step + 1], sems, slot + step + 1, target)

    begin(right_low, low, RING_A, 4, net.right)
    begin(left_high, high, RING_D, -4, net.left)
    begin(right_high, high, RING_B, 3, net.right)
    begin(left_low, low, RING_C, -3, net.left)
    for step in range(3):
        hand_on(right_low, low, RING_A, step, 3 - step, net.right)
        hand_on(left_high, high, RING_D, step, step - 3, net.left)
        if step < 2:
            hand_on(right_high, high, RING_B, step, 2 - step, net.right)
            hand_on(left_low, low, RING_C, step, step - 2, net.left)

    def close(rows, from_left, from_right):
        total = part[net.z, rows].astype(f32) + from_left.astype(f32) + from_right.astype(f32)
        start = pl.multiple_of(net.z * 2 * half + rows.start, half)
        layer_out = (middle_all[pl.ds(start, half), :] + total).astype(bf16)
        return jnp.where(accept[rows] == 1, fresh[rows], layer_out)

    net.arrived(left_low.at[2], sems, RING_C + 2)
    net.arrived(right_low.at[3], sems, RING_A + 3)
    result = close(low, right_low[3], left_low[2])
    if last:
        out[net.x, net.z, low] = result
        gather_begin_low(net, out, gather_sems, half)
    else:
        out[net.z, low] = result
        ring_begin(net, out, gather_sems, half, False)
    net.arrived(right_high.at[2], sems, RING_B + 2)
    net.arrived(left_high.at[3], sems, RING_D + 3)
    result = close(high, right_high[2], left_high[3])
    if last:
        out[net.x, net.z, high] = result
        gather_begin_high(net, out, gather_sems, half)
        gather_rest(net, out, gather_sems, half)
    else:
        out[net.z, high] = result
        ring_begin(net, out, gather_sems, half, True)
        ring_rest(net, out, gather_sems, half)
        rows_f32 = out[...].reshape(8 * 2 * half, out.shape[2]).astype(f32)
        w_own, w_pair = held[4:6]
        stage[...] = project(rows_f32, w_pair[...])
        net.send(stage, qkv.at[net.x], swap_sems, 0, net.pair)
        qkv[net.x] = project(rows_f32, w_own[...])
        net.arrived(qkv.at[1 - net.x], swap_sems, 0)
    net.finish()


def run_pass(heads, current, w_out, w_mlp, w_mlp_pair, fresh, accept, w_qkv_both, collective_id):
    rows, width = current.shape[-2:]
    lanes, share = heads.shape[2], rows // 8
    bf16 = jnp.bfloat16
    last = w_qkv_both is None
    block = (share // 2, width)
    operands = (heads, fresh, accept, current, w_out, w_mlp, w_mlp_pair)
    if last:
        shapes = (jax.ShapeDtypeStruct((2, 8, share, width), bf16),)
        first, gather = [], GATHER_SLOTS
    else:
        operands = operands + w_qkv_both
        shapes = (
            jax.ShapeDtypeStruct((8, share, width), bf16),
            jax.ShapeDtypeStruct((2, rows, 256), bf16),
        )
        first, gather = [pltpu.VMEM((rows, 256), bf16)], RING_SLOTS
    held = [pltpu.VMEM(array.shape[-2:] if array is current else array.shape, bf16) for array in operands[3:]]
    scratch = first + held + [pltpu.SemaphoreType.DMA((len(held),))] + [
        pltpu.VMEM((rows, lanes), bf16),
        pltpu.VMEM((8, rows, lanes), bf16),
        pltpu.VMEM((rows, 8 * lanes), bf16),
        pltpu.VMEM((rows, width), jnp.float32),
        pltpu.VMEM((8, share, width), bf16),
    ]
    rings = [pltpu.VMEM((count,) + block, bf16) for count in (4, 3, 3, 4)]
    sems = []
    for count in (RING_SLOTS, gather, RING_SLOTS, 2, 1):
        sems = sems + sem_pair(count)
    return pl.pallas_call(
        functools.partial(pass_kernel, last=last),
        out_shape=shapes,
        in_specs=whole(3) + [pl.BlockSpec(memory_space=pl.ANY)] * len(held),
        out_specs=tuple(whole(len(shapes))),
        scratch_shapes=scratch + rings + sems,
        compiler_params=pltpu.CompilerParams(
            collective_id=collective_id, has_side_effects=True, vmem_limit_bytes=56 << 20
        ),
        cost_estimate=busy(50),
        name=f"pass_{collective_id}",
    )(*operands)


R_A, R_B, R_O, L_A, L_B, L_O, X_A, X_B = 0, 4, 8, 12, 16, 20, 24, 25
GATHER_SLOTS = 33


def gather_begin_low(net, out, sems, half):
    low = out.at[net.x, net.z, 0:half]
    net.send(low, low, sems, R_A + 0, net.right)
    net.send(low, low, sems, L_A + 0, net.left)
    net.send(low, low, sems, X_A, net.pair)


def gather_begin_high(net, out, sems, half):
    high = out.at[net.x, net.z, half : 2 * half]
    net.send(high, high, sems, R_B + 0, net.right)
    net.send(high, high, sems, L_B + 0, net.left)
    net.send(high, high, sems, X_B + 0, net.pair)


def gather_rest(net, out, sems, half):
    other = 1 - net.x
    peer_low = out.at[other, net.z, 0:half]
    net.arrived(peer_low, sems, X_A)
    net.send(peer_low, peer_low, sems, R_O + 0, net.right)
    net.send(peer_low, peer_low, sems, L_O + 0, net.left)
    for step in range(1, 5):
        before, after = net.ring(-step), net.ring(step)
        piece = out.at[net.x, before, 0:half]
        net.arrived(piece, sems, R_A + step - 1)
        if step < 4:
            net.send(piece, piece, sems, R_A + step, net.right)
        piece = out.at[net.x, after, half : 2 * half]
        net.arrived(piece, sems, L_B + step - 1)
        if step < 4:
            net.send(piece, piece, sems, L_B + step, net.left)
        net.send(piece, piece, sems, X_B + (step if step < 4 else 7), net.pair)
        piece = out.at[other, after, 0:half]
        net.arrived(piece, sems, L_O + step - 1)
        if step < 4:
            net.send(piece, piece, sems, L_O + step, net.left)
        if step < 4:
            piece = out.at[net.x, after, 0:half]
            net.arrived(piece, sems, L_A + step - 1)
            if step < 3:
                net.send(piece, piece, sems, L_A + step, net.left)
            piece = out.at[net.x, before, half : 2 * half]
            net.arrived(piece, sems, R_B + step - 1)
            if step < 3:
                net.send(piece, piece, sems, R_B + step, net.right)
            net.send(piece, piece, sems, X_B + 3 + step, net.pair)
            piece = out.at[other, before, 0:half]
            net.arrived(piece, sems, R_O + step - 1)
            if step < 3:
                net.send(piece, piece, sems, R_O + step, net.right)
    for slot, offset in ((0, 0), (1, 1), (2, 2), (3, 3), (7, 4), (4, -1), (5, -2), (6, -3)):
        net.arrived(out.at[other, net.ring(offset), half : 2 * half], sems, X_B + slot)


PIECES = (0, 2, 1, 3)


SLOTS = 128


def start_kernel(
    own, w_own, ids, raw_table, tokens_in, w_qkv_in, w_mlp, out, w_all, w_mlp_pair, w_qkv_pair, fresh, rows_out,
    qkv, tokens, w_qkv, table, ranks, relatives, sent, got, picked, mine, copy_sems,
    send_sems, recv_sems, send_w, recv_w, send_f, recv_f, send_g, recv_g, send_m, recv_m,
):
    net = Net()
    f32, bf16 = jnp.float32, jnp.bfloat16
    me = lax.axis_index("req")
    y, x, core = me // 4, (me // 2) % 2, me % 2

    def device(step, other_x, other_core=False):
        return (
            lax.rem(y + 4 + step, 4) * 4
            + (1 - x if other_x else x) * 2
            + (1 - core if other_core else core)
        )

    up, down, side, twin = device(1, 0), device(-1, 0), device(0, 1), device(0, 0, True)
    barrier = pltpu.get_barrier_semaphore()
    for step in range(1, 16):
        other = lax.rem(me + step, 16)
        pl.semaphore_signal(barrier, inc=1, device_id={"req": other}, device_id_type=MESH)
    for step in range(1, 16):
        other = lax.rem(net.blk + step, 16)
        pl.semaphore_signal(barrier, inc=1, device_id={"blk": other}, device_id_type=MESH)
    cross = {"req": side, "blk": net.pair}
    pl.semaphore_signal(barrier, inc=1, device_id=cross, device_id_type=MESH)
    pl.semaphore_wait(barrier, 31)
    w_sems, f_sems, g_sems, m_sems = (send_w, recv_w), (send_f, recv_f), (send_g, recv_g), (send_m, recv_m)
    columns, vocab_dev = raw_table.shape
    started = []

    def copy_of(src, dst, slot, other):
        return pltpu.make_async_remote_copy(
            src_ref=src,
            dst_ref=dst,
            send_sem=send_sems.at[slot],
            recv_sem=recv_sems.at[slot],
            device_id={"req": other},
            device_id_type=MESH,
        )

    def send(src, dst, slot, other):
        copy = copy_of(src, dst, slot, other)
        copy.start()
        started.append(copy)

    def arrived(dst, slot):
        copy_of(dst, dst, slot, twin).wait_recv()

    U0, D0, SIDE, U1, D1, UF0, UF1, DF0, DF1, TWIN = 0, 4, 8, 12, 16, 20, 22, 24, 26, 28
    places = {(0, 0): 0, (0, 1): 1, (-1, 0): 2, (1, 0): 3, (-1, 1): 4, (1, 1): 5, (2, 0): 6, (2, 1): 7}

    def share(step, other_x, g):
        piece = out.at[g, device(step, other_x)]
        send(piece, piece, TWIN + 4 * places[(step, other_x)] + g, twin)

    for g in PIECES:
        dst = out.at[g, me]
        send(own.at[g], dst, U0 + g, up)
        send(own.at[g], dst, D0 + g, down)
        send(own.at[g], dst, SIDE + g, side)
    RO, LO, RQ, LQ, PX, TW = 0, 4, 7, 10, 14, 15

    def w_piece(offset, parity, half):
        return w_all.at[net.ring(offset), parity, half]

    def w_twin(offset, parity, slot):
        piece = w_piece(offset, parity, core)
        net.send(piece, piece, w_sems, TW + slot, twin, "req")

    w_half, w_mine = w_own.at[core], w_piece(0, net.x, core)
    net.send(w_half, w_mine, w_sems, PX, net.pair)
    net.send(w_half, w_mine, w_sems, RO, net.right)
    net.send(w_half, w_mine, w_sems, LO, net.left)
    net.send(w_half, w_mine, w_sems, TW, twin, "req")
    keeps = [
        pltpu.make_async_copy(own, out.at[:, me], copy_sems.at[0]),
        pltpu.make_async_copy(w_half, w_mine, copy_sems.at[1]),
    ]
    loads = [
        pltpu.make_async_copy(tokens_in, tokens, copy_sems.at[2]),
        pltpu.make_async_copy(w_qkv_in, w_qkv, copy_sems.at[3]),
    ]
    for copy in keeps + loads:
        copy.start()

    units, half_qkv = w_mlp.shape[1] // 5, w_qkv_pair.shape[0] // 2

    def pair_pieces(which):
        for index in range(5):
            rows = pl.ds(index * units, units)
            yield w_mlp.at[which, rows], w_mlp_pair.at[which, rows]
        rows = pl.ds(pl.multiple_of(which * half_qkv, half_qkv), half_qkv)
        yield w_qkv_in.at[rows], w_qkv_pair.at[rows]

    def pair_send():
        for slot, (src, dst) in enumerate(pair_pieces(core)):
            where = {"blk": net.pair} if slot < 3 else cross
            copy = pltpu.make_async_remote_copy(
                src_ref=src,
                dst_ref=dst,
                send_sem=m_sems[0].at[slot],
                recv_sem=m_sems[1].at[slot],
                device_id=where,
                device_id_type=MESH,
            )
            copy.start()
            started.append(copy)

    def pair_share():
        for slot, (_, dst) in enumerate(pair_pieces(core)):
            net.arrived(dst, m_sems, slot)
            net.send(dst, dst, m_sems, 6 + slot, twin, "req")

    def pair_end():
        for slot, (_, dst) in enumerate(pair_pieces(1 - core)):
            net.arrived(dst, m_sems, 6 + slot)

    def w_begin():
        piece = w_piece(0, 1 - net.x, core)
        net.arrived(piece, w_sems, PX)
        net.send(piece, piece, w_sems, RQ, net.right)
        net.send(piece, piece, w_sems, LQ, net.left)
        w_twin(0, 1 - net.x, 8)

    def w_step(step):
        for parity, slot_r, slot_l, last_r, last_l, twin_slot in (
            (net.x, RO, LO, 4, 3, 0), (1 - net.x, RQ, LQ, 3, 4, 8)
        ):
            if step < last_r:
                piece = w_piece(-1 - step, parity, core)
                net.arrived(piece, w_sems, slot_r + step)
                if step < last_r - 1:
                    net.send(piece, piece, w_sems, slot_r + step + 1, net.right)
                w_twin(-1 - step, parity, twin_slot + (7 - step))
            if step < last_l:
                piece = w_piece(1 + step, parity, core)
                net.arrived(piece, w_sems, slot_l + step)
                if step < last_l - 1:
                    net.send(piece, piece, w_sems, slot_l + step + 1, net.left)
                w_twin(1 + step, parity, twin_slot + 1 + step)

    def w_end():
        for twin_slot, parity in ((0, net.x), (8, 1 - net.x)):
            for offset in range(8):
                net.arrived(w_piece(offset, parity, 1 - core), w_sems, TW + twin_slot + offset)

    count = ids.shape[1]

    def within(values, owner):
        offset = values - owner * vocab_dev
        return (offset >= 0) & (offset < vocab_dev), offset

    table[...] = jnp.zeros_like(table)
    table[0:columns, 0:vocab_dev] = raw_table[...]
    inside, offset = within(ids[...], me)
    owners = lax.broadcasted_iota(jnp.int32, (16, 1), 0)
    theirs, _ = within(ids[pl.ds(me, 1), :], owners)
    both = jnp.concatenate([jnp.where(inside, 1.0, 0.0), jnp.where(theirs, 1.0, 0.0)], 0)
    earlier = lax.broadcasted_iota(jnp.int32, (count, count), 0) < lax.broadcasted_iota(
        jnp.int32, (count, count), 1
    )
    rank = jnp.dot(
        both.astype(bf16), jnp.where(earlier, 1.0, 0.0).astype(bf16), preferred_element_type=f32
    )
    ranks[...] = jnp.where(inside, rank[0:16], -1.0)
    relatives[...] = offset.astype(f32)
    slot_of = jnp.where(theirs, rank[16:32] + owners.astype(f32) * SLOTS, 0.0)
    place_row = jnp.sum(slot_of, 0, keepdims=True)

    def pick(chunk, _):
        slots = lax.broadcasted_iota(jnp.int32, (SLOTS, 1), 0).astype(f32)
        wanted = []
        for step in range(4):
            other = pl.ds(lax.rem(me + 4 * chunk + step, 16), 1)
            chosen = ranks[other, :] == slots
            wanted.append(jnp.sum(jnp.where(chosen, relatives[other, :], 0.0), 1, keepdims=True))
        wanted = jnp.concatenate(wanted, 0).astype(jnp.int32)
        row = lax.broadcasted_iota(jnp.int32, (1, table.shape[1]), 1)
        one_hot = jnp.where(wanted == row, 1.0, 0.0).astype(bf16)
        rows = lax.dot_general(
            one_hot, table[...], (((1,), (1,)), ((), ())), preferred_element_type=f32
        ).astype(bf16)
        sent[pl.ds(4 * chunk, 4)] = rows.reshape(4, SLOTS, rows.shape[1])
        return 0

    def send_picked():
        got[me] = sent[0]
        for step in range(1, 16):
            other = lax.rem(me + step, 16)
            net.send(sent.at[step], got.at[me], f_sems, step - 1, other, "req")

    def spread():
        for step in range(1, 16):
            net.arrived(got.at[lax.rem(me + 16 - step, 16)], f_sems, step - 1)
        place = jnp.transpose(jnp.broadcast_to(place_row, (8, count)))[:, 0:1].astype(jnp.int32)
        slot = lax.broadcasted_iota(jnp.int32, (1, 16 * SLOTS), 1)
        one_hot = jnp.where(place == slot, 1.0, 0.0).astype(bf16)
        rows = jnp.dot(
            one_hot, got[...].reshape(16 * SLOTS, got.shape[2]), preferred_element_type=f32
        )
        picked[...] = rows.astype(bf16).reshape(picked.shape)
        mine[net.blk] = picked[net.blk]
        for step in range(1, 16):
            other = lax.rem(net.blk + step, 16)
            net.send(picked.at[other], mine.at[net.blk], g_sems, step - 1, other)

    def join():
        for step in range(1, 16):
            net.arrived(mine.at[lax.rem(net.blk + 16 - step, 16)], g_sems, step - 1)
        fresh[...] = jnp.concatenate([mine[index, :, 0:columns] for index in range(16)], 1)

    def first_qkv(request, _):
        rows_f32 = jnp.transpose(tokens[request].astype(f32))
        rows_out[request] = rows_f32.astype(bf16)
        qkv[request] = project(rows_f32, w_qkv[...])
        return 0

    lax.fori_loop(0, 4, pick, 0)
    send_picked()
    for g in PIECES:
        send(own.at[g], out.at[g, me], TWIN + g, twin)

    def from_below(g, other_x, base, forward):
        piece = out.at[g, device(-1, other_x)]
        arrived(piece, base + g)
        if g < 2:
            send(piece, piece, forward + g, up)
        share(-1, other_x, g)

    def from_above(g, other_x, base, forward):
        piece = out.at[g, device(1, other_x)]
        arrived(piece, base + g)
        if g >= 2:
            send(piece, piece, forward + g - 2, down)
        share(1, other_x, g)

    def from_far(g, other_x):
        piece = out.at[g, device(2, other_x)]
        if g < 2:
            arrived(piece, (UF1 if other_x else UF0) + g)
        else:
            arrived(piece, (DF1 if other_x else DF0) + g - 2)
        share(2, other_x, g)

    for g in PIECES:
        piece = out.at[g, side]
        arrived(piece, SIDE + g)
        send(piece, piece, U1 + g, up)
        send(piece, piece, D1 + g, down)
        share(0, 1, g)
        from_below(g, 0, U0, UF0)
        from_above(g, 0, D0, DF0)
        if g == PIECES[0]:
            w_begin()
        else:
            w_step(PIECES.index(g) - 1)
        if g == PIECES[-1]:
            pair_send()
            spread()
    for g in PIECES:
        from_far(g, 0)
        from_below(g, 1, U1, UF1)
        from_above(g, 1, D1, DF1)
        if g == PIECES[0]:
            w_step(3)
            for load in loads:
                load.wait()
            lax.fori_loop(0, 2, first_qkv, 0)
    for g in PIECES:
        from_far(g, 1)
    for (step, other_x), place in places.items():
        for g in PIECES:
            arrived(out.at[g, device(step, other_x, True)], TWIN + 4 * place + g)
    pair_share()
    join()
    w_end()
    pair_end()
    for keep in keeps:
        keep.wait()
    for copy in started:
        copy.wait_send()
    net.finish()


def start_gathers(own, w_own, ids, table, tokens, w_qkv, w_mlp, collective_id):
    groups = own.shape[0]
    count = ids.shape[1]
    columns, vocab_dev = table.shape
    requests, width, rows = tokens.shape
    bf16 = jnp.bfloat16
    blocks = pltpu.VMEM((16, SLOTS, 128), bf16)
    asked = pltpu.VMEM((16, count // 16, 128), bf16)
    anywhere = [pl.BlockSpec(memory_space=pl.ANY)]
    return pl.pallas_call(
        start_kernel,
        out_shape=(
            jax.ShapeDtypeStruct((groups, 16) + own.shape[1:], own.dtype),
            jax.ShapeDtypeStruct((8, 2) + w_own.shape, w_own.dtype),
            jax.ShapeDtypeStruct(w_mlp.shape, w_mlp.dtype),
            jax.ShapeDtypeStruct(w_qkv.shape, w_qkv.dtype),
            jax.ShapeDtypeStruct((count // 16, 16 * columns), bf16),
            jax.ShapeDtypeStruct((requests, rows, width), bf16),
            jax.ShapeDtypeStruct((requests, rows, 256), bf16),
        ),
        in_specs=anywhere * 2 + whole(2) + anywhere * 3,
        out_specs=tuple(anywhere * 4 + whole(3)),
        scratch_shapes=[
            pltpu.VMEM(tokens.shape, bf16),
            pltpu.VMEM(w_qkv.shape, bf16),
            pltpu.VMEM((128, -(-vocab_dev // 128) * 128), bf16),
            pltpu.VMEM((16, count), jnp.float32),
            pltpu.VMEM((16, count), jnp.float32),
            blocks,
            blocks,
            asked,
            asked,
            pltpu.SemaphoreType.DMA((4,)),
        ]
        + sem_pair(60)
        + sem_pair(31)
        + sem_pair(15)
        + sem_pair(15)
        + sem_pair(12),
        compiler_params=pltpu.CompilerParams(
            collective_id=collective_id, has_side_effects=True, vmem_limit_bytes=58 << 20
        ),
        cost_estimate=busy(45),
        name="start_gathers",
    )(own, w_own, ids, table, tokens, w_qkv, w_mlp)


def asked_rows(new_ids):
    by_device = new_ids.reshape(new_ids.shape[0], 16, 2, 8, -1)
    return jnp.transpose(by_device, (1, 3, 2, 0, 4)).reshape(16, -1)


def settle_fresh(quick, ids, embed_table, req_index):
    vocab_dev = embed_table.shape[0]
    owner = ids // vocab_dev
    owners = jnp.arange(16)[:, None]
    asked = jnp.sum((owner[:, None, :] == owners[None]).astype(jnp.int32), -1)
    crowded = jnp.max(asked) > SLOTS

    def dense():
        relative = (ids - req_index * vocab_dev).reshape(-1)
        here = (relative >= 0) & (relative < vocab_dev)
        looked = jnp.take(embed_table, jnp.clip(relative, 0, vocab_dev - 1), axis=0)
        looked = jnp.where(here[:, None], looked, jnp.zeros((), jnp.bfloat16))
        looked = lax.all_to_all(
            looked.reshape(16, -1, looked.shape[1]), "req", split_axis=0, concat_axis=0, tiled=True
        )
        summed = jnp.sum(looked.astype(jnp.float32), 0).astype(jnp.bfloat16)
        summed = summed.reshape(16, -1, summed.shape[1])
        mine = lax.all_to_all(summed, "blk", split_axis=0, concat_axis=0, tiled=True)
        return jnp.transpose(mine, (1, 0, 2)).reshape(quick.shape)

    return lax.cond(crowded, dense, lambda: quick)


def attend_kernel(groups, lengths, qkv, cache, out, *, span):
    length = lengths[pl.program_id(0)]
    q, own_block = qkv[0, :, 0:128], qkv[0, :, 128:256]
    f32 = jnp.float32

    def scores_of(keys):
        return lax.dot_general(q, keys, (((1,), (1,)), ((), ())), preferred_element_type=f32)

    def weigh(weights, values):
        return jnp.dot(weights.astype(jnp.bfloat16), values, preferred_element_type=f32)

    scores = scores_of(own_block)
    top = jnp.max(scores, -1, keepdims=True)
    weights = jnp.exp(scores - top)
    total = jnp.sum(weights, -1, keepdims=True)
    mixed = weigh(weights, own_block)
    for start in range(0, cache.shape[1], span):
        block = cache[0, start : start + span, :]
        position = start + lax.broadcasted_iota(jnp.int32, (1, span), 1)
        scores = scores_of(block) + jnp.where(position < length, 0.0, NEG).astype(f32)
        raised = jnp.maximum(top, jnp.max(scores, -1, keepdims=True))
        shrink = jnp.exp(top - raised)
        weights = jnp.exp(scores - raised)
        total = total * shrink + jnp.sum(weights, -1, keepdims=True)
        mixed = mixed * shrink + weigh(weights, block)
        top = raised
    head = mixed / total
    parity = lax.axis_index("blk") % 2
    lane = lax.broadcasted_iota(jnp.int32, (1, 128), 1)
    moved = jnp.where(parity == 0, pltpu.roll(head, 64, 1), head)
    out[0] = jnp.where(lane // 64 == parity, moved, 0.0).astype(out.dtype)


def attend(qkv, cache, groups, lengths):
    requests, rows, width = qkv.shape
    size = cache.shape[1]
    return pl.pallas_call(
        functools.partial(attend_kernel, span=min(2048, size)),
        out_shape=jax.ShapeDtypeStruct((requests, rows, 128), jnp.bfloat16),
        grid_spec=pltpu.PrefetchScalarGridSpec(
            num_scalar_prefetch=2,
            grid=(requests,),
            in_specs=[
                pl.BlockSpec((1, rows, width), lambda r, g, n: (r, 0, 0)),
                pl.BlockSpec((1, size, 128), lambda r, g, n: (g[r], 0, 0)),
            ],
            out_specs=pl.BlockSpec((1, rows, 128), lambda r, g, n: (r, 0, 0)),
        ),
        compiler_params=pltpu.CompilerParams(vmem_limit_bytes=58 << 20),
        cost_estimate=busy(11),
        name="attend",
    )(groups, lengths, qkv, cache)


def shards(
    tokens, cache_kv, w_qkv, w_out, w_fc, w_proj, embed_table, group_ids, cache_len, accept, new_ids
):
    req_index = lax.axis_index("req")
    blk_index = lax.axis_index("blk")
    z, x = blk_index // 2, blk_index % 2
    requests, rows, width = tokens.shape
    kv_width = cache_kv.shape[3]
    head_dim = kv_width // 2
    share = rows // 8
    my_groups = lax.dynamic_slice_in_dim(group_ids, req_index * requests, requests)
    lengths = jnp.take(cache_len, my_groups)
    w_own = jnp.transpose(w_qkv[:, 0, :])
    w_mlp = jnp.stack([jnp.transpose(w_fc), w_proj])
    ids = asked_rows(new_ids)
    every_cache, w_out_all, w_mlp_pair, w_other, fresh, current, qkv = start_gathers(
        cache_kv[:, :, 0, :],
        w_out.reshape(2, head_dim // 2, width),
        ids,
        jnp.transpose(embed_table),
        jnp.transpose(tokens, (0, 2, 1)),
        w_own,
        w_mlp,
        1,
    )
    w_out_all = w_out_all.reshape(16 * head_dim, width)
    every_cache = every_cache.reshape(cache_kv.shape[0], -1, kv_width)
    my_accept = lax.dynamic_index_in_dim(accept, x, 1, keepdims=False)
    my_accept = lax.dynamic_slice_in_dim(my_accept, z * share, share, 1)[..., None]
    fresh = settle_fresh(fresh, ids, embed_table, req_index).reshape(PASSES, share, width)
    for pass_index in range(PASSES):
        last = pass_index == PASSES - 1
        done = run_pass(
            attend(qkv, every_cache, my_groups, lengths),
            current,
            w_out_all,
            w_mlp,
            w_mlp_pair,
            fresh[pass_index],
            my_accept[pass_index],
            None if last else (w_own, w_other),
            2 + pass_index,
        )
        if last:
            return done[0].reshape(requests, rows, width)
        current, qkv = done[0].reshape(rows, width), done[1]


def solution(mesh):
    return jax.shard_map(
        shards,
        mesh=mesh,
        in_specs=(
            P("req", None, None),
            P(None, "req", "blk", None),
            P(None, "blk", None),
            P("blk", None, None),
            P(None, "blk"),
            P("blk", None),
            P("req", "blk"),
            P(),
            P(),
            P(None, "req", None),
            P(),
        ),
        out_specs=P("req", None, None),
        check_vma=False,
    )
```

```python
import functools

import jax
import jax.numpy as jnp
from jax import lax
from jax.experimental import pallas as pl
from jax.experimental.pallas import tpu as pltpu
from jax.sharding import PartitionSpec as P

PASSES = 2
MESH = pl.DeviceIdType.MESH
NEG = -1e30


def layer_norm(values):
    centre = values - jnp.mean(values, -1, keepdims=True)
    spread = jnp.mean(centre * centre, -1, keepdims=True)
    return centre * lax.rsqrt(spread + 1e-05)


class Net:
    def __init__(self):
        self.blk = lax.axis_index("blk")
        self.z = self.blk // 2
        self.x = self.blk % 2
        self.right = self.ring(1) * 2 + self.x
        self.left = self.ring(-1) * 2 + self.x
        self.pair = self.z * 2 + 1 - self.x
        self.started = []

    def ring(self, offset):
        return lax.rem(self.z + 8 + offset, 8)

    def greet(self, axis="blk", others=None):
        barrier = pltpu.get_barrier_semaphore()
        others = (self.right, self.left, self.pair) if others is None else others
        for other in others:
            pl.semaphore_signal(barrier, inc=1, device_id={axis: other}, device_id_type=MESH)
        pl.semaphore_wait(barrier, len(others))

    def copy_of(self, src, dst, sems, slot, other, axis):
        return pltpu.make_async_remote_copy(
            src_ref=src,
            dst_ref=dst,
            send_sem=sems[0].at[slot],
            recv_sem=sems[1].at[slot],
            device_id={axis: other},
            device_id_type=MESH,
        )

    def send(self, src, dst, sems, slot, other, axis="blk"):
        copy = self.copy_of(src, dst, sems, slot, other, axis)
        copy.start()
        self.started.append(copy)

    def arrived(self, dst, sems, slot):
        self.copy_of(dst, dst, sems, slot, self.pair, "blk").wait_recv()

    def finish(self):
        for copy in self.started:
            copy.wait_send()


def busy(us):
    return pl.CostEstimate(flops=us * 400_000_000, bytes_accessed=us * 3_000_000, transcendentals=0)


def sem_pair(count):
    return [pltpu.SemaphoreType.DMA((count,)), pltpu.SemaphoreType.DMA((count,))]


def whole(count):
    return [pl.BlockSpec(memory_space=pltpu.VMEM)] * count


RING_A, RING_B, RING_C, RING_D = 0, 4, 7, 10
RING_SLOTS = 14


def ring_begin(net, out, sems, half, high):
    piece = out.at[net.z, half : 2 * half] if high else out.at[net.z, 0:half]
    net.send(piece, piece, sems, RING_B if high else RING_A, net.right)
    net.send(piece, piece, sems, RING_D if high else RING_C, net.left)


def ring_rest(net, out, sems, half):
    def take(offset, high, slot, last, target):
        at = net.ring(offset)
        piece = out.at[at, half : 2 * half] if high else out.at[at, 0:half]
        net.arrived(piece, sems, slot)
        if not last:
            net.send(piece, piece, sems, slot + 1, target)

    for step in range(1, 5):
        take(-step, False, RING_A + step - 1, step == 4, net.right)
        take(step, True, RING_D + step - 1, step == 4, net.left)
        if step < 4:
            take(-step, True, RING_B + step - 1, step == 3, net.right)
            take(step, False, RING_C + step - 1, step == 3, net.left)


def swap_heads(net, heads, peer, out, ring_sems, pair_sems):
    half = heads.shape[1] // 2
    parts = (slice(0, half), slice(half, 2 * half))
    for part, rows in enumerate(parts):
        net.send(heads.at[1 - net.x, rows], peer.at[rows], pair_sems, part, net.pair)
    for part, rows in enumerate(parts):
        net.arrived(peer.at[rows], pair_sems, part)
        out[net.z, rows] = heads[net.x, rows] + peer[rows]
        ring_begin(net, out, ring_sems, half, part == 1)
    ring_rest(net, out, ring_sems, half)


def mlp(every_head, current, w_out, w_fc, w_proj, w_mlp_pair, head_rows, middle):
    f32, bf16 = jnp.float32, jnp.bfloat16
    for z in range(8):
        head_rows[:, 128 * z : 128 * (z + 1)] = every_head[z]
    middle[...] = current[...].astype(f32) + jnp.dot(
        head_rows[...], w_out[...], preferred_element_type=f32
    )
    normed = layer_norm(middle[...]).astype(bf16)

    def term(enter, leave):
        raw = lax.dot_general(normed, enter, (((1,), (1,)), ((), ())), preferred_element_type=f32)
        rows = jax.nn.gelu(raw, approximate=True).astype(bf16)
        return jnp.dot(rows, leave, preferred_element_type=f32)

    return (term(w_fc[...], w_proj[...]) + term(w_mlp_pair[0], w_mlp_pair[1])).astype(bf16)


def project(normed, weights):
    f32, bf16 = jnp.float32, jnp.bfloat16
    got = lax.dot_general(normed, weights, (((1,), (1,)), ((), ())), preferred_element_type=f32)
    got = jnp.concatenate([got, jnp.zeros((got.shape[0], 64), f32)], 1)
    lane = lax.broadcasted_iota(jnp.int32, (1, 128), 1)
    queries = jnp.where(lane < 64, got[:, 0:128].astype(bf16).astype(f32) * 0.125, 0.0)
    return jnp.concatenate([queries, pltpu.roll(got, 192, 1)[:, 0:128]], 1).astype(bf16)


def pass_kernel(heads, fresh, accept, current_in, *refs, last):
    net = Net()
    current_in = current_in.at[net.x] if len(current_in.shape) == 3 else current_in
    loads = 5 if last else 7
    sources, refs = (current_in,) + tuple(refs[0 : loads - 1]), refs[loads - 1 :]
    if last:
        out, *refs = refs
    else:
        out, qkv, stage, *refs = refs
    held, refs = refs[0:loads], refs[loads:]
    load_sems, peer, every_head, head_rows, middle_all, part, *refs = refs
    right_low, right_high, left_low, left_high, *sem_refs = refs
    copies = [
        pltpu.make_async_copy(source, place, load_sems.at[index])
        for index, (source, place) in enumerate(zip(sources, held))
    ]
    current, w_out, w_fc, w_proj, w_mlp_pair = held[0:5]
    sems, gather_sems, head_sems, pair_sems, swap_sems = (
        tuple(sem_refs[index : index + 2]) for index in range(0, 10, 2)
    )
    half = part.shape[1] // 2
    f32, bf16 = jnp.float32, jnp.bfloat16
    low, high = slice(0, half), slice(half, 2 * half)
    for copy in copies:
        copy.start()
    net.greet()
    swap_heads(net, heads, peer, every_head, head_sems, pair_sems)
    for copy in copies:
        copy.wait()
    grown = mlp(every_head, current, w_out, w_fc, w_proj, w_mlp_pair, head_rows, middle_all)
    part[...] = grown.reshape(part.shape)

    def begin(buf, rows, slot, offset, target):
        net.send(part.at[net.ring(offset), rows], buf.at[0], sems, slot, target)

    def hand_on(buf, rows, slot, step, offset, target):
        piece = buf.at[step]
        net.arrived(piece, sems, slot + step)
        total = piece[...].astype(f32) + part[net.ring(offset), rows].astype(f32)
        buf[step] = total.astype(bf16)
        net.send(piece, buf.at[step + 1], sems, slot + step + 1, target)

    begin(right_low, low, RING_A, 4, net.right)
    begin(left_high, high, RING_D, -4, net.left)
    begin(right_high, high, RING_B, 3, net.right)
    begin(left_low, low, RING_C, -3, net.left)
    for step in range(3):
        hand_on(right_low, low, RING_A, step, 3 - step, net.right)
        hand_on(left_high, high, RING_D, step, step - 3, net.left)
        if step < 2:
            hand_on(right_high, high, RING_B, step, 2 - step, net.right)
            hand_on(left_low, low, RING_C, step, step - 2, net.left)

    def close(rows, from_left, from_right):
        total = part[net.z, rows].astype(f32) + from_left.astype(f32) + from_right.astype(f32)
        start = pl.multiple_of(net.z * 2 * half + rows.start, half)
        layer_out = (middle_all[pl.ds(start, half), :] + total).astype(bf16)
        return jnp.where(accept[rows] == 1, fresh[rows], layer_out)

    net.arrived(left_low.at[2], sems, RING_C + 2)
    net.arrived(right_low.at[3], sems, RING_A + 3)
    result = close(low, right_low[3], left_low[2])
    if last:
        out[net.x, net.z, low] = result
        gather_begin_low(net, out, gather_sems, half)
    else:
        out[net.z, low] = result
        ring_begin(net, out, gather_sems, half, False)
    net.arrived(right_high.at[2], sems, RING_B + 2)
    net.arrived(left_high.at[3], sems, RING_D + 3)
    result = close(high, right_high[2], left_high[3])
    if last:
        out[net.x, net.z, high] = result
        gather_begin_high(net, out, gather_sems, half)
        gather_rest(net, out, gather_sems, half)
    else:
        out[net.z, high] = result
        ring_begin(net, out, gather_sems, half, True)
        ring_rest(net, out, gather_sems, half)
        rows_f32 = out[...].reshape(8 * 2 * half, out.shape[2]).astype(f32)
        w_own, w_pair = held[5:7]
        normed = layer_norm(rows_f32).astype(bf16)
        stage[...] = project(normed, w_pair[...])
        net.send(stage, qkv.at[net.x], swap_sems, 0, net.pair)
        qkv[net.x] = project(normed, w_own[...])
        net.arrived(qkv.at[1 - net.x], swap_sems, 0)
    net.finish()


def run_pass(
    heads, current, w_out, w_fc, w_proj, w_mlp_pair, fresh, accept, w_qkv_both, collective_id
):
    rows, width = current.shape[-2:]
    lanes, share = heads.shape[2], rows // 8
    bf16 = jnp.bfloat16
    last = w_qkv_both is None
    block = (share // 2, width)
    operands = (heads, fresh, accept, current, w_out, w_fc, w_proj, w_mlp_pair)
    if last:
        shapes = (jax.ShapeDtypeStruct((2, 8, share, width), bf16),)
        first, gather = [], GATHER_SLOTS
    else:
        operands = operands + w_qkv_both
        shapes = (
            jax.ShapeDtypeStruct((8, share, width), bf16),
            jax.ShapeDtypeStruct((2, rows, 256), bf16),
        )
        first, gather = [pltpu.VMEM((rows, 256), bf16)], RING_SLOTS
    held = [pltpu.VMEM(array.shape[-2:] if array is current else array.shape, bf16) for array in operands[3:]]
    scratch = first + held + [pltpu.SemaphoreType.DMA((len(held),))] + [
        pltpu.VMEM((rows, lanes), bf16),
        pltpu.VMEM((8, rows, lanes), bf16),
        pltpu.VMEM((rows, 8 * lanes), bf16),
        pltpu.VMEM((rows, width), jnp.float32),
        pltpu.VMEM((8, share, width), bf16),
    ]
    rings = [pltpu.VMEM((count,) + block, bf16) for count in (4, 3, 3, 4)]
    sems = []
    for count in (RING_SLOTS, gather, RING_SLOTS, 2, 1):
        sems = sems + sem_pair(count)
    return pl.pallas_call(
        functools.partial(pass_kernel, last=last),
        out_shape=shapes,
        in_specs=whole(3) + [pl.BlockSpec(memory_space=pl.ANY)] * len(held),
        out_specs=tuple(whole(len(shapes))),
        scratch_shapes=scratch + rings + sems,
        compiler_params=pltpu.CompilerParams(
            collective_id=collective_id, has_side_effects=True, vmem_limit_bytes=56 << 20
        ),
        cost_estimate=busy(50),
        name=f"pass_{collective_id}",
    )(*operands)


R_A, R_B, R_O, L_A, L_B, L_O, X_A, X_B = 0, 4, 8, 12, 16, 20, 24, 25
GATHER_SLOTS = 33


def gather_begin_low(net, out, sems, half):
    low = out.at[net.x, net.z, 0:half]
    net.send(low, low, sems, R_A + 0, net.right)
    net.send(low, low, sems, L_A + 0, net.left)
    net.send(low, low, sems, X_A, net.pair)


def gather_begin_high(net, out, sems, half):
    high = out.at[net.x, net.z, half : 2 * half]
    net.send(high, high, sems, R_B + 0, net.right)
    net.send(high, high, sems, L_B + 0, net.left)
    net.send(high, high, sems, X_B + 0, net.pair)


def gather_rest(net, out, sems, half):
    other = 1 - net.x
    peer_low = out.at[other, net.z, 0:half]
    net.arrived(peer_low, sems, X_A)
    net.send(peer_low, peer_low, sems, R_O + 0, net.right)
    net.send(peer_low, peer_low, sems, L_O + 0, net.left)
    for step in range(1, 5):
        before, after = net.ring(-step), net.ring(step)
        piece = out.at[net.x, before, 0:half]
        net.arrived(piece, sems, R_A + step - 1)
        if step < 4:
            net.send(piece, piece, sems, R_A + step, net.right)
        piece = out.at[net.x, after, half : 2 * half]
        net.arrived(piece, sems, L_B + step - 1)
        if step < 4:
            net.send(piece, piece, sems, L_B + step, net.left)
        net.send(piece, piece, sems, X_B + (step if step < 4 else 7), net.pair)
        piece = out.at[other, after, 0:half]
        net.arrived(piece, sems, L_O + step - 1)
        if step < 4:
            net.send(piece, piece, sems, L_O + step, net.left)
        if step < 4:
            piece = out.at[net.x, after, 0:half]
            net.arrived(piece, sems, L_A + step - 1)
            if step < 3:
                net.send(piece, piece, sems, L_A + step, net.left)
            piece = out.at[net.x, before, half : 2 * half]
            net.arrived(piece, sems, R_B + step - 1)
            if step < 3:
                net.send(piece, piece, sems, R_B + step, net.right)
            net.send(piece, piece, sems, X_B + 3 + step, net.pair)
            piece = out.at[other, before, 0:half]
            net.arrived(piece, sems, R_O + step - 1)
            if step < 3:
                net.send(piece, piece, sems, R_O + step, net.right)
    for slot, offset in ((0, 0), (1, 1), (2, 2), (3, 3), (7, 4), (4, -1), (5, -2), (6, -3)):
        net.arrived(out.at[other, net.ring(offset), half : 2 * half], sems, X_B + slot)


PIECES = (0, 2, 1, 3)


SLOTS = 128


def start_kernel(
    own, w_own, ids, raw_table, tokens_in, w_qkv_in, w_fc, w_proj, out, w_all, w_mlp_pair, w_qkv_pair, fresh, rows_out,
    qkv, tokens, w_qkv, table, ranks, relatives, sent, got, picked, mine, copy_sems,
    send_sems, recv_sems, send_w, recv_w, send_f, recv_f, send_g, recv_g, send_m, recv_m,
):
    net = Net()
    f32, bf16 = jnp.float32, jnp.bfloat16
    me = lax.axis_index("req")
    y, x, core = me // 4, (me // 2) % 2, me % 2

    def device(step, other_x, other_core=False):
        return (
            lax.rem(y + 4 + step, 4) * 4
            + (1 - x if other_x else x) * 2
            + (1 - core if other_core else core)
        )

    up, down, side, twin = device(1, 0), device(-1, 0), device(0, 1), device(0, 0, True)
    barrier = pltpu.get_barrier_semaphore()
    for step in range(1, 16):
        other = lax.rem(me + step, 16)
        pl.semaphore_signal(barrier, inc=1, device_id={"req": other}, device_id_type=MESH)
    for step in range(1, 16):
        other = lax.rem(net.blk + step, 16)
        pl.semaphore_signal(barrier, inc=1, device_id={"blk": other}, device_id_type=MESH)
    cross = {"req": side, "blk": net.pair}
    pl.semaphore_signal(barrier, inc=1, device_id=cross, device_id_type=MESH)
    pl.semaphore_wait(barrier, 31)
    w_sems, f_sems, g_sems, m_sems = (send_w, recv_w), (send_f, recv_f), (send_g, recv_g), (send_m, recv_m)
    columns, vocab_dev = raw_table.shape
    started = []

    def copy_of(src, dst, slot, other):
        return pltpu.make_async_remote_copy(
            src_ref=src,
            dst_ref=dst,
            send_sem=send_sems.at[slot],
            recv_sem=recv_sems.at[slot],
            device_id={"req": other},
            device_id_type=MESH,
        )

    def send(src, dst, slot, other):
        copy = copy_of(src, dst, slot, other)
        copy.start()
        started.append(copy)

    def arrived(dst, slot):
        copy_of(dst, dst, slot, twin).wait_recv()

    U0, D0, SIDE, U1, D1, UF0, UF1, DF0, DF1, TWIN = 0, 4, 8, 12, 16, 20, 22, 24, 26, 28
    places = {(0, 0): 0, (0, 1): 1, (-1, 0): 2, (1, 0): 3, (-1, 1): 4, (1, 1): 5, (2, 0): 6, (2, 1): 7}

    def share(step, other_x, g):
        piece = out.at[g, device(step, other_x)]
        send(piece, piece, TWIN + 4 * places[(step, other_x)] + g, twin)

    for g in PIECES:
        dst = out.at[g, me]
        send(own.at[g], dst, U0 + g, up)
        send(own.at[g], dst, D0 + g, down)
        send(own.at[g], dst, SIDE + g, side)
    RO, LO, RQ, LQ, PX, TW = 0, 4, 7, 10, 14, 15

    def w_piece(offset, parity, half):
        return w_all.at[net.ring(offset), parity, half]

    def w_twin(offset, parity, slot):
        piece = w_piece(offset, parity, core)
        net.send(piece, piece, w_sems, TW + slot, twin, "req")

    w_half, w_mine = w_own.at[core], w_piece(0, net.x, core)
    net.send(w_half, w_mine, w_sems, PX, net.pair)
    net.send(w_half, w_mine, w_sems, RO, net.right)
    net.send(w_half, w_mine, w_sems, LO, net.left)
    net.send(w_half, w_mine, w_sems, TW, twin, "req")
    keeps = [
        pltpu.make_async_copy(own, out.at[:, me], copy_sems.at[0]),
        pltpu.make_async_copy(w_half, w_mine, copy_sems.at[1]),
    ]
    loads = [
        pltpu.make_async_copy(tokens_in, tokens, copy_sems.at[2]),
        pltpu.make_async_copy(w_qkv_in, w_qkv, copy_sems.at[3]),
    ]
    for copy in keeps + loads:
        copy.start()

    units, half_qkv = w_fc.shape[0] // 5, w_qkv_pair.shape[0] // 2

    def pair_pieces(which):
        pieces = [w_mlp_pair.at[which, pl.ds(index * units, units)] for index in range(5)]
        rows = pl.ds(pl.multiple_of(which * half_qkv, half_qkv), half_qkv)
        return pieces + [w_qkv_pair.at[rows]]

    def pair_send():
        def copy_from(src, dst, slot):
            return pltpu.make_async_remote_copy(
                src_ref=src,
                dst_ref=dst,
                send_sem=m_sems[0].at[slot],
                recv_sem=m_sems[1].at[slot],
                device_id={"blk": net.pair} if slot < 3 else cross,
                device_id_type=MESH,
            )

        for slot in range(5):
            rows = pl.ds(slot * units, units)
            for which, weights in enumerate((w_fc, w_proj)):
                copy = copy_from(weights.at[rows], w_mlp_pair.at[which, rows], slot)
                pl.when(core == which)(copy.start)
            started.append(copy)
        rows = pl.ds(pl.multiple_of(core * half_qkv, half_qkv), half_qkv)
        copy = copy_from(w_qkv_in.at[rows], w_qkv_pair.at[rows], 5)
        copy.start()
        started.append(copy)

    def pair_share():
        for slot, dst in enumerate(pair_pieces(core)):
            net.arrived(dst, m_sems, slot)
            net.send(dst, dst, m_sems, 6 + slot, twin, "req")

    def pair_end():
        for slot, dst in enumerate(pair_pieces(1 - core)):
            net.arrived(dst, m_sems, 6 + slot)

    def w_begin():
        piece = w_piece(0, 1 - net.x, core)
        net.arrived(piece, w_sems, PX)
        net.send(piece, piece, w_sems, RQ, net.right)
        net.send(piece, piece, w_sems, LQ, net.left)
        w_twin(0, 1 - net.x, 8)

    def w_step(step):
        for parity, slot_r, slot_l, last_r, last_l, twin_slot in (
            (net.x, RO, LO, 4, 3, 0), (1 - net.x, RQ, LQ, 3, 4, 8)
        ):
            if step < last_r:
                piece = w_piece(-1 - step, parity, core)
                net.arrived(piece, w_sems, slot_r + step)
                if step < last_r - 1:
                    net.send(piece, piece, w_sems, slot_r + step + 1, net.right)
                w_twin(-1 - step, parity, twin_slot + (7 - step))
            if step < last_l:
                piece = w_piece(1 + step, parity, core)
                net.arrived(piece, w_sems, slot_l + step)
                if step < last_l - 1:
                    net.send(piece, piece, w_sems, slot_l + step + 1, net.left)
                w_twin(1 + step, parity, twin_slot + 1 + step)

    def w_end():
        for twin_slot, parity in ((0, net.x), (8, 1 - net.x)):
            for offset in range(8):
                net.arrived(w_piece(offset, parity, 1 - core), w_sems, TW + twin_slot + offset)

    count = ids.shape[1]

    def within(values, owner):
        offset = values - owner * vocab_dev
        return (offset >= 0) & (offset < vocab_dev), offset

    table[...] = jnp.zeros_like(table)
    table[0:columns, 0:vocab_dev] = raw_table[...]
    inside, offset = within(ids[...], me)
    owners = lax.broadcasted_iota(jnp.int32, (16, 1), 0)
    theirs, _ = within(ids[pl.ds(me, 1), :], owners)
    both = jnp.concatenate([jnp.where(inside, 1.0, 0.0), jnp.where(theirs, 1.0, 0.0)], 0)
    earlier = lax.broadcasted_iota(jnp.int32, (count, count), 0) < lax.broadcasted_iota(
        jnp.int32, (count, count), 1
    )
    rank = jnp.dot(
        both.astype(bf16), jnp.where(earlier, 1.0, 0.0).astype(bf16), preferred_element_type=f32
    )
    ranks[...] = jnp.where(inside, rank[0:16], -1.0)
    relatives[...] = offset.astype(f32)
    slot_of = jnp.where(theirs, rank[16:32] + owners.astype(f32) * SLOTS, 0.0)
    place_row = jnp.sum(slot_of, 0, keepdims=True)

    def pick(chunk, _):
        slots = lax.broadcasted_iota(jnp.int32, (SLOTS, 1), 0).astype(f32)
        wanted = []
        for step in range(4):
            other = pl.ds(lax.rem(me + 4 * chunk + step, 16), 1)
            chosen = ranks[other, :] == slots
            wanted.append(jnp.sum(jnp.where(chosen, relatives[other, :], 0.0), 1, keepdims=True))
        wanted = jnp.concatenate(wanted, 0).astype(jnp.int32)
        row = lax.broadcasted_iota(jnp.int32, (1, table.shape[1]), 1)
        one_hot = jnp.where(wanted == row, 1.0, 0.0).astype(bf16)
        rows = lax.dot_general(
            one_hot, table[...], (((1,), (1,)), ((), ())), preferred_element_type=f32
        ).astype(bf16)
        sent[pl.ds(4 * chunk, 4)] = rows.reshape(4, SLOTS, rows.shape[1])
        return 0

    def send_picked():
        got[me] = sent[0]
        for step in range(1, 16):
            other = lax.rem(me + step, 16)
            net.send(sent.at[step], got.at[me], f_sems, step - 1, other, "req")

    def spread():
        for step in range(1, 16):
            net.arrived(got.at[lax.rem(me + 16 - step, 16)], f_sems, step - 1)
        place = jnp.transpose(jnp.broadcast_to(place_row, (8, count)))[:, 0:1].astype(jnp.int32)
        slot = lax.broadcasted_iota(jnp.int32, (1, 16 * SLOTS), 1)
        one_hot = jnp.where(place == slot, 1.0, 0.0).astype(bf16)
        rows = jnp.dot(
            one_hot, got[...].reshape(16 * SLOTS, got.shape[2]), preferred_element_type=f32
        )
        picked[...] = rows.astype(bf16).reshape(picked.shape)
        mine[net.blk] = picked[net.blk]
        for step in range(1, 16):
            other = lax.rem(net.blk + step, 16)
            net.send(picked.at[other], mine.at[net.blk], g_sems, step - 1, other)

    def join():
        for step in range(1, 16):
            net.arrived(mine.at[lax.rem(net.blk + 16 - step, 16)], g_sems, step - 1)
        fresh[...] = jnp.concatenate([mine[index, :, 0:columns] for index in range(16)], 1)

    def first_qkv(request, _):
        rows_f32 = jnp.transpose(tokens[request].astype(f32))
        rows_out[request] = rows_f32.astype(bf16)
        qkv[request] = project(layer_norm(rows_f32).astype(bf16), w_qkv[...])
        return 0

    lax.fori_loop(0, 4, pick, 0)
    send_picked()
    for g in PIECES:
        send(own.at[g], out.at[g, me], TWIN + g, twin)

    def from_below(g, other_x, base, forward):
        piece = out.at[g, device(-1, other_x)]
        arrived(piece, base + g)
        if g < 2:
            send(piece, piece, forward + g, up)
        share(-1, other_x, g)

    def from_above(g, other_x, base, forward):
        piece = out.at[g, device(1, other_x)]
        arrived(piece, base + g)
        if g >= 2:
            send(piece, piece, forward + g - 2, down)
        share(1, other_x, g)

    def from_far(g, other_x):
        piece = out.at[g, device(2, other_x)]
        if g < 2:
            arrived(piece, (UF1 if other_x else UF0) + g)
        else:
            arrived(piece, (DF1 if other_x else DF0) + g - 2)
        share(2, other_x, g)

    for index, g in enumerate(PIECES):
        piece = out.at[g, side]
        arrived(piece, SIDE + g)
        send(piece, piece, U1 + g, up)
        send(piece, piece, D1 + g, down)
        share(0, 1, g)
        from_below(g, 0, U0, UF0)
        from_above(g, 0, D0, DF0)
        if index == 0:
            w_begin()
        elif index == 2:
            w_step(0)
    pair_send()
    w_step(1)
    spread()
    for index, g in enumerate(PIECES):
        from_below(g, 1, U1, UF1)
        from_above(g, 1, D1, DF1)
        from_far(g, 0)
        if index == 1:
            w_step(2)
    for load in loads:
        load.wait()
    lax.fori_loop(0, 2, first_qkv, 0)
    w_step(3)
    for g in PIECES:
        from_far(g, 1)
    for (step, other_x), place in places.items():
        for g in PIECES:
            arrived(out.at[g, device(step, other_x, True)], TWIN + 4 * place + g)
    pair_share()
    join()
    w_end()
    pair_end()
    for keep in keeps:
        keep.wait()
    for copy in started:
        copy.wait_send()
    net.finish()


def start_gathers(own, w_own, ids, table, tokens, w_qkv, w_fc, w_proj, collective_id):
    groups = own.shape[0]
    count = ids.shape[1]
    columns, vocab_dev = table.shape
    requests, width, rows = tokens.shape
    bf16 = jnp.bfloat16
    blocks = pltpu.VMEM((16, SLOTS, 128), bf16)
    asked = pltpu.VMEM((16, count // 16, 128), bf16)
    anywhere = [pl.BlockSpec(memory_space=pl.ANY)]
    return pl.pallas_call(
        start_kernel,
        out_shape=(
            jax.ShapeDtypeStruct((groups, 16) + own.shape[1:], own.dtype),
            jax.ShapeDtypeStruct((8, 2) + w_own.shape, w_own.dtype),
            jax.ShapeDtypeStruct((2,) + w_fc.shape, w_fc.dtype),
            jax.ShapeDtypeStruct(w_qkv.shape, w_qkv.dtype),
            jax.ShapeDtypeStruct((count // 16, 16 * columns), bf16),
            jax.ShapeDtypeStruct((requests, rows, width), bf16),
            jax.ShapeDtypeStruct((requests, rows, 256), bf16),
        ),
        in_specs=anywhere * 2 + whole(2) + anywhere * 4,
        out_specs=tuple(anywhere * 4 + whole(3)),
        scratch_shapes=[
            pltpu.VMEM(tokens.shape, bf16),
            pltpu.VMEM(w_qkv.shape, bf16),
            pltpu.VMEM((128, -(-vocab_dev // 128) * 128), bf16),
            pltpu.VMEM((16, count), jnp.float32),
            pltpu.VMEM((16, count), jnp.float32),
            blocks,
            blocks,
            asked,
            asked,
            pltpu.SemaphoreType.DMA((4,)),
        ]
        + sem_pair(60)
        + sem_pair(31)
        + sem_pair(15)
        + sem_pair(15)
        + sem_pair(12),
        compiler_params=pltpu.CompilerParams(
            collective_id=collective_id, has_side_effects=True, vmem_limit_bytes=58 << 20
        ),
        cost_estimate=busy(45),
        name="start_gathers",
    )(own, w_own, ids, table, tokens, w_qkv, w_fc, w_proj)


def asked_rows(new_ids):
    by_device = new_ids.reshape(new_ids.shape[0], 16, 2, 8, -1)
    return jnp.transpose(by_device, (1, 3, 2, 0, 4)).reshape(16, -1)


def settle_fresh(quick, ids, embed_table, req_index):
    vocab_dev = embed_table.shape[0]
    owner = ids // vocab_dev
    owners = jnp.arange(16)[:, None]
    asked = jnp.sum((owner[:, None, :] == owners[None]).astype(jnp.int32), -1)
    crowded = jnp.max(asked) > SLOTS

    def dense():
        relative = (ids - req_index * vocab_dev).reshape(-1)
        here = (relative >= 0) & (relative < vocab_dev)
        looked = jnp.take(embed_table, jnp.clip(relative, 0, vocab_dev - 1), axis=0)
        looked = jnp.where(here[:, None], looked, jnp.zeros((), jnp.bfloat16))
        looked = lax.all_to_all(
            looked.reshape(16, -1, looked.shape[1]), "req", split_axis=0, concat_axis=0, tiled=True
        )
        summed = jnp.sum(looked.astype(jnp.float32), 0).astype(jnp.bfloat16)
        summed = summed.reshape(16, -1, summed.shape[1])
        mine = lax.all_to_all(summed, "blk", split_axis=0, concat_axis=0, tiled=True)
        return jnp.transpose(mine, (1, 0, 2)).reshape(quick.shape)

    return lax.cond(crowded, dense, lambda: quick)


def attend_kernel(groups, lengths, qkv, cache, out, *, span):
    length = lengths[pl.program_id(0)]
    q, own_block = qkv[0, :, 0:128], qkv[0, :, 128:256]
    f32 = jnp.float32

    def scores_of(keys):
        return lax.dot_general(q, keys, (((1,), (1,)), ((), ())), preferred_element_type=f32)

    def weigh(weights, values):
        return jnp.dot(weights.astype(jnp.bfloat16), values, preferred_element_type=f32)

    scores = scores_of(own_block)
    top = jnp.max(scores, -1, keepdims=True)
    weights = jnp.exp(scores - top)
    total = jnp.sum(weights, -1, keepdims=True)
    mixed = weigh(weights, own_block)
    for start in range(0, cache.shape[1], span):
        block = cache[0, start : start + span, :]
        position = start + lax.broadcasted_iota(jnp.int32, (1, span), 1)
        scores = scores_of(block) + jnp.where(position < length, 0.0, NEG).astype(f32)
        raised = jnp.maximum(top, jnp.max(scores, -1, keepdims=True))
        shrink = jnp.exp(top - raised)
        weights = jnp.exp(scores - raised)
        total = total * shrink + jnp.sum(weights, -1, keepdims=True)
        mixed = mixed * shrink + weigh(weights, block)
        top = raised
    head = mixed / total
    parity = lax.axis_index("blk") % 2
    lane = lax.broadcasted_iota(jnp.int32, (1, 128), 1)
    moved = jnp.where(parity == 0, pltpu.roll(head, 64, 1), head)
    out[0] = jnp.where(lane // 64 == parity, moved, 0.0).astype(out.dtype)


def attend(qkv, cache, groups, lengths):
    requests, rows, width = qkv.shape
    size = cache.shape[1]
    return pl.pallas_call(
        functools.partial(attend_kernel, span=min(2048, size)),
        out_shape=jax.ShapeDtypeStruct((requests, rows, 128), jnp.bfloat16),
        grid_spec=pltpu.PrefetchScalarGridSpec(
            num_scalar_prefetch=2,
            grid=(requests,),
            in_specs=[
                pl.BlockSpec((1, rows, width), lambda r, g, n: (r, 0, 0)),
                pl.BlockSpec((1, size, 128), lambda r, g, n: (g[r], 0, 0)),
            ],
            out_specs=pl.BlockSpec((1, rows, 128), lambda r, g, n: (r, 0, 0)),
        ),
        compiler_params=pltpu.CompilerParams(vmem_limit_bytes=58 << 20),
        cost_estimate=busy(11),
        name="attend",
    )(groups, lengths, qkv, cache)


def shards(
    tokens, cache_kv, w_qkv, w_out, w_fc, w_proj, embed_table, group_ids, cache_len, accept, new_ids
):
    req_index = lax.axis_index("req")
    blk_index = lax.axis_index("blk")
    z, x = blk_index // 2, blk_index % 2
    requests, rows, width = tokens.shape
    kv_width = cache_kv.shape[3]
    head_dim = kv_width // 2
    share = rows // 8
    my_groups = lax.dynamic_slice_in_dim(group_ids, req_index * requests, requests)
    lengths = jnp.take(cache_len, my_groups)
    w_own = jnp.transpose(w_qkv[:, 0, :])
    w_fc = jnp.transpose(w_fc)
    ids = asked_rows(new_ids)
    every_cache, w_out_all, w_mlp_pair, w_other, fresh, current, qkv = start_gathers(
        cache_kv[:, :, 0, :],
        w_out.reshape(2, head_dim // 2, width),
        ids,
        jnp.transpose(embed_table),
        jnp.transpose(tokens, (0, 2, 1)),
        w_own,
        w_fc,
        w_proj,
        1,
    )
    w_out_all = w_out_all.reshape(16 * head_dim, width)
    every_cache = every_cache.reshape(cache_kv.shape[0], -1, kv_width)
    my_accept = lax.dynamic_index_in_dim(accept, x, 1, keepdims=False)
    my_accept = lax.dynamic_slice_in_dim(my_accept, z * share, share, 1)[..., None]
    fresh = settle_fresh(fresh, ids, embed_table, req_index).reshape(PASSES, share, width)
    for pass_index in range(PASSES):
        last = pass_index == PASSES - 1
        done = run_pass(
            attend(qkv, every_cache, my_groups, lengths),
            current,
            w_out_all,
            w_fc,
            w_proj,
            w_mlp_pair,
            fresh[pass_index],
            my_accept[pass_index],
            None if last else (w_own, w_other),
            2 + pass_index,
        )
        if last:
            return done[0].reshape(requests, rows, width)
        current, qkv = done[0].reshape(rows, width), done[1]


def solution(mesh):
    return jax.shard_map(
        shards,
        mesh=mesh,
        in_specs=(
            P("req", None, None),
            P(None, "req", "blk", None),
            P(None, "blk", None),
            P("blk", None, None),
            P(None, "blk"),
            P("blk", None),
            P("req", "blk"),
            P(),
            P(),
            P(None, "req", None),
            P(),
        ),
        out_specs=P("req", None, None),
        check_vma=False,
    )
```

```python
import functools

import jax
import jax.numpy as jnp
from jax import lax
from jax.experimental import pallas as pl
from jax.experimental.pallas import tpu as pltpu
from jax.sharding import PartitionSpec as P

PASSES = 2
MESH = pl.DeviceIdType.MESH
NEG = -1e30


def layer_norm(values):
    centre = values - jnp.mean(values, -1, keepdims=True)
    spread = jnp.mean(centre * centre, -1, keepdims=True)
    return centre * lax.rsqrt(spread + 1e-05)


class Net:
    def __init__(self):
        self.blk = lax.axis_index("blk")
        self.z = self.blk // 2
        self.x = self.blk % 2
        self.right = self.ring(1) * 2 + self.x
        self.left = self.ring(-1) * 2 + self.x
        self.pair = self.z * 2 + 1 - self.x
        self.started = []

    def ring(self, offset):
        return lax.rem(self.z + 8 + offset, 8)

    def greet(self, axis="blk", others=None):
        barrier = pltpu.get_barrier_semaphore()
        others = (self.right, self.left, self.pair) if others is None else others
        for other in others:
            pl.semaphore_signal(barrier, inc=1, device_id={axis: other}, device_id_type=MESH)
        pl.semaphore_wait(barrier, len(others))

    def copy_of(self, src, dst, sems, slot, other, axis):
        return pltpu.make_async_remote_copy(
            src_ref=src,
            dst_ref=dst,
            send_sem=sems[0].at[slot],
            recv_sem=sems[1].at[slot],
            device_id={axis: other},
            device_id_type=MESH,
        )

    def send(self, src, dst, sems, slot, other, axis="blk"):
        copy = self.copy_of(src, dst, sems, slot, other, axis)
        copy.start()
        self.started.append(copy)

    def arrived(self, dst, sems, slot):
        self.copy_of(dst, dst, sems, slot, self.pair, "blk").wait_recv()

    def finish(self):
        for copy in self.started:
            copy.wait_send()


def busy(us):
    return pl.CostEstimate(flops=us * 400_000_000, bytes_accessed=us * 3_000_000, transcendentals=0)


def sem_pair(count):
    return [pltpu.SemaphoreType.DMA((count,)), pltpu.SemaphoreType.DMA((count,))]


def whole(count):
    return [pl.BlockSpec(memory_space=pltpu.VMEM)] * count


RING_A, RING_B, RING_C, RING_D = 0, 4, 7, 10
RING_SLOTS = 14


def ring_begin(net, out, sems, half, high):
    piece = out.at[net.z, half : 2 * half] if high else out.at[net.z, 0:half]
    net.send(piece, piece, sems, RING_B if high else RING_A, net.right)
    net.send(piece, piece, sems, RING_D if high else RING_C, net.left)


def ring_rest(net, out, sems, half):
    def take(offset, high, slot, last, target):
        at = net.ring(offset)
        piece = out.at[at, half : 2 * half] if high else out.at[at, 0:half]
        net.arrived(piece, sems, slot)
        if not last:
            net.send(piece, piece, sems, slot + 1, target)

    for step in range(1, 5):
        take(-step, False, RING_A + step - 1, step == 4, net.right)
        take(step, True, RING_D + step - 1, step == 4, net.left)
        if step < 4:
            take(-step, True, RING_B + step - 1, step == 3, net.right)
            take(step, False, RING_C + step - 1, step == 3, net.left)


def swap_heads(net, heads, peer, out, ring_sems, pair_sems):
    half = heads.shape[1] // 2
    parts = (slice(0, half), slice(half, 2 * half))
    for part, rows in enumerate(parts):
        net.send(heads.at[1 - net.x, rows], peer.at[rows], pair_sems, part, net.pair)
    for part, rows in enumerate(parts):
        net.arrived(peer.at[rows], pair_sems, part)
        out[net.z, rows] = heads[net.x, rows] + peer[rows]
        ring_begin(net, out, ring_sems, half, part == 1)
    ring_rest(net, out, ring_sems, half)


def mlp(every_head, current, w_out, w_fc, w_proj, w_mlp_pair, head_rows, middle):
    f32, bf16 = jnp.float32, jnp.bfloat16
    for z in range(8):
        head_rows[:, 128 * z : 128 * (z + 1)] = every_head[z]
    middle[...] = current[...].astype(f32) + jnp.dot(
        head_rows[...], w_out[...], preferred_element_type=f32
    )
    normed = layer_norm(middle[...]).astype(bf16)

    def term(enter, leave):
        raw = lax.dot_general(normed, enter, (((1,), (1,)), ((), ())), preferred_element_type=f32)
        rows = jax.nn.gelu(raw, approximate=True).astype(bf16)
        return jnp.dot(rows, leave, preferred_element_type=f32)

    return (term(w_fc[...], w_proj[...]) + term(w_mlp_pair[0], w_mlp_pair[1])).astype(bf16)


def project(normed, weights):
    f32, bf16 = jnp.float32, jnp.bfloat16
    got = lax.dot_general(normed, weights, (((1,), (1,)), ((), ())), preferred_element_type=f32)
    got = jnp.concatenate([got, jnp.zeros((got.shape[0], 64), f32)], 1)
    lane = lax.broadcasted_iota(jnp.int32, (1, 128), 1)
    queries = jnp.where(lane < 64, got[:, 0:128].astype(bf16).astype(f32) * 0.125, 0.0)
    return jnp.concatenate([queries, pltpu.roll(got, 192, 1)[:, 0:128]], 1).astype(bf16)


def pass_kernel(heads, fresh, accept, current_in, *refs, last):
    net = Net()
    current_in = current_in.at[net.x] if len(current_in.shape) == 3 else current_in
    loads = 5 if last else 7
    sources, refs = (current_in,) + tuple(refs[0 : loads - 1]), refs[loads - 1 :]
    if last:
        out, *refs = refs
    else:
        out, qkv, stage, *refs = refs
    held, refs = refs[0:loads], refs[loads:]
    load_sems, peer, every_head, head_rows, middle_all, part, *refs = refs
    right_low, right_high, left_low, left_high, *sem_refs = refs
    copies = [
        pltpu.make_async_copy(source, place, load_sems.at[index])
        for index, (source, place) in enumerate(zip(sources, held))
    ]
    current, w_out, w_fc, w_proj, w_mlp_pair = held[0:5]
    sems, gather_sems, head_sems, pair_sems, swap_sems = (
        tuple(sem_refs[index : index + 2]) for index in range(0, 10, 2)
    )
    half = part.shape[1] // 2
    f32, bf16 = jnp.float32, jnp.bfloat16
    low, high = slice(0, half), slice(half, 2 * half)
    for copy in copies:
        copy.start()
    net.greet()
    swap_heads(net, heads, peer, every_head, head_sems, pair_sems)
    for copy in copies:
        copy.wait()
    grown = mlp(every_head, current, w_out, w_fc, w_proj, w_mlp_pair, head_rows, middle_all)
    part[...] = grown.reshape(part.shape)

    def begin(buf, rows, slot, offset, target):
        net.send(part.at[net.ring(offset), rows], buf.at[0], sems, slot, target)

    def hand_on(buf, rows, slot, step, offset, target):
        piece = buf.at[step]
        net.arrived(piece, sems, slot + step)
        total = piece[...].astype(f32) + part[net.ring(offset), rows].astype(f32)
        buf[step] = total.astype(bf16)
        net.send(piece, buf.at[step + 1], sems, slot + step + 1, target)

    begin(right_low, low, RING_A, 4, net.right)
    begin(left_high, high, RING_D, -4, net.left)
    begin(right_high, high, RING_B, 3, net.right)
    begin(left_low, low, RING_C, -3, net.left)
    for step in range(3):
        hand_on(right_low, low, RING_A, step, 3 - step, net.right)
        hand_on(left_high, high, RING_D, step, step - 3, net.left)
        if step < 2:
            hand_on(right_high, high, RING_B, step, 2 - step, net.right)
            hand_on(left_low, low, RING_C, step, step - 2, net.left)

    def close(rows, from_left, from_right):
        total = part[net.z, rows].astype(f32) + from_left.astype(f32) + from_right.astype(f32)
        start = pl.multiple_of(net.z * 2 * half + rows.start, half)
        layer_out = (middle_all[pl.ds(start, half), :] + total).astype(bf16)
        return jnp.where(accept[rows] == 1, fresh[rows], layer_out)

    net.arrived(left_low.at[2], sems, RING_C + 2)
    net.arrived(right_low.at[3], sems, RING_A + 3)
    result = close(low, right_low[3], left_low[2])
    if last:
        out[net.x, net.z, low] = result
        gather_begin_low(net, out, gather_sems, half)
    else:
        out[net.z, low] = result
        ring_begin(net, out, gather_sems, half, False)
    net.arrived(right_high.at[2], sems, RING_B + 2)
    net.arrived(left_high.at[3], sems, RING_D + 3)
    result = close(high, right_high[2], left_high[3])
    if last:
        out[net.x, net.z, high] = result
        gather_begin_high(net, out, gather_sems, half)
        gather_rest(net, out, gather_sems, half)
    else:
        out[net.z, high] = result
        ring_begin(net, out, gather_sems, half, True)
        ring_rest(net, out, gather_sems, half)
        rows_f32 = out[...].reshape(8 * 2 * half, out.shape[2]).astype(f32)
        w_own, w_pair = held[5:7]
        normed = layer_norm(rows_f32).astype(bf16)
        stage[...] = project(normed, w_pair[...])
        net.send(stage, qkv.at[net.x], swap_sems, 0, net.pair)
        qkv[net.x] = project(normed, w_own[...])
        net.arrived(qkv.at[1 - net.x], swap_sems, 0)
    net.finish()


def run_pass(
    heads, current, w_out, w_fc, w_proj, w_mlp_pair, fresh, accept, w_qkv_both, collective_id
):
    rows, width = current.shape[-2:]
    lanes, share = heads.shape[2], rows // 8
    bf16 = jnp.bfloat16
    last = w_qkv_both is None
    block = (share // 2, width)
    operands = (heads, fresh, accept, current, w_out, w_fc, w_proj, w_mlp_pair)
    if last:
        shapes = (jax.ShapeDtypeStruct((2, 8, share, width), bf16),)
        first, gather = [], GATHER_SLOTS
    else:
        operands = operands + w_qkv_both
        shapes = (
            jax.ShapeDtypeStruct((8, share, width), bf16),
            jax.ShapeDtypeStruct((2, rows, 256), bf16),
        )
        first, gather = [pltpu.VMEM((rows, 256), bf16)], RING_SLOTS
    held = [pltpu.VMEM(array.shape[-2:] if array is current else array.shape, bf16) for array in operands[3:]]
    scratch = first + held + [pltpu.SemaphoreType.DMA((len(held),))] + [
        pltpu.VMEM((rows, lanes), bf16),
        pltpu.VMEM((8, rows, lanes), bf16),
        pltpu.VMEM((rows, 8 * lanes), bf16),
        pltpu.VMEM((rows, width), jnp.float32),
        pltpu.VMEM((8, share, width), bf16),
    ]
    rings = [pltpu.VMEM((count,) + block, bf16) for count in (4, 3, 3, 4)]
    sems = []
    for count in (RING_SLOTS, gather, RING_SLOTS, 2, 1):
        sems = sems + sem_pair(count)
    return pl.pallas_call(
        functools.partial(pass_kernel, last=last),
        out_shape=shapes,
        in_specs=whole(3) + [pl.BlockSpec(memory_space=pl.ANY)] * len(held),
        out_specs=tuple(whole(len(shapes))),
        scratch_shapes=scratch + rings + sems,
        compiler_params=pltpu.CompilerParams(
            collective_id=collective_id, has_side_effects=True, vmem_limit_bytes=56 << 20
        ),
        cost_estimate=busy(50),
        name=f"pass_{collective_id}",
    )(*operands)


R_A, R_B, R_O, L_A, L_B, L_O, X_A, X_B = 0, 4, 8, 12, 16, 20, 24, 25
GATHER_SLOTS = 33


def gather_begin_low(net, out, sems, half):
    low = out.at[net.x, net.z, 0:half]
    net.send(low, low, sems, R_A + 0, net.right)
    net.send(low, low, sems, L_A + 0, net.left)
    net.send(low, low, sems, X_A, net.pair)


def gather_begin_high(net, out, sems, half):
    high = out.at[net.x, net.z, half : 2 * half]
    net.send(high, high, sems, R_B + 0, net.right)
    net.send(high, high, sems, L_B + 0, net.left)
    net.send(high, high, sems, X_B + 0, net.pair)


def gather_rest(net, out, sems, half):
    other = 1 - net.x
    peer_low = out.at[other, net.z, 0:half]
    net.arrived(peer_low, sems, X_A)
    net.send(peer_low, peer_low, sems, R_O + 0, net.right)
    net.send(peer_low, peer_low, sems, L_O + 0, net.left)
    for step in range(1, 5):
        before, after = net.ring(-step), net.ring(step)
        piece = out.at[net.x, before, 0:half]
        net.arrived(piece, sems, R_A + step - 1)
        if step < 4:
            net.send(piece, piece, sems, R_A + step, net.right)
        piece = out.at[net.x, after, half : 2 * half]
        net.arrived(piece, sems, L_B + step - 1)
        if step < 4:
            net.send(piece, piece, sems, L_B + step, net.left)
        net.send(piece, piece, sems, X_B + (step if step < 4 else 7), net.pair)
        piece = out.at[other, after, 0:half]
        net.arrived(piece, sems, L_O + step - 1)
        if step < 4:
            net.send(piece, piece, sems, L_O + step, net.left)
        if step < 4:
            piece = out.at[net.x, after, 0:half]
            net.arrived(piece, sems, L_A + step - 1)
            if step < 3:
                net.send(piece, piece, sems, L_A + step, net.left)
            piece = out.at[net.x, before, half : 2 * half]
            net.arrived(piece, sems, R_B + step - 1)
            if step < 3:
                net.send(piece, piece, sems, R_B + step, net.right)
            net.send(piece, piece, sems, X_B + 3 + step, net.pair)
            piece = out.at[other, before, 0:half]
            net.arrived(piece, sems, R_O + step - 1)
            if step < 3:
                net.send(piece, piece, sems, R_O + step, net.right)
    for slot, offset in ((0, 0), (1, 1), (2, 2), (3, 3), (7, 4), (4, -1), (5, -2), (6, -3)):
        net.arrived(out.at[other, net.ring(offset), half : 2 * half], sems, X_B + slot)


PIECES = (0, 2, 1, 3)


SLOTS = 112


def start_kernel(
    own, w_own, ids, raw_table, tokens_in, w_qkv_in, w_fc, w_proj, out, w_all, w_mlp_pair, w_qkv_pair, fresh, rows_out,
    qkv, tokens, w_qkv, table, ranks, relatives, sent, got, picked, mine, copy_sems,
    send_sems, recv_sems, send_w, recv_w, send_f, recv_f, send_g, recv_g, send_m, recv_m,
):
    net = Net()
    f32, bf16 = jnp.float32, jnp.bfloat16
    me = lax.axis_index("req")
    y, x, core = me // 4, (me // 2) % 2, me % 2

    def device(step, other_x, other_core=False):
        return (
            lax.rem(y + 4 + step, 4) * 4
            + (1 - x if other_x else x) * 2
            + (1 - core if other_core else core)
        )

    up, down, side, twin = device(1, 0), device(-1, 0), device(0, 1), device(0, 0, True)
    barrier = pltpu.get_barrier_semaphore()
    for step in range(1, 16):
        other = lax.rem(me + step, 16)
        pl.semaphore_signal(barrier, inc=1, device_id={"req": other}, device_id_type=MESH)
    for step in range(1, 16):
        other = lax.rem(net.blk + step, 16)
        pl.semaphore_signal(barrier, inc=1, device_id={"blk": other}, device_id_type=MESH)
    cross = {"req": side, "blk": net.pair}
    pl.semaphore_signal(barrier, inc=1, device_id=cross, device_id_type=MESH)
    pl.semaphore_wait(barrier, 31)
    w_sems, f_sems, g_sems, m_sems = (send_w, recv_w), (send_f, recv_f), (send_g, recv_g), (send_m, recv_m)
    columns, vocab_dev = raw_table.shape
    started = []

    def copy_of(src, dst, slot, other):
        return pltpu.make_async_remote_copy(
            src_ref=src,
            dst_ref=dst,
            send_sem=send_sems.at[slot],
            recv_sem=recv_sems.at[slot],
            device_id={"req": other},
            device_id_type=MESH,
        )

    def send(src, dst, slot, other):
        copy = copy_of(src, dst, slot, other)
        copy.start()
        started.append(copy)

    def arrived(dst, slot):
        copy_of(dst, dst, slot, twin).wait_recv()

    U0, D0, SIDE, U1, D1, UF0, UF1, DF0, DF1, TWIN = 0, 4, 8, 12, 16, 20, 22, 24, 26, 28
    places = {(0, 0): 0, (0, 1): 1, (-1, 0): 2, (1, 0): 3, (-1, 1): 4, (1, 1): 5, (2, 0): 6, (2, 1): 7}

    def share(step, other_x, g):
        piece = out.at[g, device(step, other_x)]
        send(piece, piece, TWIN + 4 * places[(step, other_x)] + g, twin)

    for g in PIECES:
        dst = out.at[g, me]
        send(own.at[g], dst, U0 + g, up)
        send(own.at[g], dst, D0 + g, down)
        send(own.at[g], dst, SIDE + g, side)
    RO, LO, RQ, LQ, PX, TW = 0, 4, 7, 10, 14, 15

    def w_piece(offset, parity, half):
        return w_all.at[net.ring(offset), parity, half]

    def w_twin(offset, parity, slot):
        piece = w_piece(offset, parity, core)
        net.send(piece, piece, w_sems, TW + slot, twin, "req")

    w_half, w_mine = w_own.at[core], w_piece(0, net.x, core)
    net.send(w_half, w_mine, w_sems, PX, net.pair)
    net.send(w_half, w_mine, w_sems, RO, net.right)
    net.send(w_half, w_mine, w_sems, LO, net.left)
    net.send(w_half, w_mine, w_sems, TW, twin, "req")
    keeps = [
        pltpu.make_async_copy(own, out.at[:, me], copy_sems.at[0]),
        pltpu.make_async_copy(w_half, w_mine, copy_sems.at[1]),
    ]
    loads = [
        pltpu.make_async_copy(tokens_in, tokens, copy_sems.at[2]),
        pltpu.make_async_copy(w_qkv_in, w_qkv, copy_sems.at[3]),
    ]
    for copy in keeps + loads:
        copy.start()

    units, half_qkv = w_fc.shape[0] // 5, w_qkv_pair.shape[0] // 2

    def pair_pieces(which):
        pieces = [w_mlp_pair.at[which, pl.ds(index * units, units)] for index in range(5)]
        rows = pl.ds(pl.multiple_of(which * half_qkv, half_qkv), half_qkv)
        return pieces + [w_qkv_pair.at[rows]]

    def pair_send():
        def copy_from(src, dst, slot):
            return pltpu.make_async_remote_copy(
                src_ref=src,
                dst_ref=dst,
                send_sem=m_sems[0].at[slot],
                recv_sem=m_sems[1].at[slot],
                device_id={"blk": net.pair} if slot < 3 else cross,
                device_id_type=MESH,
            )

        for slot in range(5):
            rows = pl.ds(slot * units, units)
            for which, weights in enumerate((w_fc, w_proj)):
                copy = copy_from(weights.at[rows], w_mlp_pair.at[which, rows], slot)
                pl.when(core == which)(copy.start)
            started.append(copy)
        rows = pl.ds(pl.multiple_of(core * half_qkv, half_qkv), half_qkv)
        copy = copy_from(w_qkv_in.at[rows], w_qkv_pair.at[rows], 5)
        copy.start()
        started.append(copy)

    def pair_share():
        for slot, dst in enumerate(pair_pieces(core)):
            net.arrived(dst, m_sems, slot)
            net.send(dst, dst, m_sems, 6 + slot, twin, "req")

    def pair_end():
        for slot, dst in enumerate(pair_pieces(1 - core)):
            net.arrived(dst, m_sems, 6 + slot)

    def w_begin():
        piece = w_piece(0, 1 - net.x, core)
        net.arrived(piece, w_sems, PX)
        net.send(piece, piece, w_sems, RQ, net.right)
        net.send(piece, piece, w_sems, LQ, net.left)
        w_twin(0, 1 - net.x, 8)

    def w_step(step):
        for parity, slot_r, slot_l, last_r, last_l, twin_slot in (
            (net.x, RO, LO, 4, 3, 0), (1 - net.x, RQ, LQ, 3, 4, 8)
        ):
            if step < last_r:
                piece = w_piece(-1 - step, parity, core)
                net.arrived(piece, w_sems, slot_r + step)
                if step < last_r - 1:
                    net.send(piece, piece, w_sems, slot_r + step + 1, net.right)
                w_twin(-1 - step, parity, twin_slot + (7 - step))
            if step < last_l:
                piece = w_piece(1 + step, parity, core)
                net.arrived(piece, w_sems, slot_l + step)
                if step < last_l - 1:
                    net.send(piece, piece, w_sems, slot_l + step + 1, net.left)
                w_twin(1 + step, parity, twin_slot + 1 + step)

    def w_end():
        for twin_slot, parity in ((0, net.x), (8, 1 - net.x)):
            for offset in range(8):
                net.arrived(w_piece(offset, parity, 1 - core), w_sems, TW + twin_slot + offset)

    count = ids.shape[1]

    def within(values, owner):
        offset = values - owner * vocab_dev
        return (offset >= 0) & (offset < vocab_dev), offset

    table[...] = jnp.zeros_like(table)
    table[0:columns, 0:vocab_dev] = raw_table[...]
    inside, offset = within(ids[...], me)
    owners = lax.broadcasted_iota(jnp.int32, (16, 1), 0)
    theirs, _ = within(ids[pl.ds(me, 1), :], owners)
    both = jnp.concatenate([jnp.where(inside, 1.0, 0.0), jnp.where(theirs, 1.0, 0.0)], 0)
    earlier = lax.broadcasted_iota(jnp.int32, (count, count), 0) < lax.broadcasted_iota(
        jnp.int32, (count, count), 1
    )
    rank = jnp.dot(
        both.astype(bf16), jnp.where(earlier, 1.0, 0.0).astype(bf16), preferred_element_type=f32
    )
    ranks[...] = jnp.where(inside, rank[0:16], -1.0)
    relatives[...] = offset.astype(f32)
    slot_of = jnp.where(theirs, rank[16:32] + owners.astype(f32) * SLOTS, 0.0)
    place_row = jnp.sum(slot_of, 0, keepdims=True)

    def pick(chunk, _):
        slots = lax.broadcasted_iota(jnp.int32, (SLOTS, 1), 0).astype(f32)
        wanted = []
        for step in range(4):
            other = pl.ds(lax.rem(me + 4 * chunk + step, 16), 1)
            chosen = ranks[other, :] == slots
            wanted.append(jnp.sum(jnp.where(chosen, relatives[other, :], 0.0), 1, keepdims=True))
        wanted = jnp.concatenate(wanted, 0).astype(jnp.int32)
        row = lax.broadcasted_iota(jnp.int32, (1, table.shape[1]), 1)
        one_hot = jnp.where(wanted == row, 1.0, 0.0).astype(bf16)
        rows = lax.dot_general(
            one_hot, table[...], (((1,), (1,)), ((), ())), preferred_element_type=f32
        ).astype(bf16)
        sent[pl.ds(4 * chunk, 4)] = rows.reshape(4, SLOTS, rows.shape[1])
        return 0

    def send_picked():
        got[me] = sent[0]
        for step in range(1, 16):
            other = lax.rem(me + step, 16)
            net.send(sent.at[step], got.at[me], f_sems, step - 1, other, "req")

    def spread():
        for step in range(1, 16):
            net.arrived(got.at[lax.rem(me + 16 - step, 16)], f_sems, step - 1)
        place = jnp.transpose(jnp.broadcast_to(place_row, (8, count)))[:, 0:1].astype(jnp.int32)
        slot = lax.broadcasted_iota(jnp.int32, (1, 16 * SLOTS), 1)
        one_hot = jnp.where(place == slot, 1.0, 0.0).astype(bf16)
        rows = jnp.dot(
            one_hot, got[...].reshape(16 * SLOTS, got.shape[2]), preferred_element_type=f32
        )
        picked[...] = rows.astype(bf16).reshape(picked.shape)
        mine[net.blk] = picked[net.blk]
        for step in range(1, 16):
            other = lax.rem(net.blk + step, 16)
            net.send(picked.at[other], mine.at[net.blk], g_sems, step - 1, other)

    def join():
        for step in range(1, 16):
            net.arrived(mine.at[lax.rem(net.blk + 16 - step, 16)], g_sems, step - 1)
        fresh[...] = jnp.concatenate([mine[index, :, 0:columns] for index in range(16)], 1)

    def first_qkv(request, _):
        rows_f32 = jnp.transpose(tokens[request].astype(f32))
        rows_out[request] = rows_f32.astype(bf16)
        qkv[request] = project(layer_norm(rows_f32).astype(bf16), w_qkv[...])
        return 0

    lax.fori_loop(0, 4, pick, 0)
    send_picked()
    for g in PIECES:
        send(own.at[g], out.at[g, me], TWIN + g, twin)

    def from_below(g, other_x, base, forward):
        piece = out.at[g, device(-1, other_x)]
        arrived(piece, base + g)
        if g < 2:
            send(piece, piece, forward + g, up)
        share(-1, other_x, g)

    def from_above(g, other_x, base, forward):
        piece = out.at[g, device(1, other_x)]
        arrived(piece, base + g)
        if g >= 2:
            send(piece, piece, forward + g - 2, down)
        share(1, other_x, g)

    def from_far(g, other_x):
        piece = out.at[g, device(2, other_x)]
        if g < 2:
            arrived(piece, (UF1 if other_x else UF0) + g)
        else:
            arrived(piece, (DF1 if other_x else DF0) + g - 2)
        share(2, other_x, g)

    for index, g in enumerate(PIECES):
        piece = out.at[g, side]
        arrived(piece, SIDE + g)
        send(piece, piece, U1 + g, up)
        send(piece, piece, D1 + g, down)
        share(0, 1, g)
        from_below(g, 0, U0, UF0)
        from_above(g, 0, D0, DF0)
        if index == 0:
            w_begin()
        elif index == 2:
            w_step(0)
    pair_send()
    w_step(1)
    spread()
    for index, g in enumerate(PIECES):
        from_below(g, 1, U1, UF1)
        from_above(g, 1, D1, DF1)
        from_far(g, 0)
        if index == 1:
            w_step(2)
    for load in loads:
        load.wait()
    lax.fori_loop(0, 2, first_qkv, 0)
    w_step(3)
    for g in PIECES:
        from_far(g, 1)
    for (step, other_x), place in places.items():
        for g in PIECES:
            arrived(out.at[g, device(step, other_x, True)], TWIN + 4 * place + g)
    pair_share()
    join()
    w_end()
    pair_end()
    for keep in keeps:
        keep.wait()
    for copy in started:
        copy.wait_send()
    net.finish()


def start_gathers(own, w_own, ids, table, tokens, w_qkv, w_fc, w_proj, collective_id):
    groups = own.shape[0]
    count = ids.shape[1]
    columns, vocab_dev = table.shape
    requests, width, rows = tokens.shape
    bf16 = jnp.bfloat16
    blocks = pltpu.VMEM((16, SLOTS, 128), bf16)
    asked = pltpu.VMEM((16, count // 16, 128), bf16)
    anywhere = [pl.BlockSpec(memory_space=pl.ANY)]
    return pl.pallas_call(
        start_kernel,
        out_shape=(
            jax.ShapeDtypeStruct((groups, 16) + own.shape[1:], own.dtype),
            jax.ShapeDtypeStruct((8, 2) + w_own.shape, w_own.dtype),
            jax.ShapeDtypeStruct((2,) + w_fc.shape, w_fc.dtype),
            jax.ShapeDtypeStruct(w_qkv.shape, w_qkv.dtype),
            jax.ShapeDtypeStruct((count // 16, 16 * columns), bf16),
            jax.ShapeDtypeStruct((requests, rows, width), bf16),
            jax.ShapeDtypeStruct((requests, rows, 256), bf16),
        ),
        in_specs=anywhere * 2 + whole(2) + anywhere * 4,
        out_specs=tuple(anywhere * 4 + whole(3)),
        scratch_shapes=[
            pltpu.VMEM(tokens.shape, bf16),
            pltpu.VMEM(w_qkv.shape, bf16),
            pltpu.VMEM((128, -(-vocab_dev // 128) * 128), bf16),
            pltpu.VMEM((16, count), jnp.float32),
            pltpu.VMEM((16, count), jnp.float32),
            blocks,
            blocks,
            asked,
            asked,
            pltpu.SemaphoreType.DMA((4,)),
        ]
        + sem_pair(60)
        + sem_pair(31)
        + sem_pair(15)
        + sem_pair(15)
        + sem_pair(12),
        compiler_params=pltpu.CompilerParams(
            collective_id=collective_id, has_side_effects=True, vmem_limit_bytes=58 << 20
        ),
        cost_estimate=busy(45),
        name="start_gathers",
    )(own, w_own, ids, table, tokens, w_qkv, w_fc, w_proj)


def asked_rows(new_ids):
    by_device = new_ids.reshape(new_ids.shape[0], 16, 2, 8, -1)
    return jnp.transpose(by_device, (1, 3, 2, 0, 4)).reshape(16, -1)


def settle_fresh(quick, ids, embed_table, req_index):
    vocab_dev = embed_table.shape[0]
    owner = ids // vocab_dev
    owners = jnp.arange(16)[:, None]
    asked = jnp.sum((owner[:, None, :] == owners[None]).astype(jnp.int32), -1)
    crowded = jnp.max(asked) > SLOTS

    def dense():
        relative = (ids - req_index * vocab_dev).reshape(-1)
        here = (relative >= 0) & (relative < vocab_dev)
        looked = jnp.take(embed_table, jnp.clip(relative, 0, vocab_dev - 1), axis=0)
        looked = jnp.where(here[:, None], looked, jnp.zeros((), jnp.bfloat16))
        looked = lax.all_to_all(
            looked.reshape(16, -1, looked.shape[1]), "req", split_axis=0, concat_axis=0, tiled=True
        )
        summed = jnp.sum(looked.astype(jnp.float32), 0).astype(jnp.bfloat16)
        summed = summed.reshape(16, -1, summed.shape[1])
        mine = lax.all_to_all(summed, "blk", split_axis=0, concat_axis=0, tiled=True)
        return jnp.transpose(mine, (1, 0, 2)).reshape(quick.shape)

    return lax.cond(crowded, dense, lambda: quick)


def attend_kernel(groups, lengths, qkv, cache, out, *, span):
    length = lengths[pl.program_id(0)]
    q, own_block = qkv[0, :, 0:128], qkv[0, :, 128:256]
    f32 = jnp.float32

    def scores_of(keys):
        return lax.dot_general(q, keys, (((1,), (1,)), ((), ())), preferred_element_type=f32)

    def weigh(weights, values):
        return jnp.dot(weights.astype(jnp.bfloat16), values, preferred_element_type=f32)

    scores = scores_of(own_block)
    top = jnp.max(scores, -1, keepdims=True)
    weights = jnp.exp(scores - top)
    total = jnp.sum(weights, -1, keepdims=True)
    mixed = weigh(weights, own_block)
    for start in range(0, cache.shape[1], span):
        block = cache[0, start : start + span, :]
        position = start + lax.broadcasted_iota(jnp.int32, (1, span), 1)
        scores = scores_of(block) + jnp.where(position < length, 0.0, NEG).astype(f32)
        raised = jnp.maximum(top, jnp.max(scores, -1, keepdims=True))
        shrink = jnp.exp(top - raised)
        weights = jnp.exp(scores - raised)
        total = total * shrink + jnp.sum(weights, -1, keepdims=True)
        mixed = mixed * shrink + weigh(weights, block)
        top = raised
    head = mixed / total
    parity = lax.axis_index("blk") % 2
    lane = lax.broadcasted_iota(jnp.int32, (1, 128), 1)
    moved = jnp.where(parity == 0, pltpu.roll(head, 64, 1), head)
    out[0] = jnp.where(lane // 64 == parity, moved, 0.0).astype(out.dtype)


def attend(qkv, cache, groups, lengths):
    requests, rows, width = qkv.shape
    size = cache.shape[1]
    return pl.pallas_call(
        functools.partial(attend_kernel, span=min(2048, size)),
        out_shape=jax.ShapeDtypeStruct((requests, rows, 128), jnp.bfloat16),
        grid_spec=pltpu.PrefetchScalarGridSpec(
            num_scalar_prefetch=2,
            grid=(requests,),
            in_specs=[
                pl.BlockSpec((1, rows, width), lambda r, g, n: (r, 0, 0)),
                pl.BlockSpec((1, size, 128), lambda r, g, n: (g[r], 0, 0)),
            ],
            out_specs=pl.BlockSpec((1, rows, 128), lambda r, g, n: (r, 0, 0)),
        ),
        compiler_params=pltpu.CompilerParams(vmem_limit_bytes=58 << 20),
        cost_estimate=busy(11),
        name="attend",
    )(groups, lengths, qkv, cache)


def shards(
    tokens, cache_kv, w_qkv, w_out, w_fc, w_proj, embed_table, group_ids, cache_len, accept, new_ids
):
    req_index = lax.axis_index("req")
    blk_index = lax.axis_index("blk")
    z, x = blk_index // 2, blk_index % 2
    requests, rows, width = tokens.shape
    kv_width = cache_kv.shape[3]
    head_dim = kv_width // 2
    share = rows // 8
    my_groups = lax.dynamic_slice_in_dim(group_ids, req_index * requests, requests)
    lengths = jnp.take(cache_len, my_groups)
    w_own = jnp.transpose(w_qkv[:, 0, :])
    w_fc = jnp.transpose(w_fc)
    ids = asked_rows(new_ids)
    every_cache, w_out_all, w_mlp_pair, w_other, fresh, current, qkv = start_gathers(
        cache_kv[:, :, 0, :],
        w_out.reshape(2, head_dim // 2, width),
        ids,
        jnp.transpose(embed_table),
        jnp.transpose(tokens, (0, 2, 1)),
        w_own,
        w_fc,
        w_proj,
        1,
    )
    w_out_all = w_out_all.reshape(16 * head_dim, width)
    every_cache = every_cache.reshape(cache_kv.shape[0], -1, kv_width)
    my_accept = lax.dynamic_index_in_dim(accept, x, 1, keepdims=False)
    my_accept = lax.dynamic_slice_in_dim(my_accept, z * share, share, 1)[..., None]
    fresh = settle_fresh(fresh, ids, embed_table, req_index).reshape(PASSES, share, width)
    for pass_index in range(PASSES):
        last = pass_index == PASSES - 1
        done = run_pass(
            attend(qkv, every_cache, my_groups, lengths),
            current,
            w_out_all,
            w_fc,
            w_proj,
            w_mlp_pair,
            fresh[pass_index],
            my_accept[pass_index],
            None if last else (w_own, w_other),
            2 + pass_index,
        )
        if last:
            return done[0].reshape(requests, rows, width)
        current, qkv = done[0].reshape(rows, width), done[1]


def solution(mesh):
    return jax.shard_map(
        shards,
        mesh=mesh,
        in_specs=(
            P("req", None, None),
            P(None, "req", "blk", None),
            P(None, "blk", None),
            P("blk", None, None),
            P(None, "blk"),
            P("blk", None),
            P("req", "blk"),
            P(),
            P(),
            P(None, "req", None),
            P(),
        ),
        out_specs=P("req", None, None),
        check_vma=False,
    )
```
